32 devices in a mesh: dp: 8 (over z, x), rows: 4 (over y, core).
Axes of the slice: x: 2, y: 2, z: 4, core: 2. Of those that a mesh axis runs over, the one named last changes fastest.
Arguments:
- atoms: bfloat16 [24, 256, 512], P('dp', 'rows'), may hold values from -6 to 6
- pair_bias: bfloat16 [24, 64, 256, 256], P('dp', None, 'rows'), may hold values from -6 to 6
- mol_counts: int32 [24, 8], P('dp'), may hold values from 1 to 96, 256 in all within a row
- attn_gain: bfloat16 [512], replicated, may hold values from 0.5 to 1.5
- attn_shift: bfloat16 [512], replicated, may hold values from -1.75 to 1.75
- query_weight: bfloat16 [512, 512], replicated, may hold values from -0.25 to 0.25
- query_bias: bfloat16 [512], replicated, may hold values from -3 to 3
- key_weight: bfloat16 [512, 512], replicated, may hold values from -0.25 to 0.25
- value_weight: bfloat16 [512, 512], replicated, may hold values from -0.25 to 0.25
- value_bias: bfloat16 [512], replicated, may hold values from -3 to 3
- out_weight: bfloat16 [512, 512], replicated, may hold values from -0.75 to 0.75
- out_bias: bfloat16 [512], replicated, may hold values from -1.75 to 1.75
- ffn_gain: bfloat16 [512], replicated, may hold values from 0.5 to 1.5
- ffn_shift: bfloat16 [512], replicated, may hold values from -1.75 to 1.75
- inner_weight: bfloat16 [512, 2048], replicated, may hold values from -0.25 to 0.25
- inner_bias: bfloat16 [2048], replicated, may hold values from -3 to 3
- outer_weight: bfloat16 [2048, 512], replicated, may hold values from -0.1875 to 0.1875
- outer_bias: bfloat16 [512], replicated, may hold values from -1.75 to 1.75
- atoms_cotangent: bfloat16 [24, 256, 512], P('dp', 'rows'), may hold values from -6 to 6
- pair_cotangent: bfloat16 [24, 64, 256, 256], P('dp', None, 'rows'), may hold values from -6 to 6
Outputs:
- atoms_out: bfloat16 [24, 256, 512], P('dp', 'rows')
- pair_out: bfloat16 [24, 64, 256, 256], P('dp', None, 'rows')
- atoms_grad: bfloat16 [24, 256, 512], P('dp', 'rows')
- pair_grad: bfloat16 [24, 64, 256, 256], P('dp', None, 'rows')
- attn_gain_grad: float32 [512], P('dp')
- attn_shift_grad: float32 [512], P('dp')
- query_weight_grad: float32 [512, 512], P('dp')
- query_bias_grad: float32 [512], P('dp')
- key_weight_grad: float32 [512, 512], P('dp')
- value_weight_grad: float32 [512, 512], P('dp')
- value_bias_grad: float32 [512], P('dp')
- out_weight_grad: float32 [512, 512], P('dp')
- out_bias_grad: float32 [512], P('dp')
- ffn_gain_grad: float32 [512], P('dp')
- ffn_shift_grad: float32 [512], P('dp')
- inner_weight_grad: float32 [512, 2048], P('dp')
- inner_bias_grad: float32 [2048], P('dp')
- outer_weight_grad: float32 [2048, 512], P('dp')
- outer_bias_grad: float32 [512], P('dp')
The draws below stay inside these ranges and needn't reach their ends.
Inputs may be any that keep to these rules, and one draw needn't show every extreme that they name: `mol_counts`: each slot's counts sum to 256, and the largest count of every slot is 96.
All inputs are finite; a program needn't handle non-finite values.
Results may differ from the reference program's by a relative error of at most 0.0083.
Values may be sent and summed in bfloat16 or wider, within the bound.
A program may use at most 128 MiB of HBM per device.

```python
import math
import jax
import jax.numpy as jnp
import numpy as np
from jax import lax

D = 512
FF = 2048
H = 64
DH = 8
L = 256
MOLS = 8
MOST = 96
SLOTS = 24


def level_of(key, extent, cuts, least, high):
    def one(dim, blocks):
        draws = jax.random.uniform(jax.random.fold_in(jax.random.fold_in(key, 6), dim), (blocks,), jnp.float32, least / len(cuts), high / len(cuts))
        return jnp.repeat(jnp.exp(draws), extent[dim] // blocks).reshape((-1,) + (1,) * (len(extent) - dim - 1))

    loudness = one(*cuts[0])
    for cut in cuts[1:]:
        loudness = loudness * one(*cut)
    return loudness


def length_profile(count, total, reach, skew):
    weights = [(1 << 20) // math.isqrt(rank ** skew) + 1 for rank in range(2, count + 1)]
    rest, holding = total - reach - (count - 1), [1] * (count - 1)
    while rest > 0:
        free = [i for i in range(count - 1) if holding[i] < reach]
        mass, remaining = sum([weights[i] for i in free]), rest
        for i in free:
            more = min(reach - holding[i], max(1, remaining * weights[i] // mass), rest)
            holding[i] = holding[i] + more
            rest = rest - more
    return np.array([reach] + holding)


def ragged(rng, amount, total, reach, slope):
    if amount == 2:
        one = jax.random.randint(rng, (), max(1, total - reach), min(reach, total - 1) + 1)
        return jnp.stack([one, total - one])
    sizes = jnp.asarray(length_profile(amount, total, reach, slope), jnp.int32)
    couples = (amount - 1) // 2
    donor, taker = sizes[1:1 + 2 * couples:2], sizes[2:2 + 2 * couples:2]
    room = jnp.minimum(donor - 1, reach - taker)
    passed = jax.random.randint(jax.random.fold_in(rng, 1), (couples,), 0, 1 << 20) % (room + 1)
    sizes = sizes.at[1:1 + 2 * couples:2].set(donor - passed).at[2:2 + 2 * couples:2].set(taker + passed)
    return sizes[jax.random.permutation(jax.random.fold_in(rng, 2), amount)]


def noise(rng, extent, deviation, limit, pieces=(), kind=jnp.bfloat16):
    level = level_of(rng, extent, pieces, -0.22, 0.18) if pieces else 1.0
    array = jax.random.normal(rng, extent, jnp.float32) * deviation * level
    return jnp.minimum(jnp.maximum(array, -limit), limit).astype(kind)


def setup_inputs(seed: int = 0) -> dict:
    key_list = jax.random.split(jax.random.key(seed), 21)
    return {
        "atoms": noise(key_list[0], (SLOTS, L, D), 1.0, 6.0, ((0, 8), (1, 4))),
        "pair_bias": noise(key_list[1], (SLOTS, H, L, L), 1.0, 6.0, ((0, 8), (2, 4))),
        "mol_counts": jax.vmap(lambda own: ragged(own, MOLS, L, MOST, 2))(jax.random.split(key_list[2], SLOTS)).reshape((SLOTS, MOLS)).astype(jnp.int32),
        "attn_gain": jnp.clip(1.0 + 0.1 * jax.random.normal(key_list[3], (D,), jnp.float32), 0.5, 1.5).astype(jnp.bfloat16),
        "attn_shift": noise(key_list[4], (D,), 0.3, 1.75),
        "query_weight": noise(key_list[5], (D, D), D ** -0.5, 0.25),
        "query_bias": noise(key_list[6], (D,), 0.5, 3.0),
        "key_weight": noise(key_list[7], (D, D), D ** -0.5, 0.25),
        "value_weight": noise(key_list[8], (D, D), D ** -0.5, 0.25),
        "value_bias": noise(key_list[9], (D,), 0.5, 3.0),
        "out_weight": noise(key_list[10], (D, D), (D // 8) ** -0.5, 0.75),
        "out_bias": noise(key_list[11], (D,), 0.3, 1.75),
        "ffn_gain": jnp.clip(1.0 + 0.1 * jax.random.normal(key_list[12], (D,), jnp.float32), 0.5, 1.5).astype(jnp.bfloat16),
        "ffn_shift": noise(key_list[13], (D,), 0.3, 1.75),
        "inner_weight": noise(key_list[14], (D, FF), D ** -0.5, 0.25),
        "inner_bias": noise(key_list[15], (FF,), 0.5, 3.0),
        "outer_weight": noise(key_list[16], (FF, D), (FF // 2) ** -0.5, 0.1875),
        "outer_bias": noise(key_list[17], (D,), 0.3, 1.75),
        "atoms_cotangent": noise(key_list[18], (SLOTS, L, D), 1.0, 6.0, ((0, 8), (1, 4))),
        "pair_cotangent": noise(key_list[19], (SLOTS, H, L, L), 1.0, 6.0, ((0, 8), (2, 4))),
    }


@jax.custom_vjp
def low(v):
    return lax.optimization_barrier(v.astype(jnp.bfloat16)).astype(jnp.float32)

@jax.custom_vjp
def low_back(v):
    return v

def low_keep(v):
    return (low(v), None)

def low_pass(kept, grad):
    return (grad,)

def back_keep(v):
    return (v, None)

def back_low(kept, grad):
    return (low(grad),)
low.defvjp(low_keep, low_pass)
low_back.defvjp(back_keep, back_low)

def matmul(left, right):
    return jnp.dot(left, right, precision=lax.Precision.HIGHEST, preferred_element_type=jnp.float32)

def layer_norm(value, gain, shift):
    centred = value - lax.optimization_barrier(jnp.mean(value, axis=-1, keepdims=True))
    inverse = lax.rsqrt(lax.optimization_barrier(jnp.mean(centred * centred, axis=-1, keepdims=True)) + 1e-05)
    return centred * inverse * gain + shift

def layer(params, atoms_slot, pair_slot, segment):
    attn_gain, attn_shift, query_weight, query_bias, key_weight, value_weight, value_bias, out_weight, out_bias, ffn_gain, ffn_shift, inner_weight, inner_bias, outer_weight, outer_bias = params
    scale = DH ** (-0.5)
    normed = low(layer_norm(atoms_slot, attn_gain, attn_shift))
    queries = low_back(low((matmul(normed, query_weight) + query_bias) * scale))
    keys = low_back(low(matmul(normed, key_weight)))
    values = low_back(low(matmul(normed, value_weight) + value_bias))
    query_heads = queries.reshape(L, H, DH)
    key_heads = keys.reshape(L, H, DH)
    value_heads = values.reshape(L, H, DH)
    scores = jnp.einsum('qhd,khd->hqk', query_heads, key_heads, precision=lax.Precision.HIGHEST)
    scores = low_back(scores + pair_slot)
    allowed = (segment[:, None] == segment[None, :])[None]
    masked = jnp.where(allowed, scores, -1000000000.0)
    probs = low(jax.nn.softmax(masked, axis=-1))
    mixed = jnp.einsum('hqk,khd->qhd', probs, value_heads, precision=lax.Precision.HIGHEST)
    mixed = low_back(low(mixed.reshape(L, D)))
    branch = low_back(matmul(mixed, out_weight) + out_bias)
    middle = atoms_slot + branch
    inner = low(layer_norm(middle, ffn_gain, ffn_shift))
    pre = low_back(matmul(inner, inner_weight) + inner_bias)
    act = low(jax.nn.gelu(pre, approximate=False))
    final = low_back(matmul(act, outer_weight) + outer_bias)
    return (middle + final, scores)

def reference(atoms, pair_bias, mol_counts, attn_gain, attn_shift, query_weight, query_bias, key_weight, value_weight, value_bias, out_weight, out_bias, ffn_gain, ffn_shift, inner_weight, inner_bias, outer_weight, outer_bias, atoms_cotangent, pair_cotangent):
    params = tuple((w.astype(jnp.float32) for w in (attn_gain, attn_shift, query_weight, query_bias, key_weight, value_weight, value_bias, out_weight, out_bias, ffn_gain, ffn_shift, inner_weight, inner_bias, outer_weight, outer_bias)))
    cumulative = jnp.cumsum(mol_counts, axis=1).astype(jnp.int32)
    position = jnp.arange(L, dtype=jnp.int32)
    segments = lax.optimization_barrier(jnp.sum((cumulative[:, None, :] <= position[None, :, None]).astype(jnp.int32), axis=-1)).astype(jnp.int32)

    def forward(weights, atoms_all, pair_all):

        def one_slot(items):
            return layer(weights, items[0], items[1], items[2])
        return lax.map(jax.checkpoint(one_slot), (atoms_all, pair_all, segments))
    outputs, backward = jax.vjp(forward, params, atoms.astype(jnp.float32), pair_bias.astype(jnp.float32))
    grads, atoms_grad, pair_grad = backward((atoms_cotangent.astype(jnp.float32), pair_cotangent.astype(jnp.float32)))
    return (outputs[0].astype(jnp.bfloat16), outputs[1].astype(jnp.bfloat16), atoms_grad.astype(jnp.bfloat16), pair_grad.astype(jnp.bfloat16), grads[0], grads[1], grads[2], grads[3], grads[4], grads[5], grads[6], grads[7], grads[8], grads[9], grads[10], grads[11], grads[12], grads[13], grads[14])
```

```python
import functools

import jax
import jax.numpy as jnp
from jax import lax
from jax.experimental import pallas as pl
from jax.experimental.pallas import tpu as pltpu
from jax.sharding import PartitionSpec as P

f32, bf16 = jnp.float32, jnp.bfloat16
BIG = 1e9
HPL = 16
CHUNK = 8
STEP = 32


def standardize(value):
    centred = value - jnp.mean(value, axis=-1, keepdims=True)
    inverse = lax.rsqrt(jnp.mean(centred * centred, axis=-1, keepdims=True) + 1e-05)
    return (centred * inverse, inverse)


def norm_back(grad_normed, standard, inverse):
    return inverse * (
        grad_normed
        - jnp.mean(grad_normed, axis=-1, keepdims=True)
        - standard * jnp.mean(grad_normed * standard, axis=-1, keepdims=True)
    )


def matmul(left, right):
    return jnp.dot(left, right, preferred_element_type=f32)


def times_transposed(left, right):
    return lax.dot_general(left, right, (((1,), (1,)), ((), ())), preferred_element_type=f32)


def outer_sum(left, right):
    return lax.dot_general(left, right, (((0,), (0,)), ((), ())), preferred_element_type=f32)


def forward_kernel(q_ref, kt_ref, v_ref, bias_ref, mask_ref, out_ref, e_ref, mix_ref, rl_ref):
    _, heads, rows, full = bias_ref.shape
    lane_head = lax.broadcasted_iota(jnp.int32, (rows, 128), 1) // 8
    mask = mask_ref[0]
    ones = jnp.ones((full, 128), bf16)
    for b in range(heads // HPL):
        cols = slice(128 * b, 128 * b + 128)
        q = q_ref[0, :, cols].astype(f32)
        kt = kt_ref[0, cols, :]
        v = jnp.concatenate([v_ref[0, :, cols], ones], axis=1)
        mixed = jnp.zeros((rows, 128), f32)
        total = jnp.zeros((rows, 128), f32)
        for c in range(HPL // CHUNK):
            own = [lane_head == CHUNK * c + i for i in range(CHUNK)]
            left = jnp.concatenate([jnp.where(o, q, 0.0).astype(bf16) for o in own], axis=0)
            scores = matmul(left, kt).reshape(CHUNK, rows, full)
            hs = slice(HPL * b + CHUNK * c, HPL * b + CHUNK * (c + 1))
            scores = scores + bias_ref[0, hs].astype(f32)
            out_ref[0, hs] = scores.astype(bf16)
            scores = scores + mask[None]
            highest = jnp.max(scores, axis=-1, keepdims=True)
            e = jnp.exp(scores - highest).astype(bf16)
            e_ref[0, hs] = e
            sums = matmul(e.reshape(CHUNK * rows, full), v)
            for i, o in enumerate(own):
                mixed = jnp.where(o, sums[rows * i : rows * (i + 1), :128], mixed)
                total = jnp.where(o, sums[rows * i : rows * (i + 1), 128:], total)
        inverse = 1.0 / total
        mix_ref[0, :, cols] = mixed * inverse
        rl_ref[0, :, cols] = inverse


def attention_forward(q, kt, v, bias, mask):
    slots, heads, rows, full = bias.shape
    step = min(STEP, heads)
    width = step * 8
    natural = lambda n: pl.BlockSpec((1, n, width), lambda s, h: (s, 0, h))
    pair = pl.BlockSpec((1, step, rows, full), lambda s, h: (s, h, 0, 0))
    return pl.pallas_call(
        forward_kernel,
        grid=(slots, heads // step),
        in_specs=[
            natural(rows),
            pl.BlockSpec((1, width, full), lambda s, h: (s, h, 0)),
            natural(full),
            pair,
            pl.BlockSpec((1, rows, full), lambda s, h: (s, 0, 0)),
        ],
        out_specs=[pair, pair, natural(rows), natural(rows)],
        out_shape=[
            jax.ShapeDtypeStruct(bias.shape, bf16),
            jax.ShapeDtypeStruct(bias.shape, bf16),
            jax.ShapeDtypeStruct(q.shape, f32),
            jax.ShapeDtypeStruct(q.shape, f32),
        ],
        name="attention_forward",
        cost_estimate=pl.CostEstimate(
            flops=2 * bias.size * 512, transcendentals=bias.size, bytes_accessed=bias.size * 6
        ),
        compiler_params=pltpu.CompilerParams(vmem_limit_bytes=48 << 20),
    )(q, kt, v, bias, mask)


def backward_kernel(
    qt_ref, dm_ref, dmt_ref, nm_ref, k_ref, vt_ref, e_ref, cot_ref, pg_ref, dq_ref, dkt_ref, dvt_ref
):
    _, heads, rows, full = cot_ref.shape
    lane_head = lax.broadcasted_iota(jnp.int32, (rows, 128), 1) // 8
    shape = (8 * CHUNK, CHUNK * rows)
    same = lax.broadcasted_iota(jnp.int32, shape, 0) // 8 == lax.broadcasted_iota(jnp.int32, shape, 1) // rows
    ones = jnp.ones((128, full), bf16)
    for b in range(heads // HPL):
        cols = slice(128 * b, 128 * b + 128)
        dm = dm_ref[0, :, cols].astype(f32)
        nm = nm_ref[0, :, cols].astype(f32)
        vt = jnp.concatenate([vt_ref[0, cols, :], ones], axis=0)
        k = k_ref[0, :, cols]
        dq = jnp.zeros((rows, 128), f32)
        for c in range(HPL // CHUNK):
            own = [lane_head == CHUNK * c + i for i in range(CHUNK)]
            left = jnp.concatenate(
                [
                    jnp.concatenate([jnp.where(o, dm, 0.0), jnp.where(o, nm, 0.0)], axis=1).astype(bf16)
                    for o in own
                ],
                axis=0,
            )
            centred = matmul(left, vt).reshape(CHUNK, rows, full)
            hs = slice(HPL * b + CHUNK * c, HPL * b + CHUNK * (c + 1))
            e = e_ref[0, hs]
            grad = (e.astype(f32) * centred + cot_ref[0, hs].astype(f32)).astype(bf16)
            pg_ref[0, hs] = grad
            grad = grad.reshape(CHUNK * rows, full)
            sums = matmul(grad, k)
            for i, o in enumerate(own):
                dq = jnp.where(o, sums[rows * i : rows * (i + 1)], dq)
            rs = slice(hs.start * 8, hs.stop * 8)
            spread = lambda ref: jnp.where(
                same, jnp.concatenate([ref[0, rs, :].astype(f32)] * CHUNK, axis=1), 0.0
            ).astype(bf16)
            dkt_ref[0, rs, :] = matmul(spread(qt_ref), grad).astype(bf16)
            dvt_ref[0, rs, :] = matmul(spread(dmt_ref), e.reshape(CHUNK * rows, full)).astype(bf16)
        dq_ref[0, :, cols] = dq.astype(bf16)


def attention_backward(qt, dm, dmt, nm, k, vt, e, cot):
    slots, heads, rows, full = cot.shape
    step = min(STEP, heads)
    width = step * 8
    natural = lambda n: pl.BlockSpec((1, n, width), lambda s, h: (s, 0, h))
    turned = lambda n: pl.BlockSpec((1, width, n), lambda s, h: (s, h, 0))
    pair = pl.BlockSpec((1, step, rows, full), lambda s, h: (s, h, 0, 0))
    return pl.pallas_call(
        backward_kernel,
        grid=(slots, heads // step),
        in_specs=[
            turned(rows),
            natural(rows),
            turned(rows),
            natural(rows),
            natural(full),
            turned(full),
            pair,
            pair,
        ],
        out_specs=[pair, natural(rows), turned(full), turned(full)],
        out_shape=[
            jax.ShapeDtypeStruct(cot.shape, bf16),
            jax.ShapeDtypeStruct(dm.shape, bf16),
            jax.ShapeDtypeStruct(vt.shape, bf16),
            jax.ShapeDtypeStruct(vt.shape, bf16),
        ],
        name="attention_backward",
        cost_estimate=pl.CostEstimate(
            flops=2 * cot.size * 768, transcendentals=0, bytes_accessed=cot.size * 6
        ),
        compiler_params=pltpu.CompilerParams(vmem_limit_bytes=48 << 20),
    )(qt, dm, dmt, nm, k, vt, e, cot)


def ffn_grad_kernel(me_ref, act_ref, dy_ref, inner_ref, dpre_ref, mixed_ref, branch_ref, out_ref):
    parts = out_ref.shape[0]
    me = me_ref[0]
    tall = act_ref.shape[2] // parts
    short = inner_ref.shape[2] // parts
    half = dy_ref.shape[2]
    blocks = dpre_ref.shape[2] // half
    both = lambda left, right: sum(outer_sum(left[i], right[i]) for i in range(2))
    inner = [inner_ref[i] for i in range(2)]
    for cb in range(blocks):
        grad = both(inner, [dpre_ref[i, :, half * cb : half * (cb + 1)] for i in range(2)]).astype(bf16)
        for j in range(parts):
            out_ref[me ^ j, pl.ds(tall + short * cb, short), :] = grad[short * j : short * (j + 1)]
    grad = both([mixed_ref[i] for i in range(2)], [branch_ref[i] for i in range(2)]).astype(bf16)
    for j in range(parts):
        out_ref[me ^ j, pl.ds(tall + short * blocks, short), :] = grad[short * j : short * (j + 1)]
    dy = [dy_ref[i] for i in range(2)]
    wide = max(tall, 256)
    for n in range(act_ref.shape[2] // wide):
        grad = both([act_ref[i, :, wide * n : wide * (n + 1)] for i in range(2)], dy).astype(bf16)
        for j in range(wide // tall):
            out_ref[me ^ (n * (wide // tall) + j), pl.ds(0, tall), :] = grad[tall * j : tall * (j + 1)]


def ffn_grads(me, parts, act, dy, inner, dpre, mixed, branch):
    half = dy.shape[2]
    rows = (act.shape[2] * 2 + mixed.shape[2]) // parts
    vm = pl.BlockSpec(memory_space=pltpu.VMEM)
    return pl.pallas_call(
        ffn_grad_kernel,
        in_specs=[pl.BlockSpec(memory_space=pltpu.SMEM)] + [vm] * 6,
        out_specs=vm,
        out_shape=jax.ShapeDtypeStruct((parts, rows, half), bf16),
        name="ffn_grads",
        cost_estimate=pl.CostEstimate(flops=2 * 384 * 2304 * 512, transcendentals=0, bytes_accessed=6 << 20),
        compiler_params=pltpu.CompilerParams(vmem_limit_bytes=40 << 20),
    )(me, act, dy, inner, dpre, mixed, branch)


def attn_grad_kernel(scale, me_ref, normed_ref, own_ref, dq_ref, dkt_ref, dvt_ref, vec_ref, out_ref):
    parts = out_ref.shape[0]
    me = me_ref[0]
    short = normed_ref.shape[2] // parts
    slots = normed_ref.shape[0]

    def put(grad, at):
        grad = grad.astype(bf16)
        for j in range(parts):
            out_ref[me ^ j, pl.ds(at * short, short), :] = grad[short * j : short * (j + 1)]

    put(sum(outer_sum(own_ref[i], dq_ref[i]) for i in range(2)) * scale, 0)
    normed = [normed_ref[s].T for s in range(slots)]
    for at, ref in ((1, dkt_ref), (2, dvt_ref)):
        total = 0.0
        for s in range(slots):
            both = (ref[0, s].astype(f32) + ref[1, s].astype(f32)).astype(bf16)
            total = total + times_transposed(normed[s], both)
        put(total, at)
    out_ref[:, pl.ds(3 * short, 16), :] = vec_ref[...]


def attn_grads(me, parts, scale, normed, own, dq, dkt, dvt, vec):
    half = dq.shape[2]
    vm = pl.BlockSpec(memory_space=pltpu.VMEM)
    return pl.pallas_call(
        functools.partial(attn_grad_kernel, scale),
        in_specs=[pl.BlockSpec(memory_space=pltpu.SMEM)] + [vm] * 6,
        out_specs=vm,
        out_shape=jax.ShapeDtypeStruct((parts, 3 * normed.shape[2] // parts + 16, half), bf16),
        name="attn_grads",
        cost_estimate=pl.CostEstimate(flops=2 * 768 * 512 * 768, transcendentals=0, bytes_accessed=4 << 20),
        compiler_params=pltpu.CompilerParams(vmem_limit_bytes=40 << 20),
    )(me, normed, own, dq, dkt, dvt, vec)


def make_swap(parts, group):
    def swap(array, dp_bit=None, row_bit=None):
        pairs = []
        for d in range(parts):
            for r in range(group):
                e = d if dp_bit is None else d ^ (1 << dp_bit)
                t = r if row_bit is None else r ^ (1 << row_bit)
                pairs.append((d * group + r, e * group + t))
        return lax.ppermute(array, ("dp", "rows"), pairs)

    return swap


def add_low(left, right):
    return (left.astype(f32) + right.astype(f32)).astype(bf16)


def fold(swap, grads, bit):
    count = grads.shape[0]
    low = 1 << bit
    view = grads.reshape((count // (2 * low), 2, low) + grads.shape[1:])
    got = swap(view[:, 1], dp_bit=bit)
    return view[:, 0], got


def scatter_first(swap, grads, bits):
    remaining = list(bits)
    for n, bit in enumerate(remaining):
        view, got = fold_at(swap, grads, bit, remaining[n + 1 :])
        grads = add_low(view, got)
    return grads


def fold_at(swap, grads, bit, later):
    at = sum(1 for b in later if b < bit)
    low = 1 << at
    view = grads.reshape((grads.shape[0] // (2 * low), 2, low) + grads.shape[1:])
    keep, send = view[:, 0], view[:, 1]
    flat = lambda a: a.reshape((-1,) + grads.shape[1:])
    return flat(keep), swap(flat(send), dp_bit=bit)


def reduce_x_first(swap, grads, bits):
    total = scatter_first(swap, grads, bits)[0]
    return total.astype(f32) + swap(total, row_bit=1).astype(f32)


def reduce_y_first(swap, grads, bits, y):
    parts, rows, half = grads.shape
    view = grads.reshape(parts, 2, rows // 2, half)
    keep = lax.dynamic_index_in_dim(view, y, 1, keepdims=False)
    send = lax.dynamic_index_in_dim(view, 1 - y, 1, keepdims=False)
    total = scatter_first(swap, add_low(keep, swap(send, row_bit=1)), bits)[0]
    other = swap(total, row_bit=1)
    lower = jnp.where(y == 0, total, other)
    upper = jnp.where(y == 0, other, total)
    return jnp.concatenate([lower, upper], axis=0).astype(f32)


def local(
    parts,
    group,
    atoms,
    pair_bias,
    mol_counts,
    attn_gain,
    attn_shift,
    query_weight,
    query_bias,
    key_weight,
    value_weight,
    value_bias,
    out_weight,
    out_bias,
    ffn_gain,
    ffn_shift,
    inner_weight,
    inner_bias,
    outer_weight,
    outer_bias,
    atoms_cotangent,
    pair_cotangent,
):
    slots, part_rows, width = atoms.shape
    heads = pair_bias.shape[1]
    full = pair_bias.shape[3]
    depth = width // heads
    scale = depth ** (-0.5)
    here = slots * part_rows
    hidden = inner_weight.shape[1]
    half = width // 2
    swap = make_swap(parts, group)
    row = lax.axis_index("rows")
    core, y = row % 2, row // 2
    dp = lax.axis_index("dp")
    me = dp.astype(jnp.int32).reshape(1)
    dp_bits = list(range(parts.bit_length() - 1))

    sibling = swap(atoms, row_bit=0)
    across = swap(atoms, row_bit=1)
    corner = swap(across, row_bit=0)
    stack = jnp.stack([atoms, sibling, across, corner])
    order = jnp.arange(group, dtype=jnp.int32) ^ row
    atoms_all = jnp.take(stack, order, axis=0)
    atoms_all = jnp.swapaxes(atoms_all, 0, 1).reshape(slots, full, width)
    top_other = swap(atoms_cotangent, row_bit=0)

    cumulative = jnp.cumsum(mol_counts, axis=1)
    position = jnp.arange(full, dtype=jnp.int32)
    segment = jnp.sum(
        (cumulative[:, None, :] <= position[None, :, None]).astype(jnp.int32), axis=-1
    )
    query_segment = lax.dynamic_slice_in_dim(segment, row * part_rows, part_rows, 1)
    mask = jnp.where(query_segment[:, :, None] == segment[:, None, :], 0.0, -BIG).astype(f32)

    gain_one = attn_gain.astype(f32)
    shift_one = attn_shift.astype(f32)
    gain_two = ffn_gain.astype(f32)
    atoms_flat = atoms.astype(f32).reshape(here, width)
    standard_one, inverse_one = standardize(atoms_flat)
    normed = (standard_one * gain_one + shift_one).astype(bf16)
    standard_sib, _ = standardize(sibling.astype(f32).reshape(here, width))
    normed_sib = (standard_sib * gain_one + shift_one).astype(bf16)
    standard_all, _ = standardize(atoms_all.astype(f32).reshape(slots * full, width))
    normed_all = (standard_all * gain_one + shift_one).astype(bf16)
    queries = ((matmul(normed, query_weight) + query_bias.astype(f32)) * scale).astype(bf16)
    keys = matmul(normed_all, key_weight).astype(bf16).reshape(slots, full, width)
    values = (matmul(normed_all, value_weight) + value_bias.astype(f32)).astype(bf16)
    values = values.reshape(slots, full, width)
    queries = queries.reshape(slots, part_rows, width)
    turn = lambda a: jnp.swapaxes(a, 1, 2)
    values_turned = turn(values)
    pair_out, weights, mixed_wide, inverse_sum = attention_forward(
        queries, turn(keys), values, pair_bias, mask
    )
    mixed = mixed_wide.reshape(here, width).astype(bf16)
    middle = atoms_flat + matmul(mixed, out_weight) + out_bias.astype(f32)
    standard_two, inverse_two = standardize(middle)
    inner = (standard_two * gain_two + ffn_shift.astype(f32)).astype(bf16)
    pre = matmul(inner, inner_weight) + inner_bias.astype(f32)
    activation, gelu_back = jax.vjp(lambda u: jax.nn.gelu(u, approximate=False), pre)
    act_low = activation.astype(bf16)
    result = middle + matmul(act_low, outer_weight) + outer_bias.astype(f32)
    atoms_out = result.astype(bf16).reshape(slots, part_rows, width)
    grad_top = atoms_cotangent.reshape(here, width)
    grad_act = times_transposed(grad_top, outer_weight)
    grad_pre = gelu_back(grad_act)[0].astype(bf16)
    grad_inner = times_transposed(grad_pre, inner_weight)
    grad_middle = grad_top.astype(f32) + norm_back(grad_inner * gain_two, standard_two, inverse_two)
    grad_branch = grad_middle.astype(bf16)
    grad_mixed = times_transposed(grad_branch, out_weight).astype(bf16)

    def pick(array, which):
        return lax.dynamic_slice_in_dim(array, which * (array.shape[1] // 2), array.shape[1] // 2, 1)

    pair_of = lambda own, send: jnp.stack([own, swap(send, row_bit=0)])
    act_two = pair_of(act_low, act_low)
    inner_two = pair_of(inner, inner)
    mixed_two = pair_of(mixed, mixed)
    pre_two = pair_of(pick(grad_pre, core), pick(grad_pre, 1 - core))
    branch_two = pair_of(pick(grad_branch, core), pick(grad_branch, 1 - core))
    top_two = jnp.stack([pick(grad_top, core), pick(top_other.reshape(here, width), core)])
    ffn_packed = ffn_grads(me, parts, act_two, top_two, inner_two, pre_two, mixed_two, branch_two)
    cut = hidden // parts
    ffn_first = ffn_packed[:, :cut]
    ffn_second = ffn_packed[:, cut:]
    first_total = reduce_x_first(swap, ffn_first, dp_bits)
    second_total = reduce_y_first(swap, ffn_second, dp_bits, y)

    scaled = grad_mixed.astype(f32) * inverse_sum.reshape(here, width)
    centre = (-scaled * mixed_wide.reshape(here, width)).astype(bf16).reshape(queries.shape)
    scaled = scaled.astype(bf16).reshape(queries.shape)
    pair_grad, grad_queries, dkt, dvt = attention_backward(
        turn(queries), scaled, turn(scaled), centre, keys, values_turned, weights, pair_cotangent
    )
    grad_queries = grad_queries.reshape(here, width)

    partial = jnp.einsum("sok,io->ski", dkt, key_weight, preferred_element_type=f32) + jnp.einsum(
        "sok,io->ski", dvt, value_weight, preferred_element_type=f32
    )
    partial = partial.astype(bf16).reshape(slots, group, part_rows, width)
    partial = jnp.take(jnp.swapaxes(partial, 0, 1), order, axis=0)
    partial = partial.reshape(2, 2, slots, part_rows, width)
    chip = add_low(partial[:, 0], swap(partial[:, 1], row_bit=0))
    grad_normed = (
        times_transposed(grad_queries, query_weight) * scale
        + (chip[0].astype(f32) + swap(chip[1], row_bit=1).astype(f32)).reshape(here, width)
    )
    atoms_grad = grad_middle + norm_back(grad_normed * gain_one, standard_one, inverse_one)
    atoms_grad = atoms_grad.astype(bf16).reshape(slots, part_rows, width)

    short = (
        jnp.sum(grad_normed * standard_one, axis=0),
        jnp.sum(grad_normed, axis=0),
        jnp.sum(grad_queries.astype(f32), axis=0) * scale,
        jnp.sum(dvt.astype(f32), axis=(0, 2)),
        jnp.sum(grad_branch.astype(f32), axis=0),
        jnp.sum(grad_inner * standard_two, axis=0),
        jnp.sum(grad_inner, axis=0),
        jnp.sum(grad_top.astype(f32), axis=0),
    )
    vectors = jnp.concatenate(
        [v.reshape(parts, -1) for v in short] + [jnp.sum(grad_pre.astype(f32), axis=0).reshape(parts, -1)],
        axis=1,
    )
    vectors = vectors + swap(vectors, row_bit=0)
    vectors = jnp.take(vectors, jnp.arange(parts, dtype=jnp.int32) ^ dp, axis=0)
    vec = jnp.pad(vectors.astype(bf16), ((0, 0), (0, 16 * half - vectors.shape[1]))).reshape(parts, 16, half)

    def pick_rows(array, which):
        return lax.dynamic_slice_in_dim(array, which * half, half, 1)

    attn_packed = attn_grads(
        me,
        parts,
        scale,
        normed_all.reshape(slots, full, width),
        jnp.stack([normed, normed_sib]),
        pair_of(pick(grad_queries, core), pick(grad_queries, 1 - core)),
        pair_of(pick_rows(dkt, core), pick_rows(dkt, 1 - core)),
        pair_of(pick_rows(dvt, core), pick_rows(dvt, 1 - core)),
        vec,
    )
    share = width // parts
    third_total = reduce_x_first(swap, attn_packed[:, : attn_packed.shape[1] // 2], dp_bits)
    fourth_total = reduce_y_first(swap, attn_packed[:, attn_packed.shape[1] // 2 :], dp_bits, y)

    total = jnp.concatenate([first_total, second_total, third_total, fourth_total], axis=0)
    other = swap(total, row_bit=0)
    left = jnp.where(core == 0, total, other)
    right = jnp.where(core == 0, other, total)
    joined = jnp.stack([left, right])
    outer_share = hidden // parts
    blocks = hidden // 2 // half

    def flat(a, n):
        return jnp.swapaxes(joined[:, a : a + n], 0, 1).reshape(n, width)

    grad_outer_weight = flat(0, outer_share)
    a = outer_share
    grad_inner_weight = joined[:, a : a + share * blocks].reshape(2, blocks, share, half)
    grad_inner_weight = grad_inner_weight.transpose(2, 0, 1, 3).reshape(share, hidden)
    a += share * blocks
    grad_out_weight = flat(a, share)
    a += share
    grad_query_weight, grad_key_weight, grad_value_weight = (flat(a + share * i, share) for i in range(3))
    a += 3 * share
    vec_total = joined[0, a : a + 16].reshape(-1)
    v = [vec_total[share * i : share * (i + 1)] for i in range(8)]
    grad_inner_bias = vec_total[8 * share : 8 * share + outer_share]
    return (
        atoms_out,
        pair_out,
        atoms_grad,
        pair_grad,
        v[0],
        v[1],
        grad_query_weight,
        v[2],
        grad_key_weight,
        grad_value_weight,
        v[3],
        grad_out_weight,
        v[4],
        v[5],
        v[6],
        grad_inner_weight,
        grad_inner_bias,
        grad_outer_weight,
        v[7],
    )


def solution(mesh):
    one, two = P("dp"), P("dp", None)
    atoms_spec, pair_spec = P("dp", "rows", None), P("dp", None, "rows", None)
    in_specs = (atoms_spec, pair_spec, two) + (P(),) * 15 + (atoms_spec, pair_spec)
    out_specs = (
        (atoms_spec, pair_spec, atoms_spec, pair_spec, one, one, two, one, two, two, one, two)
        + (one, one, one, two, one, two, one)
    )
    run = functools.partial(local, mesh.shape["dp"], mesh.shape["rows"])
    return jax.shard_map(run, mesh=mesh, in_specs=in_specs, out_specs=out_specs, check_vma=False)
```

```python
import functools

import jax
import jax.numpy as jnp
from jax import lax
from jax.experimental import pallas as pl
from jax.experimental.pallas import tpu as pltpu
from jax.sharding import PartitionSpec as P

f32, bf16 = jnp.float32, jnp.bfloat16
BIG = 1e9
HPL = 16
CHUNK = 8
STEP = 32


def standardize(value):
    centred = value - jnp.mean(value, axis=-1, keepdims=True)
    inverse = lax.rsqrt(jnp.mean(centred * centred, axis=-1, keepdims=True) + 1e-05)
    return (centred * inverse, inverse)


def norm_back(grad_normed, standard, inverse):
    return inverse * (
        grad_normed
        - jnp.mean(grad_normed, axis=-1, keepdims=True)
        - standard * jnp.mean(grad_normed * standard, axis=-1, keepdims=True)
    )


def matmul(left, right):
    return jnp.dot(left, right, preferred_element_type=f32)


def times_transposed(left, right):
    return lax.dot_general(left, right, (((1,), (1,)), ((), ())), preferred_element_type=f32)


def outer_sum(left, right):
    return lax.dot_general(left, right, (((0,), (0,)), ((), ())), preferred_element_type=f32)


def forward_kernel(q_ref, kt_ref, v_ref, bias_ref, mask_ref, out_ref, e_ref, mix_ref, rl_ref):
    _, heads, rows, full = bias_ref.shape
    lane_head = lax.broadcasted_iota(jnp.int32, (rows, 128), 1) // 8
    mask = mask_ref[0]
    ones = jnp.ones((full, 128), bf16)
    for b in range(heads // HPL):
        cols = slice(128 * b, 128 * b + 128)
        q = q_ref[0, :, cols].astype(f32)
        kt = kt_ref[0, cols, :]
        v = jnp.concatenate([v_ref[0, :, cols], ones], axis=1)
        mixed = jnp.zeros((rows, 128), f32)
        total = jnp.zeros((rows, 128), f32)
        for c in range(HPL // CHUNK):
            own = [lane_head == CHUNK * c + i for i in range(CHUNK)]
            left = jnp.concatenate([jnp.where(o, q, 0.0).astype(bf16) for o in own], axis=0)
            scores = matmul(left, kt).reshape(CHUNK, rows, full)
            hs = slice(HPL * b + CHUNK * c, HPL * b + CHUNK * (c + 1))
            scores = scores + bias_ref[0, hs].astype(f32)
            out_ref[0, hs] = scores.astype(bf16)
            scores = scores + mask[None]
            highest = jnp.max(scores, axis=-1, keepdims=True)
            e = jnp.exp(scores - highest).astype(bf16)
            e_ref[0, hs] = e
            sums = matmul(e.reshape(CHUNK * rows, full), v)
            for i, o in enumerate(own):
                mixed = jnp.where(o, sums[rows * i : rows * (i + 1), :128], mixed)
                total = jnp.where(o, sums[rows * i : rows * (i + 1), 128:], total)
        inverse = 1.0 / total
        mix_ref[0, :, cols] = mixed * inverse
        rl_ref[0, :, cols] = inverse


def attention_forward(q, kt, v, bias, mask):
    slots, heads, rows, full = bias.shape
    step = min(STEP, heads)
    width = step * 8
    natural = lambda n: pl.BlockSpec((1, n, width), lambda s, h: (s, 0, h))
    pair = pl.BlockSpec((1, step, rows, full), lambda s, h: (s, h, 0, 0))
    return pl.pallas_call(
        forward_kernel,
        grid=(slots, heads // step),
        in_specs=[
            natural(rows),
            pl.BlockSpec((1, width, full), lambda s, h: (s, h, 0)),
            natural(full),
            pair,
            pl.BlockSpec((1, rows, full), lambda s, h: (s, 0, 0)),
        ],
        out_specs=[pair, pair, natural(rows), natural(rows)],
        out_shape=[
            jax.ShapeDtypeStruct(bias.shape, bf16),
            jax.ShapeDtypeStruct(bias.shape, bf16),
            jax.ShapeDtypeStruct(q.shape, f32),
            jax.ShapeDtypeStruct(q.shape, f32),
        ],
        name="attention_forward",
        cost_estimate=pl.CostEstimate(
            flops=2 * bias.size * 512, transcendentals=bias.size, bytes_accessed=bias.size * 6
        ),
        compiler_params=pltpu.CompilerParams(vmem_limit_bytes=48 << 20),
    )(q, kt, v, bias, mask)


def backward_kernel(
    qt_ref, dm_ref, dmt_ref, nm_ref, k_ref, vt_ref, e_ref, cot_ref, pg_ref, dq_ref, dkt_ref, dvt_ref
):
    _, heads, rows, full = cot_ref.shape
    lane_head = lax.broadcasted_iota(jnp.int32, (rows, 128), 1) // 8
    shape = (8 * CHUNK, CHUNK * rows)
    same = lax.broadcasted_iota(jnp.int32, shape, 0) // 8 == lax.broadcasted_iota(jnp.int32, shape, 1) // rows
    ones = jnp.ones((128, full), bf16)
    for b in range(heads // HPL):
        cols = slice(128 * b, 128 * b + 128)
        dm = dm_ref[0, :, cols].astype(f32)
        nm = nm_ref[0, :, cols].astype(f32)
        vt = jnp.concatenate([vt_ref[0, cols, :], ones], axis=0)
        k = k_ref[0, :, cols]
        dq = jnp.zeros((rows, 128), f32)
        for c in range(HPL // CHUNK):
            own = [lane_head == CHUNK * c + i for i in range(CHUNK)]
            left = jnp.concatenate(
                [
                    jnp.concatenate([jnp.where(o, dm, 0.0), jnp.where(o, nm, 0.0)], axis=1).astype(bf16)
                    for o in own
                ],
                axis=0,
            )
            centred = matmul(left, vt).reshape(CHUNK, rows, full)
            hs = slice(HPL * b + CHUNK * c, HPL * b + CHUNK * (c + 1))
            e = e_ref[0, hs]
            grad = (e.astype(f32) * centred + cot_ref[0, hs].astype(f32)).astype(bf16)
            pg_ref[0, hs] = grad
            grad = grad.reshape(CHUNK * rows, full)
            sums = matmul(grad, k)
            for i, o in enumerate(own):
                dq = jnp.where(o, sums[rows * i : rows * (i + 1)], dq)
            rs = slice(hs.start * 8, hs.stop * 8)
            spread = lambda ref: jnp.where(
                same, jnp.concatenate([ref[0, rs, :].astype(f32)] * CHUNK, axis=1), 0.0
            ).astype(bf16)
            dkt_ref[0, rs, :] = matmul(spread(qt_ref), grad).astype(bf16)
            dvt_ref[0, rs, :] = matmul(spread(dmt_ref), e.reshape(CHUNK * rows, full)).astype(bf16)
        dq_ref[0, :, cols] = dq.astype(bf16)


def attention_backward(qt, dm, dmt, nm, k, vt, e, cot):
    slots, heads, rows, full = cot.shape
    step = min(STEP, heads)
    width = step * 8
    natural = lambda n: pl.BlockSpec((1, n, width), lambda s, h: (s, 0, h))
    turned = lambda n: pl.BlockSpec((1, width, n), lambda s, h: (s, h, 0))
    pair = pl.BlockSpec((1, step, rows, full), lambda s, h: (s, h, 0, 0))
    return pl.pallas_call(
        backward_kernel,
        grid=(slots, heads // step),
        in_specs=[
            turned(rows),
            natural(rows),
            turned(rows),
            natural(rows),
            natural(full),
            turned(full),
            pair,
            pair,
        ],
        out_specs=[pair, natural(rows), turned(full), turned(full)],
        out_shape=[
            jax.ShapeDtypeStruct(cot.shape, bf16),
            jax.ShapeDtypeStruct(dm.shape, bf16),
            jax.ShapeDtypeStruct(vt.shape, bf16),
            jax.ShapeDtypeStruct(vt.shape, bf16),
        ],
        name="attention_backward",
        cost_estimate=pl.CostEstimate(
            flops=2 * cot.size * 768, transcendentals=0, bytes_accessed=cot.size * 6
        ),
        compiler_params=pltpu.CompilerParams(vmem_limit_bytes=48 << 20),
    )(qt, dm, dmt, nm, k, vt, e, cot)


def other_bit(index, bit, const):
    own = (index // (1 << bit)) % 2
    return 1 - own if (const >> bit) & 1 else own


def xor(index, const, bits):
    return sum(other_bit(index, b, const) * (1 << b) for b in range(bits))


def middle_kernel(
    parts,
    mix_ref,
    rl_ref,
    atoms_ref,
    dy_ref,
    small_ref,
    bias_ref,
    out_w,
    inner_w,
    outer_w,
    out_ref,
    a_keep,
    a_send,
    b_keep,
    b_send,
    c_keep,
    c_send,
    dm_ref,
    nm_ref,
    dmt_ref,
    dmid_ref,
    vec_ref,
    ow,
    iw,
    uw,
    act,
    dpre,
    dpre_in,
    inner,
    mixed,
    branch,
    branch_in,
    dyh,
    dy_in,
    grads,
    load_sem,
    send_sem,
    recv_sem,
):
    here, width = atoms_ref.shape
    half = width // 2
    blocks = act.shape[1]
    slots, _, rows = dmt_ref.shape
    bits = parts.bit_length() - 1
    row = lax.axis_index("rows")
    dp = lax.axis_index("dp")
    core = row % 2
    y = row // 2
    sibling = (dp, row + 1 - 2 * core)

    loads = [
        pltpu.make_async_copy(hbm, vmem, load_sem.at[i])
        for i, (hbm, vmem) in enumerate(((out_w, ow), (inner_w, iw), (outer_w, uw)))
    ]
    for copy in loads:
        copy.start()
    barrier = pltpu.get_barrier_semaphore()
    pl.semaphore_signal(barrier, inc=1, device_id=sibling, device_id_type=pl.DeviceIdType.MESH)
    pl.semaphore_wait(barrier, 1)
    sent = []

    def send(source, target):
        n = len(sent)
        copy = pltpu.make_async_remote_copy(
            src_ref=source,
            dst_ref=target,
            send_sem=send_sem.at[n],
            recv_sem=recv_sem.at[n],
            device_id=sibling,
            device_id_type=pl.DeviceIdType.MESH,
        )
        copy.start()
        sent.append(copy)

    dy = dy_ref[...]
    dyh[0] = dy[:, :half]
    dyh[1] = dy[:, half:]
    send(dyh.at[1 - core], dy_in)
    mix = mix_ref[...]
    mixed[0] = mix.astype(bf16)
    send(mixed.at[0], mixed.at[1])
    loads[0].wait()
    middle = atoms_ref[...].astype(f32) + matmul(mixed[0], ow[...]) + small_ref[0:1, :]
    standard, inverse = standardize(middle)
    gain = small_ref[1:2, :]
    inner[0] = (standard * gain + small_ref[2:3, :]).astype(bf16)
    send(inner.at[0], inner.at[1])
    loads[1].wait()
    loads[2].wait()
    result = middle + small_ref[3:4, :]
    grad_inner = jnp.zeros((here, width), f32)
    for b in range(blocks):
        cols = slice(width * b, width * (b + 1))
        pre = matmul(inner[0], iw[:, cols]) + bias_ref[:, cols]
        cdf = 0.5 + 0.5 * lax.erf(pre * (0.5**0.5))
        low = (pre * cdf).astype(bf16)
        act[0, b] = low
        send(act.at[0, b], act.at[1, b])
        slope = cdf + pre * (jnp.exp(-0.5 * pre * pre) * 0.3989422804014327)
        grad = (times_transposed(dy, uw[cols, :]) * slope).astype(bf16)
        dpre[b] = grad
        result = result + matmul(low, uw[cols, :])
        grad_inner = grad_inner + times_transposed(grad, iw[:, cols])
        vec_ref[b : b + 1, :] = jnp.sum(grad.astype(f32), axis=0, keepdims=True)
    for i in range(blocks // 2):
        send(dpre.at[(blocks // 2) * (1 - core) + i], dpre_in.at[i])
    out_ref[...] = result.astype(bf16)
    dy_wide = dy.astype(f32)
    grad_middle = dy_wide + norm_back(grad_inner * gain, standard, inverse)
    dmid_ref[...] = grad_middle
    low = grad_middle.astype(bf16)
    branch[0] = low[:, :half]
    branch[1] = low[:, half:]
    send(branch.at[1 - core], branch_in)
    down = lambda value: jnp.sum(value, axis=0, keepdims=True)
    vec_ref[blocks : blocks + 1, :] = down(low.astype(f32))
    vec_ref[blocks + 1 : blocks + 2, :] = down(grad_inner * standard)
    vec_ref[blocks + 2 : blocks + 3, :] = down(grad_inner)
    vec_ref[blocks + 3 : blocks + 4, :] = down(dy_wide)
    scaled = times_transposed(low, ow[...]).astype(bf16).astype(f32) * rl_ref[...]
    nm_ref[...] = (-scaled * mix).astype(bf16)
    scaled = scaled.astype(bf16)
    dm_ref[...] = scaled
    for s in range(slots):
        dmt_ref[s] = scaled[rows * s : rows * (s + 1)].astype(f32).T.astype(bf16)

    for copy in sent:
        copy.wait()
    tall, short = blocks * width // parts, width // parts
    dy_own = dyh[core]
    for b in range(blocks):
        grads[width * b : width * (b + 1), :] = outer_sum(act[0, b], dy_own) + outer_sum(act[1, b], dy_in[...])
    base = blocks * width
    for i in range(blocks // 2):
        grad = outer_sum(inner[0], dpre[(blocks // 2) * core + i]) + outer_sum(inner[1], dpre_in[i])
        for k in range(2):
            grads[base + width * (2 * i + k) : base + width * (2 * i + k + 1), :] = grad[:, half * k : half * (k + 1)]
    last = base + width * blocks
    grads[last:, :] = outer_sum(mixed[0], branch[core]) + outer_sum(mixed[1], branch_in[...])
    at = lambda start, n: grads[pl.ds(pl.multiple_of(start, 8), n), :]
    long, rest = tall // 8 * 3, tall // 4
    for p in range(parts):
        j = xor(dp, p, bits)
        ref = a_send if p & 1 else a_keep
        for r in range(2):
            h = other_bit(y, 0, r)
            ref[p >> 1, r] = at(j * tall + h * long, long).astype(ref.dtype)
        for r, ref in ((0, b_keep), (1, b_send)):
            h = other_bit(y, 0, r)
            for k in range(2):
                ref[p, short * k : short * (k + 1), :] = at(
                    base + width * (2 * h + k) + short * j, short
                ).astype(ref.dtype)
        ref = c_send if p & 2 else c_keep
        for r in range(2):
            h = other_bit(y, 0, r)
            start = h * (last + short * j) + (1 - h) * (j * tall + 2 * long)
            ref[(p >> 2) * 2 + (p & 1), r] = at(start, rest).astype(ref.dtype)


def middle(parts, mix, rl, atoms, dy, small, bias, out_w, inner_w, outer_w, slots):
    here, width = atoms.shape
    hidden = inner_w.shape[1]
    blocks, half, rows = hidden // width, width // 2, here // slots
    tall, short = hidden // parts, width // parts
    long, rest = tall // 8 * 3, tall // 4
    assert hidden == 4 * width and rest == short
    vm = pl.BlockSpec(memory_space=pltpu.VMEM)
    hbm = pl.BlockSpec(memory_space=pl.ANY)
    like = jax.ShapeDtypeStruct
    out_shape = [
        like((here, width), bf16),
        like((parts // 2, 2, long, half), f32),
        like((parts // 2, 2, long, half), bf16),
        like((parts, 2 * short, half), f32),
        like((parts, 2 * short, half), bf16),
        like((parts // 2, 2, rest, half), f32),
        like((parts // 2, 2, rest, half), bf16),
        like((here, width), bf16),
        like((here, width), bf16),
        like((slots, width, rows), bf16),
        like((here, width), f32),
        like((blocks + 4, width), f32),
    ]
    transfers = 3 + blocks + blocks // 2 + 1
    return pl.pallas_call(
        functools.partial(middle_kernel, parts),
        in_specs=[vm] * 6 + [hbm] * 3,
        out_specs=[vm] * len(out_shape),
        out_shape=out_shape,
        scratch_shapes=[
            pltpu.VMEM((width, width), bf16),
            pltpu.VMEM((width, hidden), bf16),
            pltpu.VMEM((hidden, width), bf16),
            pltpu.VMEM((2, blocks, here, width), bf16),
            pltpu.VMEM((blocks, here, width), bf16),
            pltpu.VMEM((blocks // 2, here, width), bf16),
            pltpu.VMEM((2, here, width), bf16),
            pltpu.VMEM((2, here, width), bf16),
            pltpu.VMEM((2, here, half), bf16),
            pltpu.VMEM((here, half), bf16),
            pltpu.VMEM((2, here, half), bf16),
            pltpu.VMEM((here, half), bf16),
            pltpu.VMEM((2 * hidden + width, half), f32),
            pltpu.SemaphoreType.DMA((3,)),
            pltpu.SemaphoreType.DMA((transfers,)),
            pltpu.SemaphoreType.DMA((transfers,)),
        ],
        name="middle",
        cost_estimate=pl.CostEstimate(
            flops=12 * here * width * hidden, transcendentals=2 * here * hidden, bytes_accessed=12 << 20
        ),
        compiler_params=pltpu.CompilerParams(
            vmem_limit_bytes=40 << 20, collective_id=1, has_side_effects=True
        ),
    )(mix, rl, atoms, dy, small, bias, out_w, inner_w, outer_w)


def attn_grad_kernel(scale, me_ref, normed_ref, own_ref, dq_ref, dkt_ref, dvt_ref, vec_ref, out_ref):
    parts = out_ref.shape[0]
    me = me_ref[0]
    short = normed_ref.shape[2] // parts
    slots = normed_ref.shape[0]

    def put(grad, at):
        grad = grad.astype(bf16)
        for j in range(parts):
            out_ref[me ^ j, pl.ds(at * short, short), :] = grad[short * j : short * (j + 1)]

    put(sum(outer_sum(own_ref[i], dq_ref[i]) for i in range(2)) * scale, 0)
    normed = [normed_ref[s].T for s in range(slots)]
    for at, ref in ((1, dkt_ref), (2, dvt_ref)):
        total = 0.0
        for s in range(slots):
            both = (ref[0, s].astype(f32) + ref[1, s].astype(f32)).astype(bf16)
            total = total + times_transposed(normed[s], both)
        put(total, at)
    out_ref[:, pl.ds(3 * short, 16), :] = vec_ref[...]


def attn_grads(me, parts, scale, normed, own, dq, dkt, dvt, vec):
    half = dq.shape[2]
    vm = pl.BlockSpec(memory_space=pltpu.VMEM)
    return pl.pallas_call(
        functools.partial(attn_grad_kernel, scale),
        in_specs=[pl.BlockSpec(memory_space=pltpu.SMEM)] + [vm] * 6,
        out_specs=vm,
        out_shape=jax.ShapeDtypeStruct((parts, 3 * normed.shape[2] // parts + 16, half), bf16),
        name="attn_grads",
        cost_estimate=pl.CostEstimate(flops=2 * 768 * 512 * 768, transcendentals=0, bytes_accessed=4 << 20),
        compiler_params=pltpu.CompilerParams(vmem_limit_bytes=40 << 20),
    )(me, normed, own, dq, dkt, dvt, vec)


def make_swap(parts, group):
    def swap(array, dp_bit=None, row_bit=None):
        pairs = []
        for d in range(parts):
            for r in range(group):
                e = d if dp_bit is None else d ^ (1 << dp_bit)
                t = r if row_bit is None else r ^ (1 << row_bit)
                pairs.append((d * group + r, e * group + t))
        return lax.ppermute(array, ("dp", "rows"), pairs)

    return swap


def add_low(left, right):
    return (left.astype(f32) + right.astype(f32)).astype(bf16)


def fold(swap, grads, bit):
    count = grads.shape[0]
    low = 1 << bit
    view = grads.reshape((count // (2 * low), 2, low) + grads.shape[1:])
    got = swap(view[:, 1], dp_bit=bit)
    return view[:, 0], got


def scatter_first(swap, grads, bits):
    remaining = list(bits)
    for n, bit in enumerate(remaining):
        view, got = fold_at(swap, grads, bit, remaining[n + 1 :])
        grads = add_low(view, got)
    return grads


def fold_at(swap, grads, bit, later):
    at = sum(1 for b in later if b < bit)
    low = 1 << at
    view = grads.reshape((grads.shape[0] // (2 * low), 2, low) + grads.shape[1:])
    keep, send = view[:, 0], view[:, 1]
    flat = lambda a: a.reshape((-1,) + grads.shape[1:])
    return flat(keep), swap(flat(send), dp_bit=bit)


def reduce_x_first(swap, grads, bits):
    total = scatter_first(swap, grads, bits)[0]
    return total.astype(f32) + swap(total, row_bit=1).astype(f32)


def reduce_y_first(swap, grads, bits, y):
    parts, rows, half = grads.shape
    view = grads.reshape(parts, 2, rows // 2, half)
    keep = lax.dynamic_index_in_dim(view, y, 1, keepdims=False)
    send = lax.dynamic_index_in_dim(view, 1 - y, 1, keepdims=False)
    total = scatter_first(swap, add_low(keep, swap(send, row_bit=1)), bits)[0]
    other = swap(total, row_bit=1)
    lower = jnp.where(y == 0, total, other)
    upper = jnp.where(y == 0, other, total)
    return jnp.concatenate([lower, upper], axis=0).astype(f32)


def local(
    parts,
    group,
    atoms,
    pair_bias,
    mol_counts,
    attn_gain,
    attn_shift,
    query_weight,
    query_bias,
    key_weight,
    value_weight,
    value_bias,
    out_weight,
    out_bias,
    ffn_gain,
    ffn_shift,
    inner_weight,
    inner_bias,
    outer_weight,
    outer_bias,
    atoms_cotangent,
    pair_cotangent,
):
    slots, part_rows, width = atoms.shape
    heads = pair_bias.shape[1]
    full = pair_bias.shape[3]
    depth = width // heads
    scale = depth ** (-0.5)
    here = slots * part_rows
    hidden = inner_weight.shape[1]
    half = width // 2
    swap = make_swap(parts, group)
    row = lax.axis_index("rows")
    core, y = row % 2, row // 2
    dp = lax.axis_index("dp")
    me = dp.astype(jnp.int32).reshape(1)
    dp_bits = list(range(parts.bit_length() - 1))

    sibling = swap(atoms, row_bit=0)
    across = swap(atoms, row_bit=1)
    corner = swap(across, row_bit=0)
    stack = jnp.stack([atoms, sibling, across, corner])
    order = jnp.arange(group, dtype=jnp.int32) ^ row
    atoms_all = jnp.take(stack, order, axis=0)
    atoms_all = jnp.swapaxes(atoms_all, 0, 1).reshape(slots, full, width)

    cumulative = jnp.cumsum(mol_counts, axis=1)
    position = jnp.arange(full, dtype=jnp.int32)
    segment = jnp.sum(
        (cumulative[:, None, :] <= position[None, :, None]).astype(jnp.int32), axis=-1
    )
    query_segment = lax.dynamic_slice_in_dim(segment, row * part_rows, part_rows, 1)
    mask = jnp.where(query_segment[:, :, None] == segment[:, None, :], 0.0, -BIG).astype(f32)

    gain_one = attn_gain.astype(f32)
    shift_one = attn_shift.astype(f32)
    atoms_flat = atoms.astype(f32).reshape(here, width)
    standard_one, inverse_one = standardize(atoms_flat)
    normed = (standard_one * gain_one + shift_one).astype(bf16)
    standard_sib, _ = standardize(sibling.astype(f32).reshape(here, width))
    normed_sib = (standard_sib * gain_one + shift_one).astype(bf16)
    standard_all, _ = standardize(atoms_all.astype(f32).reshape(slots * full, width))
    normed_all = (standard_all * gain_one + shift_one).astype(bf16)
    queries = ((matmul(normed, query_weight) + query_bias.astype(f32)) * scale).astype(bf16)
    keys = matmul(normed_all, key_weight).astype(bf16).reshape(slots, full, width)
    values = (matmul(normed_all, value_weight) + value_bias.astype(f32)).astype(bf16)
    values = values.reshape(slots, full, width)
    queries = queries.reshape(slots, part_rows, width)
    turn = lambda a: jnp.swapaxes(a, 1, 2)
    values_turned = turn(values)
    pair_out, weights, mixed_wide, inverse_sum = attention_forward(
        queries, turn(keys), values, pair_bias, mask
    )
    small = jnp.stack([out_bias, ffn_gain, ffn_shift, outer_bias]).astype(f32)
    (
        atoms_out,
        a_keep,
        a_send,
        b_keep,
        b_send,
        c_keep,
        c_send,
        scaled,
        centre,
        scaled_turned,
        grad_middle,
        middle_vectors,
    ) = middle(
        parts,
        mixed_wide.reshape(here, width),
        inverse_sum.reshape(here, width),
        atoms.reshape(here, width),
        atoms_cotangent.reshape(here, width),
        small,
        inner_bias.astype(f32).reshape(1, hidden),
        out_weight,
        inner_weight,
        outer_weight,
        slots,
    )
    atoms_out = atoms_out.reshape(slots, part_rows, width)

    nbits = len(dp_bits)
    names = ["d%d" % b for b in reversed(dp_bits)] + ["y"]

    def tagged(array, used):
        left = [n for n in names if n != used]
        return array.reshape((2,) * len(left) + array.shape[-2:]), left

    def partner(array, name):
        return swap(array, row_bit=1) if name == "y" else swap(array, dp_bit=int(name[1:]))

    def stage(array, left, name):
        axis = left.index(name)
        keep = lax.index_in_dim(array, 0, axis, keepdims=False)
        send = lax.index_in_dim(array, 1, axis, keepdims=False).astype(bf16)
        return keep.astype(f32) + partner(send, name).astype(f32), [n for n in left if n != name]

    def begin(keep, send, name):
        array, left = tagged(keep, name)
        got, _ = tagged(partner(send, name), name)
        return array + got.astype(f32), left

    def finish(array, left, order):
        for name in order:
            array, left = stage(array, left, name)
        other = swap(array.astype(bf16), row_bit=1).astype(f32)
        return jnp.where(y == 0, jnp.stack([array, other]), jnp.stack([other, array]))

    a_part, a_left = begin(a_keep, a_send, "d0")
    b_part, b_left = begin(
        b_keep.reshape((parts,) + b_keep.shape[1:]), b_send.reshape((parts,) + b_send.shape[1:]), "y"
    )
    c_part, c_left = begin(c_keep, c_send, "d1")
    more = ["d%d" % b for b in dp_bits[2:]]
    a_total = finish(a_part, a_left, ["y", "d1"] + more)
    b_total = finish(b_part, b_left, ["d1", "d0"] + more)
    c_total = finish(c_part, c_left, ["d0", "y"] + more)

    def pick(array, which):
        return lax.dynamic_slice_in_dim(array, which * (array.shape[1] // 2), array.shape[1] // 2, 1)

    pair_of = lambda own, send: jnp.stack([own, swap(send, row_bit=0)])

    scaled = scaled.reshape(queries.shape)
    centre = centre.reshape(queries.shape)
    pair_grad, grad_queries, dkt, dvt = attention_backward(
        turn(queries), scaled, scaled_turned, centre, keys, values_turned, weights, pair_cotangent
    )
    grad_queries = grad_queries.reshape(here, width)

    partial = jnp.einsum("sok,io->ski", dkt, key_weight, preferred_element_type=f32) + jnp.einsum(
        "sok,io->ski", dvt, value_weight, preferred_element_type=f32
    )
    partial = partial.astype(bf16).reshape(slots, group, part_rows, width)
    partial = jnp.take(jnp.swapaxes(partial, 0, 1), order, axis=0)
    partial = partial.reshape(2, 2, slots, part_rows, width)
    chip = add_low(partial[:, 0], swap(partial[:, 1], row_bit=0))
    grad_normed = (
        times_transposed(grad_queries, query_weight) * scale
        + (chip[0].astype(f32) + swap(chip[1], row_bit=1).astype(f32)).reshape(here, width)
    )
    atoms_grad = grad_middle + norm_back(grad_normed * gain_one, standard_one, inverse_one)
    atoms_grad = atoms_grad.astype(bf16).reshape(slots, part_rows, width)

    short = (
        jnp.sum(grad_normed * standard_one, axis=0),
        jnp.sum(grad_normed, axis=0),
        jnp.sum(grad_queries.astype(f32), axis=0) * scale,
        jnp.sum(dvt.astype(f32), axis=(0, 2)),
        middle_vectors[4],
        middle_vectors[5],
        middle_vectors[6],
        middle_vectors[7],
    )
    vectors = jnp.concatenate(
        [v.reshape(parts, -1) for v in short] + [middle_vectors[:4].reshape(parts, -1)],
        axis=1,
    )
    vectors = vectors + swap(vectors, row_bit=0)
    vectors = jnp.take(vectors, jnp.arange(parts, dtype=jnp.int32) ^ dp, axis=0)
    vec = jnp.pad(vectors.astype(bf16), ((0, 0), (0, 16 * half - vectors.shape[1]))).reshape(parts, 16, half)

    def pick_rows(array, which):
        return lax.dynamic_slice_in_dim(array, which * half, half, 1)

    attn_packed = attn_grads(
        me,
        parts,
        scale,
        normed_all.reshape(slots, full, width),
        jnp.stack([normed, normed_sib]),
        pair_of(pick(grad_queries, core), pick(grad_queries, 1 - core)),
        pair_of(pick_rows(dkt, core), pick_rows(dkt, 1 - core)),
        pair_of(pick_rows(dvt, core), pick_rows(dvt, 1 - core)),
        vec,
    )
    share = width // parts
    third_total = reduce_x_first(swap, attn_packed[:, : attn_packed.shape[1] // 2], dp_bits)
    fourth_total = reduce_y_first(swap, attn_packed[:, attn_packed.shape[1] // 2 :], dp_bits, y)

    first = jnp.concatenate([a_total.reshape(-1, half), c_total[0]], axis=0)
    total = jnp.concatenate([first, b_total.reshape(-1, half), c_total[1], third_total, fourth_total], axis=0)
    other = swap(total, row_bit=0)
    left = jnp.where(core == 0, total, other)
    right = jnp.where(core == 0, other, total)
    joined = jnp.stack([left, right])
    outer_share = hidden // parts
    blocks = hidden // 2 // half

    def flat(a, n):
        return jnp.swapaxes(joined[:, a : a + n], 0, 1).reshape(n, width)

    grad_outer_weight = flat(0, outer_share)
    a = outer_share
    grad_inner_weight = joined[:, a : a + share * blocks].reshape(2, blocks, share, half)
    grad_inner_weight = grad_inner_weight.transpose(2, 0, 1, 3).reshape(share, hidden)
    a += share * blocks
    grad_out_weight = flat(a, share)
    a += share
    grad_query_weight, grad_key_weight, grad_value_weight = (flat(a + share * i, share) for i in range(3))
    a += 3 * share
    vec_total = joined[0, a : a + 16].reshape(-1)
    v = [vec_total[share * i : share * (i + 1)] for i in range(8)]
    grad_inner_bias = vec_total[8 * share : 8 * share + outer_share]
    return (
        atoms_out,
        pair_out,
        atoms_grad,
        pair_grad,
        v[0],
        v[1],
        grad_query_weight,
        v[2],
        grad_key_weight,
        grad_value_weight,
        v[3],
        grad_out_weight,
        v[4],
        v[5],
        v[6],
        grad_inner_weight,
        grad_inner_bias,
        grad_outer_weight,
        v[7],
    )


def solution(mesh):
    one, two = P("dp"), P("dp", None)
    atoms_spec, pair_spec = P("dp", "rows", None), P("dp", None, "rows", None)
    in_specs = (atoms_spec, pair_spec, two) + (P(),) * 15 + (atoms_spec, pair_spec)
    out_specs = (
        (atoms_spec, pair_spec, atoms_spec, pair_spec, one, one, two, one, two, two, one, two)
        + (one, one, one, two, one, two, one)
    )
    run = functools.partial(local, mesh.shape["dp"], mesh.shape["rows"])
    return jax.shard_map(run, mesh=mesh, in_specs=in_specs, out_specs=out_specs, check_vma=False)
```

```python
import functools

import jax
import jax.numpy as jnp
from jax import lax
from jax.experimental import pallas as pl
from jax.experimental.pallas import tpu as pltpu
from jax.sharding import PartitionSpec as P

f32, bf16 = jnp.float32, jnp.bfloat16
BIG = 1e9
HPL = 16
CHUNK = 8
STEP = 32
VMEM_PAIR = 24 << 20
MESH = pl.DeviceIdType.MESH


def standardize(value):
    centred = value - jnp.mean(value, axis=-1, keepdims=True)
    inverse = lax.rsqrt(jnp.mean(centred * centred, axis=-1, keepdims=True) + 1e-05)
    return (centred * inverse, inverse)


def norm_back(grad_normed, standard, inverse):
    return inverse * (
        grad_normed
        - jnp.mean(grad_normed, axis=-1, keepdims=True)
        - standard * jnp.mean(grad_normed * standard, axis=-1, keepdims=True)
    )


def matmul(left, right):
    return jnp.dot(left, right, preferred_element_type=f32)


def times_transposed(left, right):
    return lax.dot_general(left, right, (((1,), (1,)), ((), ())), preferred_element_type=f32)


def outer_sum(left, right):
    return lax.dot_general(left, right, (((0,), (0,)), ((), ())), preferred_element_type=f32)


def other_bit(index, bit, const):
    own = (index // (1 << bit)) % 2
    return 1 - own if (const >> bit) & 1 else own


def xor(index, const, bits):
    return sum(other_bit(index, b, const) * (1 << b) for b in range(bits))


def remote(source, target, send_sem, recv_sem, device):
    copy = pltpu.make_async_remote_copy(
        src_ref=source, dst_ref=target, send_sem=send_sem, recv_sem=recv_sem, device_id=device, device_id_type=MESH
    )
    copy.start()
    return copy


def meet(devices):
    barrier = pltpu.get_barrier_semaphore()
    for device in devices:
        pl.semaphore_signal(barrier, inc=1, device_id=device, device_id_type=MESH)
    pl.semaphore_wait(barrier, len(devices))


def front_kernel(
    scale,
    atoms_ref,
    counts_ref,
    small_ref,
    query_w,
    key_w,
    value_w,
    all_ref,
    mask_ref,
    q_ref,
    qt_ref,
    k_ref,
    kt_ref,
    v_ref,
    vt_ref,
    qw,
    kw,
    vw,
    gathered,
    load_sem,
    send_sem,
    recv_sem,
):
    slots, rows, width = atoms_ref.shape
    full = mask_ref.shape[2]
    row, dp = lax.axis_index("rows"), lax.axis_index("dp")
    core, y = row % 2, row // 2
    beside, across = row + 1 - 2 * core, row + 2 - 4 * y
    loads = [
        pltpu.make_async_copy(hbm, vmem, load_sem.at[i])
        for i, (hbm, vmem) in enumerate(((query_w, qw), (key_w, kw), (value_w, vw)))
    ]
    for copy in loads:
        copy.start()
    meet([(dp, beside), (dp, across)])
    far = [
        remote(atoms_ref.at[s], gathered.at[row, s], send_sem.at[s], recv_sem.at[s], (dp, across))
        for s in range(slots)
    ]
    near = [
        remote(atoms_ref.at[s], gathered.at[row, s], send_sem.at[slots + s], recv_sem.at[slots + s], (dp, beside))
        for s in range(slots)
    ]
    gain, shift = small_ref[0:1, :], small_ref[1:2, :]
    for s in range(slots):
        gathered[row, s] = atoms_ref[s]
        ends = [counts_ref[s, 0]]
        for m in range(1, counts_ref.shape[1]):
            ends.append(ends[-1] + counts_ref[s, m])
        keys_at = lax.broadcasted_iota(jnp.int32, (rows, full), 1)
        queries_at = lax.broadcasted_iota(jnp.int32, (rows, full), 0) + row * rows
        count = lambda at: sum((end <= at).astype(jnp.int32) for end in ends)
        mask_ref[s] = jnp.where(count(keys_at) == count(queries_at), 0.0, -BIG)
    own = atoms_ref[...].reshape(slots * rows, width).astype(f32)
    normed = (standardize(own)[0] * gain + shift).astype(bf16)
    loads[0].wait()
    queries = ((matmul(normed, qw[...]) + small_ref[2:3, :]) * scale).astype(bf16)
    for s in range(slots):
        part = queries[rows * s : rows * (s + 1)]
        q_ref[s] = part
        qt_ref[s] = part.T
    loads[1].wait()
    loads[2].wait()
    forward = []
    for s in range(slots):
        far[s].wait()
        n = 2 * slots + s
        forward.append(
            remote(gathered.at[across, s], gathered.at[across, s], send_sem.at[n], recv_sem.at[n], (dp, beside))
        )
    for s in range(slots):
        near[s].wait()
        forward[s].wait()
        whole = jnp.concatenate([gathered[i, s] for i in range(full // rows)], axis=0)
        all_ref[s] = whole
        normed = (standardize(whole.astype(f32))[0] * gain + shift).astype(bf16)
        keys = matmul(normed, kw[...]).astype(bf16)
        k_ref[s] = keys
        kt_ref[s] = keys.T
        values = (matmul(normed, vw[...]) + small_ref[3:4, :]).astype(bf16)
        v_ref[s] = values
        vt_ref[s] = values.T


def front(scale, full, atoms, counts, small, query_w, key_w, value_w):
    slots, rows, width = atoms.shape
    vm = pl.BlockSpec(memory_space=pltpu.VMEM)
    hbm = pl.BlockSpec(memory_space=pl.ANY)
    like = lambda *shape: jax.ShapeDtypeStruct(shape, bf16)
    out_shape = [
        like(slots, full, width),
        jax.ShapeDtypeStruct((slots, rows, full), f32),
        like(slots, rows, width),
        like(slots, width, rows),
        like(slots, full, width),
        like(slots, width, full),
        like(slots, full, width),
        like(slots, width, full),
    ]
    return pl.pallas_call(
        functools.partial(front_kernel, scale),
        in_specs=[vm, pl.BlockSpec(memory_space=pltpu.SMEM), vm, hbm, hbm, hbm],
        out_specs=[vm] * len(out_shape),
        out_shape=out_shape,
        scratch_shapes=[pltpu.VMEM((width, width), bf16)] * 3
        + [
            pltpu.VMEM((full // rows, slots, rows, width), bf16),
            pltpu.SemaphoreType.DMA((3,)),
            pltpu.SemaphoreType.DMA((3 * slots,)),
            pltpu.SemaphoreType.DMA((3 * slots,)),
        ],
        name="front",
        cost_estimate=pl.CostEstimate(
            flops=4 * slots * full * width * width, transcendentals=0, bytes_accessed=8 << 20
        ),
        compiler_params=pltpu.CompilerParams(vmem_limit_bytes=32 << 20, collective_id=0, has_side_effects=True),
    )(atoms, counts, small, query_w, key_w, value_w)


def forward_kernel(q_ref, kt_ref, v_ref, bias_ref, mask_ref, out_ref, e_ref, mix_ref, rl_ref):
    _, heads, rows, full = bias_ref.shape
    lane_head = lax.broadcasted_iota(jnp.int32, (rows, 128), 1) // 8
    mask = mask_ref[0]
    ones = jnp.ones((full, 128), bf16)
    for b in range(heads // HPL):
        cols = slice(128 * b, 128 * b + 128)
        q = q_ref[0, :, cols].astype(f32)
        kt = kt_ref[0, cols, :]
        v = jnp.concatenate([v_ref[0, :, cols], ones], axis=1)
        mixed = jnp.zeros((rows, 128), f32)
        total = jnp.zeros((rows, 128), f32)
        for c in range(HPL // CHUNK):
            own = [lane_head == CHUNK * c + i for i in range(CHUNK)]
            left = jnp.concatenate([jnp.where(o, q, 0.0).astype(bf16) for o in own], axis=0)
            scores = matmul(left, kt).reshape(CHUNK, rows, full)
            hs = slice(HPL * b + CHUNK * c, HPL * b + CHUNK * (c + 1))
            scores = scores + bias_ref[0, hs].astype(f32)
            out_ref[0, hs] = scores.astype(bf16)
            scores = scores + mask[None]
            highest = jnp.max(scores, axis=-1, keepdims=True)
            e = jnp.exp(scores - highest).astype(bf16)
            e_ref[0, hs] = e
            sums = matmul(e.reshape(CHUNK * rows, full), v)
            for i, o in enumerate(own):
                mixed = jnp.where(o, sums[rows * i : rows * (i + 1), :128], mixed)
                total = jnp.where(o, sums[rows * i : rows * (i + 1), 128:], total)
        inverse = 1.0 / total
        mix_ref[0, :, cols] = mixed * inverse
        rl_ref[0, :, cols] = inverse


def attention_forward(q, kt, v, bias, mask):
    slots, heads, rows, full = bias.shape
    step = min(STEP, heads)
    width = step * 8
    natural = lambda n: pl.BlockSpec((1, n, width), lambda s, h: (s, 0, h))
    pair = pl.BlockSpec((1, step, rows, full), lambda s, h: (s, h, 0, 0))
    return pl.pallas_call(
        forward_kernel,
        grid=(slots, heads // step),
        in_specs=[
            natural(rows),
            pl.BlockSpec((1, width, full), lambda s, h: (s, h, 0)),
            natural(full),
            pair,
            pl.BlockSpec((1, rows, full), lambda s, h: (s, 0, 0)),
        ],
        out_specs=[pair, pair, natural(rows), natural(rows)],
        out_shape=[
            jax.ShapeDtypeStruct(bias.shape, bf16),
            jax.ShapeDtypeStruct(bias.shape, bf16),
            jax.ShapeDtypeStruct(q.shape, f32),
            jax.ShapeDtypeStruct(q.shape, f32),
        ],
        name="attention_forward",
        cost_estimate=pl.CostEstimate(
            flops=2 * bias.size * 512, transcendentals=bias.size, bytes_accessed=bias.size * 6
        ),
        compiler_params=pltpu.CompilerParams(vmem_limit_bytes=VMEM_PAIR),
    )(q, kt, v, bias, mask)


def backward_kernel(
    qt_ref, dm_ref, dmt_ref, nm_ref, k_ref, vt_ref, e_ref, cot_ref, pg_ref, dq_ref, dkt_ref, dvt_ref
):
    _, heads, rows, full = cot_ref.shape
    lane_head = lax.broadcasted_iota(jnp.int32, (rows, 128), 1) // 8
    shape = (8 * CHUNK, CHUNK * rows)
    same = lax.broadcasted_iota(jnp.int32, shape, 0) // 8 == lax.broadcasted_iota(jnp.int32, shape, 1) // rows
    ones = jnp.ones((128, full), bf16)
    for b in range(heads // HPL):
        cols = slice(128 * b, 128 * b + 128)
        dm = dm_ref[0, :, cols].astype(f32)
        nm = nm_ref[0, :, cols].astype(f32)
        vt = jnp.concatenate([vt_ref[0, cols, :], ones], axis=0)
        k = k_ref[0, :, cols]
        dq = jnp.zeros((rows, 128), f32)
        for c in range(HPL // CHUNK):
            own = [lane_head == CHUNK * c + i for i in range(CHUNK)]
            left = jnp.concatenate(
                [
                    jnp.concatenate([jnp.where(o, dm, 0.0), jnp.where(o, nm, 0.0)], axis=1).astype(bf16)
                    for o in own
                ],
                axis=0,
            )
            centred = matmul(left, vt).reshape(CHUNK, rows, full)
            hs = slice(HPL * b + CHUNK * c, HPL * b + CHUNK * (c + 1))
            e = e_ref[0, hs]
            grad = (e.astype(f32) * centred + cot_ref[0, hs].astype(f32)).astype(bf16)
            pg_ref[0, hs] = grad
            grad = grad.reshape(CHUNK * rows, full)
            sums = matmul(grad, k)
            for i, o in enumerate(own):
                dq = jnp.where(o, sums[rows * i : rows * (i + 1)], dq)
            rs = slice(hs.start * 8, hs.stop * 8)
            spread = lambda ref: jnp.where(
                same, jnp.concatenate([ref[0, rs, :].astype(f32)] * CHUNK, axis=1), 0.0
            ).astype(bf16)
            dkt_ref[0, rs, :] = matmul(spread(qt_ref), grad).astype(bf16)
            dvt_ref[0, rs, :] = matmul(spread(dmt_ref), e.reshape(CHUNK * rows, full)).astype(bf16)
        dq_ref[0, :, cols] = dq.astype(bf16)


def attention_backward(qt, dm, dmt, nm, k, vt, e, cot):
    slots, heads, rows, full = cot.shape
    step = min(STEP, heads)
    width = step * 8
    natural = lambda n: pl.BlockSpec((1, n, width), lambda s, h: (s, 0, h))
    turned = lambda n: pl.BlockSpec((1, width, n), lambda s, h: (s, h, 0))
    pair = pl.BlockSpec((1, step, rows, full), lambda s, h: (s, h, 0, 0))
    return pl.pallas_call(
        backward_kernel,
        grid=(slots, heads // step),
        in_specs=[
            turned(rows),
            natural(rows),
            turned(rows),
            natural(rows),
            natural(full),
            turned(full),
            pair,
            pair,
        ],
        out_specs=[pair, natural(rows), turned(full), turned(full)],
        out_shape=[
            jax.ShapeDtypeStruct(cot.shape, bf16),
            jax.ShapeDtypeStruct(dm.shape, bf16),
            jax.ShapeDtypeStruct(vt.shape, bf16),
            jax.ShapeDtypeStruct(vt.shape, bf16),
        ],
        name="attention_backward",
        cost_estimate=pl.CostEstimate(
            flops=2 * cot.size * 768, transcendentals=0, bytes_accessed=cot.size * 6
        ),
        compiler_params=pltpu.CompilerParams(vmem_limit_bytes=VMEM_PAIR),
    )(qt, dm, dmt, nm, k, vt, e, cot)


def middle_kernel(
    parts,
    mix_ref,
    rl_ref,
    atoms_ref,
    dy_ref,
    small_ref,
    bias_ref,
    out_w,
    inner_w,
    outer_w,
    out_ref,
    a_keep,
    a_send,
    b_keep,
    b_send,
    c_keep,
    c_send,
    dm_ref,
    nm_ref,
    dmt_ref,
    dmid_ref,
    vec_ref,
    ow,
    iw,
    uw,
    act,
    dpre,
    dpre_in,
    inner,
    mixed,
    branch,
    branch_in,
    dyh,
    dy_in,
    grads,
    load_sem,
    send_sem,
    recv_sem,
):
    here, width = atoms_ref.shape
    half = width // 2
    blocks = act.shape[1]
    slots, _, rows = dmt_ref.shape
    bits = parts.bit_length() - 1
    row = lax.axis_index("rows")
    dp = lax.axis_index("dp")
    core = row % 2
    y = row // 2
    sibling = (dp, row + 1 - 2 * core)

    loads = [
        pltpu.make_async_copy(hbm, vmem, load_sem.at[i])
        for i, (hbm, vmem) in enumerate(((out_w, ow), (inner_w, iw), (outer_w, uw)))
    ]
    for copy in loads:
        copy.start()
    barrier = pltpu.get_barrier_semaphore()
    pl.semaphore_signal(barrier, inc=1, device_id=sibling, device_id_type=pl.DeviceIdType.MESH)
    pl.semaphore_wait(barrier, 1)
    sent = []

    def send(source, target):
        n = len(sent)
        copy = pltpu.make_async_remote_copy(
            src_ref=source,
            dst_ref=target,
            send_sem=send_sem.at[n],
            recv_sem=recv_sem.at[n],
            device_id=sibling,
            device_id_type=pl.DeviceIdType.MESH,
        )
        copy.start()
        sent.append(copy)

    dy = dy_ref[...]
    dyh[0] = dy[:, :half]
    dyh[1] = dy[:, half:]
    send(dyh.at[1 - core], dy_in)
    mix = mix_ref[...]
    mixed[0] = mix.astype(bf16)
    send(mixed.at[0], mixed.at[1])
    loads[0].wait()
    middle = atoms_ref[...].astype(f32) + matmul(mixed[0], ow[...]) + small_ref[4:5, :]
    standard, inverse = standardize(middle)
    gain = small_ref[5:6, :]
    inner[0] = (standard * gain + small_ref[6:7, :]).astype(bf16)
    send(inner.at[0], inner.at[1])
    loads[1].wait()
    loads[2].wait()
    result = middle + small_ref[7:8, :]
    grad_inner = jnp.zeros((here, width), f32)
    for b in range(blocks):
        cols = slice(width * b, width * (b + 1))
        pre = matmul(inner[0], iw[:, cols]) + bias_ref[:, cols]
        cdf = 0.5 + 0.5 * lax.erf(pre * (0.5**0.5))
        low = (pre * cdf).astype(bf16)
        act[0, b] = low
        send(act.at[0, b], act.at[1, b])
        slope = cdf + pre * (jnp.exp(-0.5 * pre * pre) * 0.3989422804014327)
        grad = (times_transposed(dy, uw[cols, :]) * slope).astype(bf16)
        dpre[b] = grad
        result = result + matmul(low, uw[cols, :])
        grad_inner = grad_inner + times_transposed(grad, iw[:, cols])
        vec_ref[b : b + 1, :] = jnp.sum(grad.astype(f32), axis=0, keepdims=True)
    for i in range(blocks // 2):
        send(dpre.at[(blocks // 2) * (1 - core) + i], dpre_in.at[i])
    out_ref[...] = result.astype(bf16)
    dy_wide = dy.astype(f32)
    grad_middle = dy_wide + norm_back(grad_inner * gain, standard, inverse)
    dmid_ref[...] = grad_middle
    low = grad_middle.astype(bf16)
    branch[0] = low[:, :half]
    branch[1] = low[:, half:]
    send(branch.at[1 - core], branch_in)
    down = lambda value: jnp.sum(value, axis=0, keepdims=True)
    vec_ref[blocks : blocks + 1, :] = down(low.astype(f32))
    vec_ref[blocks + 1 : blocks + 2, :] = down(grad_inner * standard)
    vec_ref[blocks + 2 : blocks + 3, :] = down(grad_inner)
    vec_ref[blocks + 3 : blocks + 4, :] = down(dy_wide)
    scaled = times_transposed(low, ow[...]).astype(bf16).astype(f32) * rl_ref[...]
    nm_ref[...] = (-scaled * mix).astype(bf16)
    scaled = scaled.astype(bf16)
    dm_ref[...] = scaled
    for s in range(slots):
        dmt_ref[s] = scaled[rows * s : rows * (s + 1)].astype(f32).T.astype(bf16)

    for copy in sent:
        copy.wait()
    tall, short = blocks * width // parts, width // parts
    dy_own = dyh[core]
    for b in range(blocks):
        grads[width * b : width * (b + 1), :] = outer_sum(act[0, b], dy_own) + outer_sum(act[1, b], dy_in[...])
    base = blocks * width
    for i in range(blocks // 2):
        grad = outer_sum(inner[0], dpre[(blocks // 2) * core + i]) + outer_sum(inner[1], dpre_in[i])
        for k in range(2):
            grads[base + width * (2 * i + k) : base + width * (2 * i + k + 1), :] = grad[:, half * k : half * (k + 1)]
    last = base + width * blocks
    grads[last:, :] = outer_sum(mixed[0], branch[core]) + outer_sum(mixed[1], branch_in[...])

    def at(start, n, h):
        return grads[pl.ds(pl.multiple_of(start, 8), n), pl.ds(pl.multiple_of(h * 128, 128), 128)]

    rest = tall // 4
    long = tall - rest
    for p in range(parts):
        j = xor(dp, p, bits)
        for r in range(2):
            h = other_bit(y, 0, r)
            ref = a_send if p & 1 else a_keep
            ref[2 * (p >> 1) + r] = at(j * tall, long, h).astype(ref.dtype)
            ref = b_send if r else b_keep
            for k in range(blocks):
                ref[p, short * k : short * (k + 1)] = at(base + width * k + short * j, short, h).astype(ref.dtype)
            ref = c_send if p & 2 else c_keep
            q = 2 * ((p >> 2) * 2 + (p & 1)) + r
            ref[q, :rest] = at(j * tall + long, rest, h).astype(ref.dtype)
            ref[q, rest:] = at(last + short * j, short, h).astype(ref.dtype)


def middle(parts, mix, rl, atoms, dy, small, bias, out_w, inner_w, outer_w, slots):
    here, width = atoms.shape
    hidden = inner_w.shape[1]
    blocks, half, rows = hidden // width, width // 2, here // slots
    tall, short = hidden // parts, width // parts
    rest = tall // 4
    long = tall - rest
    assert hidden == 4 * width
    vm = pl.BlockSpec(memory_space=pltpu.VMEM)
    hbm = pl.BlockSpec(memory_space=pl.ANY)
    like = jax.ShapeDtypeStruct
    out_shape = [
        like((here, width), bf16),
        like((parts, long, 128), f32),
        like((parts, long, 128), bf16),
        like((parts, blocks * short, 128), f32),
        like((parts, blocks * short, 128), bf16),
        like((parts, rest + short, 128), f32),
        like((parts, rest + short, 128), bf16),
        like((here, width), bf16),
        like((here, width), bf16),
        like((slots, width, rows), bf16),
        like((here, width), f32),
        like((blocks + 4, width), f32),
    ]
    transfers = 3 + blocks + blocks // 2 + 1
    return pl.pallas_call(
        functools.partial(middle_kernel, parts),
        in_specs=[vm] * 6 + [hbm] * 3,
        out_specs=[vm] * len(out_shape),
        out_shape=out_shape,
        scratch_shapes=[
            pltpu.VMEM((width, width), bf16),
            pltpu.VMEM((width, hidden), bf16),
            pltpu.VMEM((hidden, width), bf16),
            pltpu.VMEM((2, blocks, here, width), bf16),
            pltpu.VMEM((blocks, here, width), bf16),
            pltpu.VMEM((blocks // 2, here, width), bf16),
            pltpu.VMEM((2, here, width), bf16),
            pltpu.VMEM((2, here, width), bf16),
            pltpu.VMEM((2, here, half), bf16),
            pltpu.VMEM((here, half), bf16),
            pltpu.VMEM((2, here, half), bf16),
            pltpu.VMEM((here, half), bf16),
            pltpu.VMEM((2 * hidden + width, half), f32),
            pltpu.SemaphoreType.DMA((3,)),
            pltpu.SemaphoreType.DMA((transfers,)),
            pltpu.SemaphoreType.DMA((transfers,)),
        ],
        name="middle",
        cost_estimate=pl.CostEstimate(
            flops=12 * here * width * hidden, transcendentals=2 * here * hidden, bytes_accessed=12 << 20
        ),
        compiler_params=pltpu.CompilerParams(
            vmem_limit_bytes=40 << 20, collective_id=1, has_side_effects=True
        ),
    )(mix, rl, atoms, dy, small, bias, out_w, inner_w, outer_w)


class Part:
    def __init__(self, names, order, rows, dtype=bf16):
        self.names, self.order, self.rows, self.dtype = names, order, rows, dtype
        self.steps, left = [], list(names)
        for name in order:
            others = [n for n in left if n != name]
            spots = []
            for q in range(1 << len(others)):
                base = sum(
                    self.stride(n) for i, n in enumerate(others) if (q >> (len(others) - 1 - i)) & 1
                )
                spots.append((base, base + self.stride(name)))
            self.steps.append((name, spots))
            left = others

    def stride(self, name):
        return 1 << (len(self.names) - 1 - self.names.index(name))

    def scratch(self):
        shapes = [pltpu.VMEM((1 << len(self.names), self.rows, 128), f32)]
        for _, spots in self.steps:
            shapes += [pltpu.VMEM((len(spots), self.rows, 128), self.dtype)] * 2
        shapes += [pltpu.VMEM((self.rows, 128), self.dtype)] * 2
        n = len(self.steps) + 1
        return shapes + [pltpu.SemaphoreType.DMA((n,)), pltpu.SemaphoreType.DMA((n,))]

    def bind(self, refs, partner):
        self.state, self.sends, self.recvs = refs[0], refs[1:-2:2], refs[2:-2:2]
        self.send_sem, self.recv_sem, self.partner = refs[-2], refs[-1], partner

    def go(self, n):
        name, spots = self.steps[n]
        for q, (_, far) in enumerate(spots):
            self.sends[n][q] = self.state[far].astype(self.dtype)
        self.copy = remote(
            self.sends[n], self.recvs[n], self.send_sem.at[n], self.recv_sem.at[n], self.partner(name)
        )

    def come(self, n):
        self.copy.wait()
        for q, (near, _) in enumerate(self.steps[n][1]):
            self.state[near] = self.state[near] + self.recvs[n][q].astype(f32)

    def share(self, total, core, y, row):
        n = len(self.steps)
        low = self.state[0].astype(self.dtype)
        self.sends[n][...] = low
        self.copy = remote(
            self.sends[n], self.recvs[n], self.send_sem.at[n], self.recv_sem.at[n], self.partner("y")
        )
        self.put(total, core, y, row, low)

    def shared(self, total, core, y, row):
        self.copy.wait()
        self.put(total, core, 1 - y, row, self.recvs[len(self.steps)][...])

    def put(self, total, core, y, row, value):
        total[core, row : row + self.rows, pl.ds(pl.multiple_of(y * 128, 128), 128)] = value.astype(f32)


def make_parts(parts, width, hidden):
    bits = ["d%d" % b for b in range(parts.bit_length() - 1)]
    high = bits[::-1]
    tall, short = hidden // parts, width // parts
    rest = tall // 4
    without = lambda name: [n for n in high if n != name]
    a = Part(without("d0") + ["y"], ["y", "d1"] + bits[2:], tall - rest)
    b = Part(high, ["d1", "d0"] + bits[2:], hidden // width * short)
    c = Part(without("d1") + ["y"], ["d0", "y"] + bits[2:], rest + short)
    q = Part(high + ["y"], ["d0", "y", "d1"] + bits[2:], short)
    k = Part(high + ["y"], ["y", "d1", "d0"] + bits[2:], short)
    v = Part(high + ["y"], ["d1", "d0", "y"] + bits[2:], short)
    s = Part(high + ["y"], ["d1", "d0", "y"] + bits[2:], 16, f32)
    return a, b, c, q, k, v, s


def tail_kernel(parts, scale, hidden, *refs):
    (
        dkt_in, dvt_in, dq_in, all_in, query_w, key_w, value_w, dmid_in, small_ref, vec_ref,
        a_keep, a_got, b_keep, b_got, c_keep, c_got, out_ref, total,
        dkt, dvt, dq, atoms, qw, kw, vw, dmid, ak, ag, bk, bg, ck, cg,
        dk_in, dv_in, dqh, dqh_in, vec_own, vec_in, standard, normed, partial, beside_send, beside_recv,
        across_send, across_recv, grads, vec_all, load_sem, send_sem, recv_sem,
    ) = refs[:50]
    slots, width, full = dkt.shape
    here = dq.shape[0]
    rows, half = here // slots, width // 2
    bits = parts.bit_length() - 1
    short, tall = width // parts, hidden // parts
    row, dp = lax.axis_index("rows"), lax.axis_index("dp")
    core, y = row % 2, row // 2
    beside, across = (dp, row + 1 - 2 * core), (dp, row + 2 - 4 * y)

    def partner(name):
        if name == "y":
            return across
        b = int(name[1:])
        return (xor(dp, 1 << b, bits), row)

    pieces = make_parts(parts, width, hidden)
    at = 50
    for piece in pieces:
        n = len(piece.scratch())
        piece.bind(refs[at : at + n], partner)
        at += n
    pa, pb, pc, pq, pk, pv, ps = pieces

    pairs = (
        (ak, a_keep), (ag, a_got), (bk, b_keep), (bg, b_got), (ck, c_keep), (cg, c_got), (dq, dq_in),
        (dkt, dkt_in), (dvt, dvt_in), (atoms, all_in), (kw, key_w), (vw, value_w), (qw, query_w), (dmid, dmid_in),
    )
    loads = {}
    for i, (vmem, hbm) in enumerate(pairs):
        loads[id(vmem)] = pltpu.make_async_copy(hbm, vmem, load_sem.at[i])
        loads[id(vmem)].start()
    ready = lambda *which: [loads[id(ref)].wait() for ref in which]
    meet([beside, across] + [partner("d%d" % b) for b in range(bits)])
    other = pl.ds(pl.multiple_of((1 - core) * half, half), half)
    mine = pl.ds(pl.multiple_of(core * half, half), half)
    ready(dkt, dvt, dq)
    to_sibling = [
        remote(dkt.at[:, other, :], dk_in, send_sem.at[0], recv_sem.at[0], beside),
        remote(dvt.at[:, other, :], dv_in, send_sem.at[1], recv_sem.at[1], beside),
    ]
    dq_low = dq[...]
    dqh[0] = dq_low[:, :half]
    dqh[1] = dq_low[:, half:]
    to_sibling.append(remote(dqh.at[1 - core], dqh_in, send_sem.at[2], recv_sem.at[2], beside))
    ready(ak, ag, bk, bg, ck, cg)
    for piece, keep, got in ((pa, ak, ag), (pb, bk, bg), (pc, ck, cg)):
        piece.state[...] = keep[...] + got[...].astype(f32)
        piece.go(0)

    gain, shift = small_ref[0:1, :], small_ref[1:2, :]
    down = lambda value: jnp.sum(value, axis=0, keepdims=True)
    ready(atoms, kw, vw)
    gain_grad = shift_grad = value_bias = 0.0
    send_on = []
    for s in range(slots):
        standard[s] = standardize(atoms[s].astype(f32))[0]
        normed[s] = (standard[s] * gain + shift).astype(bf16)
        dv = dvt[s].T
        grad = times_transposed(dkt[s].T, kw[...]) + times_transposed(dv, vw[...])
        value_bias = value_bias + down(dv.astype(f32))
        gain_grad = gain_grad + down(grad * standard[s])
        shift_grad = shift_grad + down(grad)
        for i in range(full // rows):
            to = xor(row, i, 2)
            partial[to, s] = grad[rows * i : rows * (i + 1)]
        beside_send[s, 0] = partial[1, s].astype(bf16)
        beside_send[s, 1] = partial[3, s].astype(bf16)
        send_on.append(remote(beside_send.at[s], beside_recv.at[s], send_sem.at[3 + s], recv_sem.at[3 + s], beside))
    ready(qw)
    own = pl.ds(pl.multiple_of(row * rows, rows), rows)
    next_to = pl.ds(pl.multiple_of((row + 1 - 2 * core) * rows, rows), rows)
    rows_of = lambda ref, which: jnp.concatenate([ref[s, which, :] for s in range(slots)], axis=0)
    standard_own = rows_of(standard, own)
    query_grad = times_transposed(dq_low, qw[...]) * scale
    vec_own[0:1, :] = gain_grad + down(query_grad * standard_own)
    vec_own[1:2, :] = shift_grad + down(query_grad)
    vec_own[2:3, :] = down(dq_low.astype(f32)) * scale
    vec_own[3:4, :] = value_bias
    vec_own[4:12, :] = vec_ref[...]
    vec_own[12:16, :] = jnp.zeros((4, width), f32)
    n = 3 + slots
    to_sibling.append(remote(vec_own, vec_in, send_sem.at[n], recv_sem.at[n], beside))

    for piece in (pa, pb, pc):
        piece.come(0)
        piece.go(1)

    for copy in to_sibling[:3]:
        copy.wait()
    grads[0] = (
        outer_sum(rows_of(normed, own), dqh[core]) + outer_sum(rows_of(normed, next_to), dqh_in[...])
    ) * scale
    key_total = value_total = 0.0
    add = lambda left, right: (left.astype(f32) + right.astype(f32)).astype(bf16)
    for s in range(slots):
        turned = normed[s].T
        key_total = key_total + times_transposed(turned, add(dkt[s, mine, :], dk_in[s]))
        value_total = value_total + times_transposed(turned, add(dvt[s, mine, :], dv_in[s]))
    grads[1] = key_total
    grads[2] = value_total
    to_sibling[3].wait()
    vec = vec_own[...] + vec_in[...]
    vec_all[...] = jnp.zeros_like(vec_all)
    for j in range(parts):
        vec_all[j, 0:4, :short] = vec[0:4, short * j : short * (j + 1)]
        vec_all[j, 4:8, :short] = vec[8:12, short * j : short * (j + 1)]
        start = tall * j
        vec_all[j, 8:9, :tall] = vec[4 + start // width : 5 + start // width, start % width : start % width + tall]
    for p in range(parts):
        j = xor(dp, p, bits)
        for r in range(2):
            lanes = pl.ds(pl.multiple_of(other_bit(y, 0, r) * 128, 128), 128)
            for i, piece in enumerate((pq, pk, pv)):
                piece.state[2 * p + r] = grads[i, pl.ds(pl.multiple_of(j * short, short), short), lanes]
            ps.state[2 * p + r] = vec_all[j, :, lanes]
    late = (pq, pk, pv, ps)
    for piece in late:
        piece.go(0)

    for s in range(slots):
        send_on[s].wait()
        across_send[s] = (partial[2, s] + beside_recv[s, 1].astype(f32)).astype(bf16)
    n = 4 + slots
    over = remote(across_send, across_recv, send_sem.at[n], recv_sem.at[n], across)

    steps = len(pa.steps)
    for piece in (pa, pb, pc):
        piece.come(1)
        piece.go(2)
    for piece in late:
        piece.come(0)
        piece.go(1)
    over.wait()
    ready(dmid)
    for s in range(slots):
        some = slice(rows * s, rows * (s + 1))
        grad = partial[0, s] + beside_recv[s, 0].astype(f32) + across_recv[s].astype(f32) + query_grad[some]
        stand, inverse = standardize(atoms[s, own, :].astype(f32))
        out_ref[some, :] = (dmid[some, :] + norm_back(grad * gain, stand, inverse)).astype(bf16)
    for n in range(2, steps):
        for piece in (pa, pb, pc):
            piece.come(n)
            if n + 1 < steps:
                piece.go(n + 1)
        for piece in late:
            piece.come(n - 1)
            piece.go(n)
    at = 0
    places = []
    for piece in (pa, pc, pb, pq, pk, pv, ps):
        places.append((piece, at))
        at += piece.rows
    for piece, at in places[:3]:
        piece.share(total, core, y, at)
    for n in range(steps - 1, len(pq.steps)):
        for piece in late:
            piece.come(n)
            if n + 1 < len(pq.steps):
                piece.go(n + 1)
    for piece, at in places[3:]:
        piece.share(total, core, y, at)
    for piece, at in places:
        piece.shared(total, core, y, at)
    n = 5 + slots
    remote(total.at[core], total.at[core], send_sem.at[n], recv_sem.at[n], beside).wait()


def tail(parts, scale, dkt, dvt, dq, all_atoms, query_w, key_w, value_w, dmid, small, vec, pieces):
    slots, width, full = dkt.shape
    here = dq.shape[0]
    hidden = width * 4
    rows, half = here // slots, width // 2
    vm = pl.BlockSpec(memory_space=pltpu.VMEM)
    hbm = pl.BlockSpec(memory_space=pl.ANY)
    kinds = make_parts(parts, width, hidden)
    count = sum(piece.rows for piece in kinds)
    same = lambda array: pltpu.VMEM(array.shape, array.dtype)
    loaded = [dkt, dvt, dq, all_atoms, query_w, key_w, value_w, dmid] + list(pieces)
    transfers = 6 + slots
    scratch = [same(array) for array in loaded] + [
        pltpu.VMEM((slots, half, full), bf16),
        pltpu.VMEM((slots, half, full), bf16),
        pltpu.VMEM((2, here, half), bf16),
        pltpu.VMEM((here, half), bf16),
        pltpu.VMEM((16, width), f32),
        pltpu.VMEM((16, width), f32),
        pltpu.VMEM((slots, full, width), f32),
        pltpu.VMEM((slots, full, width), bf16),
        pltpu.VMEM((4, slots, rows, width), f32),
        pltpu.VMEM((slots, 2, rows, width), bf16),
        pltpu.VMEM((slots, 2, rows, width), bf16),
        pltpu.VMEM((slots, rows, width), bf16),
        pltpu.VMEM((slots, rows, width), bf16),
        pltpu.VMEM((3, width, half), f32),
        pltpu.VMEM((parts, 16, half), f32),
        pltpu.SemaphoreType.DMA((len(loaded),)),
        pltpu.SemaphoreType.DMA((transfers,)),
        pltpu.SemaphoreType.DMA((transfers,)),
    ]
    for piece in kinds:
        scratch += piece.scratch()
    return pl.pallas_call(
        functools.partial(tail_kernel, parts, scale, hidden),
        in_specs=[hbm] * 8 + [vm, vm] + [hbm] * 6,
        out_specs=[vm, vm],
        out_shape=[
            jax.ShapeDtypeStruct((here, width), bf16),
            jax.ShapeDtypeStruct((2, count, half), f32),
        ],
        scratch_shapes=scratch,
        name="tail",
        cost_estimate=pl.CostEstimate(
            flops=10 * slots * full * width * width, transcendentals=0, bytes_accessed=12 << 20
        ),
        compiler_params=pltpu.CompilerParams(vmem_limit_bytes=48 << 20, collective_id=2, has_side_effects=True),
    )(dkt, dvt, dq, all_atoms, query_w, key_w, value_w, dmid, small, vec, *pieces)


def last_kernel(
    total, grad_ref, made_ref, grad_out, made_out, uw, ow, iw, qw, kw, vw, again, ashift, qb, vb, ob, fgain, fshift, ub, ib
):
    half = total.shape[2]
    grad_out[...] = grad_ref[...]
    made_out[...] = made_ref[...]
    short = ow.shape[0]
    at = 0
    for ref in (uw, ow):
        n = ref.shape[0]
        for c in range(2):
            ref[:, half * c : half * (c + 1)] = total[c, at : at + n, :]
        at += n
    blocks = iw.shape[1] // 2 // half
    for k in range(blocks):
        for c in range(2):
            n = c * blocks + k
            iw[:, half * n : half * (n + 1)] = total[c, at : at + short, :]
        at += short
    for ref in (qw, kw, vw):
        for c in range(2):
            ref[:, half * c : half * (c + 1)] = total[c, at : at + short, :]
        at += short
    vec = total[0, at : at + 16, :]
    for i, ref in enumerate((again, ashift, qb, vb, ob, fgain, fshift, ub)):
        ref[...] = vec[i : i + 1, :short]
    ib[...] = vec[8:9, : ib.shape[1]]


def last(parts, total, grad, made, hidden):
    here, width = grad.shape
    short, tall = width // parts, hidden // parts
    vm = pl.BlockSpec(memory_space=pltpu.VMEM)
    like = lambda *shape: jax.ShapeDtypeStruct(shape, f32)
    out_shape = [jax.ShapeDtypeStruct(grad.shape, bf16)] * 2
    out_shape += [like(tall, width), like(short, width), like(short, hidden)] + [like(short, width)] * 3
    out_shape += [like(1, short)] * 8 + [like(1, tall)]
    return pl.pallas_call(
        last_kernel,
        in_specs=[vm] * 3,
        out_specs=[vm] * len(out_shape),
        out_shape=out_shape,
        name="last",
        compiler_params=pltpu.CompilerParams(vmem_limit_bytes=16 << 20),
    )(total, grad, made)


def make_swap(parts, group):
    def swap(array, dp_bit=None, row_bit=None):
        pairs = []
        for d in range(parts):
            for r in range(group):
                e = d if dp_bit is None else d ^ (1 << dp_bit)
                t = r if row_bit is None else r ^ (1 << row_bit)
                pairs.append((d * group + r, e * group + t))
        return lax.ppermute(array, ("dp", "rows"), pairs)

    return swap


def local(
    parts,
    group,
    atoms,
    pair_bias,
    mol_counts,
    attn_gain,
    attn_shift,
    query_weight,
    query_bias,
    key_weight,
    value_weight,
    value_bias,
    out_weight,
    out_bias,
    ffn_gain,
    ffn_shift,
    inner_weight,
    inner_bias,
    outer_weight,
    outer_bias,
    atoms_cotangent,
    pair_cotangent,
):
    slots, part_rows, width = atoms.shape
    heads = pair_bias.shape[1]
    full = pair_bias.shape[3]
    scale = (width // heads) ** (-0.5)
    here = slots * part_rows
    hidden = inner_weight.shape[1]
    swap = make_swap(parts, group)
    flat = lambda array: array.reshape(here, width)
    small = jnp.stack(
        [attn_gain, attn_shift, query_bias, value_bias, out_bias, ffn_gain, ffn_shift, outer_bias]
    ).astype(f32)
    all_atoms, mask, q, qt, k, kt, v, vt = front(
        scale, full, atoms, mol_counts, small, query_weight, key_weight, value_weight
    )
    pair_out, weights, mixed, inverse_sum = attention_forward(q, kt, v, pair_bias, mask)
    atoms_out, a_keep, a_send, b_keep, b_send, c_keep, c_send, scaled, centre, scaled_turned, grad_middle, vec = middle(
        parts,
        flat(mixed),
        flat(inverse_sum),
        flat(atoms),
        flat(atoms_cotangent),
        small,
        inner_bias.astype(f32).reshape(1, hidden),
        out_weight,
        inner_weight,
        outer_weight,
        slots,
    )
    a_got, b_got, c_got = swap(a_send, dp_bit=0), swap(b_send, row_bit=1), swap(c_send, dp_bit=1)
    pair_grad, dq, dkt, dvt = attention_backward(
        qt, scaled.reshape(q.shape), scaled_turned, centre.reshape(q.shape), k, vt, weights, pair_cotangent
    )
    grad, total = tail(
        parts,
        scale,
        dkt,
        dvt,
        flat(dq),
        all_atoms,
        query_weight,
        key_weight,
        value_weight,
        grad_middle,
        small,
        vec,
        (a_keep, a_got, b_keep, b_got, c_keep, c_got),
    )
    grad, made, uw, ow, iw, qw, kw, vw, again, ashift, qb, vb, ob, fgain, fshift, ub, ib = last(
        parts, total, grad, atoms_out, hidden
    )
    line = lambda array: array.reshape(-1)
    return (
        made.reshape(atoms.shape),
        pair_out,
        grad.reshape(atoms.shape),
        pair_grad,
        line(again),
        line(ashift),
        qw,
        line(qb),
        kw,
        vw,
        line(vb),
        ow,
        line(ob),
        line(fgain),
        line(fshift),
        iw,
        line(ib),
        uw,
        line(ub),
    )


def solution(mesh):
    one, two = P("dp"), P("dp", None)
    atoms_spec, pair_spec = P("dp", "rows", None), P("dp", None, "rows", None)
    in_specs = (atoms_spec, pair_spec, two) + (P(),) * 15 + (atoms_spec, pair_spec)
    out_specs = (
        (atoms_spec, pair_spec, atoms_spec, pair_spec, one, one, two, one, two, two, one, two)
        + (one, one, one, two, one, two, one)
    )
    run = functools.partial(local, mesh.shape["dp"], mesh.shape["rows"])
    return jax.shard_map(run, mesh=mesh, in_specs=in_specs, out_specs=out_specs, check_vma=False)
```

```python
import functools

import jax
import jax.numpy as jnp
from jax import lax
from jax.experimental import pallas as pl
from jax.experimental.pallas import tpu as pltpu
from jax.sharding import PartitionSpec as P

f32, bf16 = jnp.float32, jnp.bfloat16
BIG = 1e9
HPL = 16
CHUNK = 8
STEP = 32
VMEM_PAIR = 16 << 20
MESH = pl.DeviceIdType.MESH


def standardize(value):
    centred = value - jnp.mean(value, axis=-1, keepdims=True)
    inverse = lax.rsqrt(jnp.mean(centred * centred, axis=-1, keepdims=True) + 1e-05)
    return (centred * inverse, inverse)


def norm_back(grad_normed, standard, inverse):
    return inverse * (
        grad_normed
        - jnp.mean(grad_normed, axis=-1, keepdims=True)
        - standard * jnp.mean(grad_normed * standard, axis=-1, keepdims=True)
    )


def matmul(left, right):
    return jnp.dot(left, right, preferred_element_type=f32)


def times_transposed(left, right):
    return lax.dot_general(left, right, (((1,), (1,)), ((), ())), preferred_element_type=f32)


def outer_sum(left, right):
    return lax.dot_general(left, right, (((0,), (0,)), ((), ())), preferred_element_type=f32)


def other_bit(index, bit, const):
    own = (index // (1 << bit)) % 2
    return 1 - own if (const >> bit) & 1 else own


def xor(index, const, bits):
    return sum(other_bit(index, b, const) * (1 << b) for b in range(bits))


def remote(source, target, send_sem, recv_sem, device):
    copy = pltpu.make_async_remote_copy(
        src_ref=source, dst_ref=target, send_sem=send_sem, recv_sem=recv_sem, device_id=device, device_id_type=MESH
    )
    copy.start()
    return copy


def meet(devices):
    barrier = pltpu.get_barrier_semaphore()
    for device in devices:
        pl.semaphore_signal(barrier, inc=1, device_id=device, device_id_type=MESH)
    pl.semaphore_wait(barrier, len(devices))


def wide(ref):
    return ref[...].astype(f32).reshape(1, -1)


def front_kernel(
    scale,
    atoms_ref,
    counts_ref,
    gain_ref,
    shift_ref,
    query_b,
    value_b,
    query_w,
    key_w,
    value_w,
    all_ref,
    mask_ref,
    q_ref,
    qt_ref,
    k_ref,
    kt_ref,
    v_ref,
    vt_ref,
    qw,
    kw,
    vw,
    load_sem,
    send_sem,
    recv_sem,
):
    slots, rows, width = atoms_ref.shape
    full = mask_ref.shape[2]
    row, dp = lax.axis_index("rows"), lax.axis_index("dp")
    core, y = row % 2, row // 2
    beside, across = row + 1 - 2 * core, row + 2 - 4 * y
    loads = [
        pltpu.make_async_copy(hbm, vmem, load_sem.at[i])
        for i, (hbm, vmem) in enumerate(((query_w, qw), (key_w, kw), (value_w, vw)))
    ]
    for copy in loads:
        copy.start()
    meet([(dp, beside), (dp, across)])
    at = lambda r: pl.ds(pl.multiple_of(r * rows, rows), rows)
    here = lambda s: all_ref.at[s, at(row), :]
    there = lambda s: all_ref.at[s, at(across), :]
    far = [remote(atoms_ref.at[s], here(s), send_sem.at[s], recv_sem.at[s], (dp, across)) for s in range(slots)]
    near = [
        remote(atoms_ref.at[s], here(s), send_sem.at[slots + s], recv_sem.at[slots + s], (dp, beside))
        for s in range(slots)
    ]
    gain, shift = wide(gain_ref), wide(shift_ref)
    bias = wide(value_b)
    for s in range(slots):
        all_ref[s, at(row), :] = atoms_ref[s]
    own = atoms_ref[...].reshape(slots * rows, width).astype(f32)
    normed = (standardize(own)[0] * gain + shift).astype(bf16)
    loads[0].wait()
    queries = ((matmul(normed, qw[...]) + wide(query_b)) * scale).astype(bf16)
    for s in range(slots):
        part = queries[rows * s : rows * (s + 1)]
        q_ref[s] = part
        qt_ref[s] = part.T
    loads[1].wait()
    loads[2].wait()

    def project(s, chip):
        some = pl.ds(pl.multiple_of(chip * 2 * rows, 2 * rows), 2 * rows)
        normed = (standardize(all_ref[s, some, :].astype(f32))[0] * gain + shift).astype(bf16)
        keys = matmul(normed, kw[...]).astype(bf16)
        k_ref[s, some, :] = keys
        kt_ref[s, :, some] = keys.T
        values = (matmul(normed, vw[...]) + bias).astype(bf16)
        v_ref[s, some, :] = values
        vt_ref[s, :, some] = values.T

    def masks(s):
        ends = [counts_ref[s, 0]]
        for m in range(1, counts_ref.shape[1]):
            ends.append(ends[-1] + counts_ref[s, m])
        keys_at = lax.broadcasted_iota(jnp.int32, (1, full), 1)
        queries_at = lax.broadcasted_iota(jnp.int32, (rows, 1), 0) + row * rows
        count = lambda at: sum((end <= at).astype(jnp.int32) for end in ends)
        mask_ref[s] = jnp.where(count(keys_at) == count(queries_at), 0.0, -BIG)

    forward = []
    for s in range(slots):
        near[s].wait()
        project(s, y)
        far[s].wait()
        n = 2 * slots + s
        forward.append(remote(there(s), there(s), send_sem.at[n], recv_sem.at[n], (dp, beside)))
        masks(s)
        if s:
            forward[s - 1].wait()
            project(s - 1, 1 - y)
    forward[-1].wait()
    project(slots - 1, 1 - y)


def front(scale, full, atoms, counts, vectors, query_w, key_w, value_w):
    slots, rows, width = atoms.shape
    vm = pl.BlockSpec(memory_space=pltpu.VMEM)
    hbm = pl.BlockSpec(memory_space=pltpu.HBM)
    like = lambda *shape: jax.ShapeDtypeStruct(shape, bf16)
    out_shape = [
        like(slots, full, width),
        jax.ShapeDtypeStruct((slots, rows, full), f32),
        like(slots, rows, width),
        like(slots, width, rows),
        like(slots, full, width),
        like(slots, width, full),
        like(slots, full, width),
        like(slots, width, full),
    ]
    return pl.pallas_call(
        functools.partial(front_kernel, scale),
        in_specs=[vm, pl.BlockSpec(memory_space=pltpu.SMEM)] + [vm] * 4 + [hbm] * 3,
        out_specs=[vm] * len(out_shape),
        out_shape=out_shape,
        scratch_shapes=[pltpu.VMEM((width, width), bf16)] * 3
        + [
            pltpu.SemaphoreType.DMA((3,)),
            pltpu.SemaphoreType.DMA((3 * slots,)),
            pltpu.SemaphoreType.DMA((3 * slots,)),
        ],
        name="front",
        cost_estimate=pl.CostEstimate(
            flops=48 * slots * full * width * width, transcendentals=0, bytes_accessed=32 << 20
        ),
        compiler_params=pltpu.CompilerParams(vmem_limit_bytes=18 << 20, collective_id=0, has_side_effects=True),
    )(*(pltpu.with_memory_space_constraint(array, pltpu.HBM) for array in (atoms, counts, *vectors, query_w, key_w, value_w)))


def forward_kernel(q_ref, kt_ref, v_ref, bias_ref, mask_ref, out_ref, e_ref, mix_ref, rl_ref):
    _, heads, rows, full = bias_ref.shape
    lane_head = lax.broadcasted_iota(jnp.int32, (rows, 128), 1) // 8
    mask = mask_ref[0]
    ones = jnp.ones((full, 128), bf16)
    for b in range(heads // HPL):
        cols = slice(128 * b, 128 * b + 128)
        q = q_ref[0, :, cols].astype(f32)
        kt = kt_ref[0, cols, :]
        v = jnp.concatenate([v_ref[0, :, cols], ones], axis=1)
        mixed = jnp.zeros((rows, 128), f32)
        total = jnp.zeros((rows, 128), f32)
        for c in range(HPL // CHUNK):
            own = [lane_head == CHUNK * c + i for i in range(CHUNK)]
            left = jnp.concatenate([jnp.where(o, q, 0.0).astype(bf16) for o in own], axis=0)
            scores = matmul(left, kt).reshape(CHUNK, rows, full)
            hs = slice(HPL * b + CHUNK * c, HPL * b + CHUNK * (c + 1))
            scores = scores + bias_ref[0, hs].astype(f32)
            out_ref[0, hs] = scores.astype(bf16)
            scores = scores + mask[None]
            highest = jnp.max(scores, axis=-1, keepdims=True)
            e = jnp.exp(scores - highest).astype(bf16)
            e_ref[0, hs] = e
            sums = matmul(e.reshape(CHUNK * rows, full), v)
            for i, o in enumerate(own):
                mixed = jnp.where(o, sums[rows * i : rows * (i + 1), :128], mixed)
                total = jnp.where(o, sums[rows * i : rows * (i + 1), 128:], total)
        inverse = 1.0 / total
        mix_ref[0, :, cols] = mixed * inverse
        rl_ref[0, :, cols] = inverse


def attention_forward(q, kt, v, bias, mask):
    slots, heads, rows, full = bias.shape
    step = min(STEP, heads)
    width = step * 8
    natural = lambda n: pl.BlockSpec((1, n, width), lambda s, h: (s, 0, h))
    pair = pl.BlockSpec((1, step, rows, full), lambda s, h: (s, h, 0, 0))
    return pl.pallas_call(
        forward_kernel,
        grid=(slots, heads // step),
        in_specs=[
            natural(rows),
            pl.BlockSpec((1, width, full), lambda s, h: (s, h, 0)),
            natural(full),
            pair,
            pl.BlockSpec((1, rows, full), lambda s, h: (s, 0, 0)),
        ],
        out_specs=[pair, pair, natural(rows), natural(rows)],
        out_shape=[
            jax.ShapeDtypeStruct(bias.shape, bf16),
            jax.ShapeDtypeStruct(bias.shape, bf16),
            jax.ShapeDtypeStruct(q.shape, f32),
            jax.ShapeDtypeStruct(q.shape, f32),
        ],
        name="attention_forward",
        cost_estimate=pl.CostEstimate(
            flops=2 * bias.size * 512, transcendentals=bias.size, bytes_accessed=bias.size * 6
        ),
        compiler_params=pltpu.CompilerParams(vmem_limit_bytes=VMEM_PAIR),
    )(q, kt, v, bias, mask)


def backward_kernel(
    qt_ref, dm_ref, dmt_ref, nm_ref, k_ref, vt_ref, e_ref, cot_ref, pg_ref, dq_ref, dkt_ref, dvt_ref
):
    _, heads, rows, full = cot_ref.shape
    lane_head = lax.broadcasted_iota(jnp.int32, (rows, 128), 1) // 8
    shape = (8 * CHUNK, CHUNK * rows)
    same = lax.broadcasted_iota(jnp.int32, shape, 0) // 8 == lax.broadcasted_iota(jnp.int32, shape, 1) // rows
    ones = jnp.ones((128, full), bf16)
    for b in range(heads // HPL):
        cols = slice(128 * b, 128 * b + 128)
        dm = dm_ref[0, :, cols].astype(f32)
        nm = nm_ref[0, :, cols].astype(f32)
        vt = jnp.concatenate([vt_ref[0, cols, :], ones], axis=0)
        k = k_ref[0, :, cols]
        dq = jnp.zeros((rows, 128), f32)
        for c in range(HPL // CHUNK):
            own = [lane_head == CHUNK * c + i for i in range(CHUNK)]
            left = jnp.concatenate(
                [
                    jnp.concatenate([jnp.where(o, dm, 0.0), jnp.where(o, nm, 0.0)], axis=1).astype(bf16)
                    for o in own
                ],
                axis=0,
            )
            centred = matmul(left, vt).reshape(CHUNK, rows, full)
            hs = slice(HPL * b + CHUNK * c, HPL * b + CHUNK * (c + 1))
            e = e_ref[0, hs]
            grad = (e.astype(f32) * centred + cot_ref[0, hs].astype(f32)).astype(bf16)
            pg_ref[0, hs] = grad
            grad = grad.reshape(CHUNK * rows, full)
            sums = matmul(grad, k)
            for i, o in enumerate(own):
                dq = jnp.where(o, sums[rows * i : rows * (i + 1)], dq)
            rs = slice(hs.start * 8, hs.stop * 8)
            spread = lambda ref: jnp.where(
                same, jnp.concatenate([ref[0, rs, :].astype(f32)] * CHUNK, axis=1), 0.0
            ).astype(bf16)
            dkt_ref[0, rs, :] = matmul(spread(qt_ref), grad).astype(bf16)
            dvt_ref[0, rs, :] = matmul(spread(dmt_ref), e.reshape(CHUNK * rows, full)).astype(bf16)
        dq_ref[0, :, cols] = dq.astype(bf16)


def attention_backward(qt, dm, dmt, nm, k, vt, e, cot):
    slots, heads, rows, full = cot.shape
    step = min(STEP, heads)
    width = step * 8
    natural = lambda n: pl.BlockSpec((1, n, width), lambda s, h: (s, 0, h))
    turned = lambda n: pl.BlockSpec((1, width, n), lambda s, h: (s, h, 0))
    pair = pl.BlockSpec((1, step, rows, full), lambda s, h: (s, h, 0, 0))
    return pl.pallas_call(
        backward_kernel,
        grid=(slots, heads // step),
        in_specs=[
            turned(rows),
            natural(rows),
            turned(rows),
            natural(rows),
            natural(full),
            turned(full),
            pair,
            pair,
        ],
        out_specs=[pair, natural(rows), turned(full), turned(full)],
        out_shape=[
            jax.ShapeDtypeStruct(cot.shape, bf16),
            jax.ShapeDtypeStruct(dm.shape, bf16),
            jax.ShapeDtypeStruct(vt.shape, bf16),
            jax.ShapeDtypeStruct(vt.shape, bf16),
        ],
        name="attention_backward",
        cost_estimate=pl.CostEstimate(
            flops=2 * cot.size * 768, transcendentals=0, bytes_accessed=cot.size * 6
        ),
        compiler_params=pltpu.CompilerParams(vmem_limit_bytes=VMEM_PAIR),
    )(qt, dm, dmt, nm, k, vt, e, cot)


def middle_kernel(
    parts,
    mix_ref,
    rl_ref,
    atoms_ref,
    dy_ref,
    out_b,
    gain_ref,
    shift_ref,
    outer_b,
    bias_ref,
    out_w,
    inner_w,
    outer_w,
    out_ref,
    a_keep,
    a_send,
    b_keep,
    b_send,
    c_keep,
    c_send,
    dm_ref,
    nm_ref,
    dmt_ref,
    dmid_ref,
    vec_ref,
    ow,
    iw,
    uw,
    act,
    dpre,
    dpre_in,
    inner,
    mixed,
    branch,
    branch_in,
    dyh,
    dy_in,
    grads,
    load_sem,
    send_sem,
    recv_sem,
):
    here, width = atoms_ref.shape
    half = width // 2
    blocks = act.shape[1]
    slots, _, rows = dmt_ref.shape
    bits = parts.bit_length() - 1
    row = lax.axis_index("rows")
    dp = lax.axis_index("dp")
    core = row % 2
    y = row // 2
    sibling = (dp, row + 1 - 2 * core)

    loads = [
        pltpu.make_async_copy(hbm, vmem, load_sem.at[i])
        for i, (hbm, vmem) in enumerate(((out_w, ow), (inner_w, iw), (outer_w, uw)))
    ]
    for copy in loads:
        copy.start()
    barrier = pltpu.get_barrier_semaphore()
    pl.semaphore_signal(barrier, inc=1, device_id=sibling, device_id_type=pl.DeviceIdType.MESH)
    pl.semaphore_wait(barrier, 1)
    sent = []

    def send(source, target):
        n = len(sent)
        copy = pltpu.make_async_remote_copy(
            src_ref=source,
            dst_ref=target,
            send_sem=send_sem.at[n],
            recv_sem=recv_sem.at[n],
            device_id=sibling,
            device_id_type=pl.DeviceIdType.MESH,
        )
        copy.start()
        sent.append(copy)

    dy = dy_ref[...]
    dyh[0] = dy[:, :half]
    dyh[1] = dy[:, half:]
    send(dyh.at[1 - core], dy_in)
    mix = mix_ref[...]
    mixed[0] = mix.astype(bf16)
    send(mixed.at[0], mixed.at[1])
    loads[0].wait()
    middle = atoms_ref[...].astype(f32) + matmul(mixed[0], ow[...]) + wide(out_b)
    standard, inverse = standardize(middle)
    gain = wide(gain_ref)
    inner[0] = (standard * gain + wide(shift_ref)).astype(bf16)
    send(inner.at[0], inner.at[1])
    loads[1].wait()
    loads[2].wait()
    result = middle + wide(outer_b)
    bias = wide(bias_ref)
    grad_inner = jnp.zeros((here, width), f32)
    for b in range(blocks):
        cols = slice(width * b, width * (b + 1))
        pre = matmul(inner[0], iw[:, cols]) + bias[:, cols]
        cdf = 0.5 + 0.5 * lax.erf(pre * (0.5**0.5))
        low = (pre * cdf).astype(bf16)
        act[0, b] = low
        send(act.at[0, b], act.at[1, b])
        slope = cdf + pre * (jnp.exp(-0.5 * pre * pre) * 0.3989422804014327)
        grad = (times_transposed(dy, uw[cols, :]) * slope).astype(bf16)
        dpre[b] = grad
        result = result + matmul(low, uw[cols, :])
        grad_inner = grad_inner + times_transposed(grad, iw[:, cols])
        vec_ref[b : b + 1, :] = jnp.sum(grad.astype(f32), axis=0, keepdims=True)
    for i in range(blocks // 2):
        send(dpre.at[(blocks // 2) * (1 - core) + i], dpre_in.at[i])
    out_ref[...] = result.astype(bf16)
    dy_wide = dy.astype(f32)
    grad_middle = dy_wide + norm_back(grad_inner * gain, standard, inverse)
    dmid_ref[...] = grad_middle
    low = grad_middle.astype(bf16)
    branch[0] = low[:, :half]
    branch[1] = low[:, half:]
    send(branch.at[1 - core], branch_in)
    down = lambda value: jnp.sum(value, axis=0, keepdims=True)
    vec_ref[blocks : blocks + 1, :] = down(low.astype(f32))
    vec_ref[blocks + 1 : blocks + 2, :] = down(grad_inner * standard)
    vec_ref[blocks + 2 : blocks + 3, :] = down(grad_inner)
    vec_ref[blocks + 3 : blocks + 4, :] = down(dy_wide)
    scaled = times_transposed(low, ow[...]).astype(bf16).astype(f32) * rl_ref[...]
    nm_ref[...] = (-scaled * mix).astype(bf16)
    scaled = scaled.astype(bf16)
    dm_ref[...] = scaled
    for s in range(slots):
        dmt_ref[s] = scaled[rows * s : rows * (s + 1)].astype(f32).T.astype(bf16)

    for copy in sent:
        copy.wait()
    tall, short = blocks * width // parts, width // parts
    dy_own = dyh[core]
    for b in range(blocks):
        grads[width * b : width * (b + 1), :] = outer_sum(act[0, b], dy_own) + outer_sum(act[1, b], dy_in[...])
    base = blocks * width
    for i in range(blocks // 2):
        grad = outer_sum(inner[0], dpre[(blocks // 2) * core + i]) + outer_sum(inner[1], dpre_in[i])
        for k in range(2):
            grads[base + width * (2 * i + k) : base + width * (2 * i + k + 1), :] = grad[:, half * k : half * (k + 1)]
    last = base + width * blocks
    grads[last:, :] = outer_sum(mixed[0], branch[core]) + outer_sum(mixed[1], branch_in[...])

    def at(start, n, h):
        return grads[pl.ds(pl.multiple_of(start, 8), n), pl.ds(pl.multiple_of(h * 128, 128), 128)]

    rest = tall // 4
    long = tall - rest
    for p in range(parts):
        j = xor(dp, p, bits)
        for r in range(2):
            h = other_bit(y, 0, r)
            ref = a_send if p & 1 else a_keep
            ref[2 * (p >> 1) + r] = at(j * tall, long, h).astype(ref.dtype)
            ref = b_send if r else b_keep
            for k in range(blocks):
                ref[p, short * k : short * (k + 1)] = at(base + width * k + short * j, short, h).astype(ref.dtype)
            ref = c_send if p & 2 else c_keep
            q = 2 * ((p >> 2) * 2 + (p & 1)) + r
            ref[q, :rest] = at(j * tall + long, rest, h).astype(ref.dtype)
            ref[q, rest:] = at(last + short * j, short, h).astype(ref.dtype)


def middle(parts, mix, rl, atoms, dy, vectors, out_w, inner_w, outer_w, slots):
    here, width = atoms.shape
    hidden = inner_w.shape[1]
    blocks, half, rows = hidden // width, width // 2, here // slots
    tall, short = hidden // parts, width // parts
    rest = tall // 4
    long = tall - rest
    assert hidden == 4 * width
    vm = pl.BlockSpec(memory_space=pltpu.VMEM)
    hbm = pl.BlockSpec(memory_space=pltpu.HBM)
    like = jax.ShapeDtypeStruct
    out_shape = [
        like((here, width), bf16),
        like((parts, long, 128), f32),
        like((parts, long, 128), bf16),
        like((parts, blocks * short, 128), f32),
        like((parts, blocks * short, 128), bf16),
        like((parts, rest + short, 128), f32),
        like((parts, rest + short, 128), bf16),
        like((here, width), bf16),
        like((here, width), bf16),
        like((slots, width, rows), bf16),
        like((here, width), f32),
        like((blocks + 4, width), f32),
    ]
    transfers = 3 + blocks + blocks // 2 + 1
    return pl.pallas_call(
        functools.partial(middle_kernel, parts),
        in_specs=[vm] * 9 + [hbm] * 3,
        out_specs=[vm] * len(out_shape),
        out_shape=out_shape,
        scratch_shapes=[
            pltpu.VMEM((width, width), bf16),
            pltpu.VMEM((width, hidden), bf16),
            pltpu.VMEM((hidden, width), bf16),
            pltpu.VMEM((2, blocks, here, width), bf16),
            pltpu.VMEM((blocks, here, width), bf16),
            pltpu.VMEM((blocks // 2, here, width), bf16),
            pltpu.VMEM((2, here, width), bf16),
            pltpu.VMEM((2, here, width), bf16),
            pltpu.VMEM((2, here, half), bf16),
            pltpu.VMEM((here, half), bf16),
            pltpu.VMEM((2, here, half), bf16),
            pltpu.VMEM((here, half), bf16),
            pltpu.VMEM((2 * hidden + width, half), f32),
            pltpu.SemaphoreType.DMA((3,)),
            pltpu.SemaphoreType.DMA((transfers,)),
            pltpu.SemaphoreType.DMA((transfers,)),
        ],
        name="middle",
        cost_estimate=pl.CostEstimate(
            flops=12 * here * width * hidden, transcendentals=2 * here * hidden, bytes_accessed=12 << 20
        ),
        compiler_params=pltpu.CompilerParams(
            vmem_limit_bytes=20 << 20, collective_id=1, has_side_effects=True
        ),
    )(mix, rl, atoms, dy, *vectors, out_w, inner_w, outer_w)


class Part:
    def __init__(self, names, order, rows, dtype=bf16):
        self.names, self.order, self.rows, self.dtype = names, order, rows, dtype
        self.steps, left = [], list(names)
        for name in order:
            others = [n for n in left if n != name]
            spots = []
            for q in range(1 << len(others)):
                base = sum(
                    self.stride(n) for i, n in enumerate(others) if (q >> (len(others) - 1 - i)) & 1
                )
                spots.append((base, base + self.stride(name)))
            self.steps.append((name, spots))
            left = others

    def stride(self, name):
        return 1 << (len(self.names) - 1 - self.names.index(name))

    def scratch(self):
        shapes = [pltpu.VMEM((1 << len(self.names), self.rows, 128), f32)]
        for _, spots in self.steps:
            shapes += [pltpu.VMEM((len(spots), self.rows, 128), self.dtype)] * 2
        shapes += [pltpu.VMEM((self.rows, 128), self.dtype)] * 2
        n = len(self.steps) + 1
        return shapes + [pltpu.SemaphoreType.DMA((n,)), pltpu.SemaphoreType.DMA((n,))]

    def bind(self, refs, partner):
        self.state, self.sends, self.recvs = refs[0], refs[1:-2:2], refs[2:-2:2]
        self.send_sem, self.recv_sem, self.partner = refs[-2], refs[-1], partner

    def go(self, n):
        name, spots = self.steps[n]
        for q, (_, far) in enumerate(spots):
            self.sends[n][q] = self.state[far].astype(self.dtype)
        self.copy = remote(
            self.sends[n], self.recvs[n], self.send_sem.at[n], self.recv_sem.at[n], self.partner(name)
        )

    def come(self, n):
        self.copy.wait()
        for q, (near, _) in enumerate(self.steps[n][1]):
            self.state[near] = self.state[near] + self.recvs[n][q].astype(f32)

    def share(self, total, core, y, row):
        n = len(self.steps)
        low = self.state[0].astype(self.dtype)
        self.sends[n][...] = low
        self.copy = remote(
            self.sends[n], self.recvs[n], self.send_sem.at[n], self.recv_sem.at[n], self.partner("y")
        )
        self.put(total, core, y, row, low)

    def shared(self, total, core, y, row):
        self.copy.wait()
        self.put(total, core, 1 - y, row, self.recvs[len(self.steps)][...])

    def put(self, total, core, y, row, value):
        total[core, row : row + self.rows, pl.ds(pl.multiple_of(y * 128, 128), 128)] = value.astype(f32)


def make_parts(parts, width, hidden):
    bits = ["d%d" % b for b in range(parts.bit_length() - 1)]
    high = bits[::-1]
    tall, short = hidden // parts, width // parts
    rest = tall // 4
    without = lambda name: [n for n in high if n != name]
    a = Part(without("d0") + ["y"], ["y", "d1"] + bits[2:], tall - rest)
    b = Part(high, ["d1", "d0"] + bits[2:], hidden // width * short)
    c = Part(without("d1") + ["y"], ["d0", "y"] + bits[2:], rest + short)
    q = Part(high + ["y"], ["d0", "y", "d1"] + bits[2:], short)
    k = Part(high + ["y"], ["y", "d1", "d0"] + bits[2:], short)
    v = Part(high + ["y"], ["d1", "d0", "y"] + bits[2:], short)
    s = Part(high + ["y"], ["d1", "d0", "y"] + bits[2:], 16, f32)
    return a, b, c, q, k, v, s


def tail_kernel(parts, scale, hidden, *refs):
    (
        dkt_in, dvt_in, dq_in, all_in, query_w, key_w, value_w, dmid_in, gain_ref, shift_ref, vec_ref,
        a_keep, a_got, b_keep, b_got, c_keep, c_got, out_ref, total,
        dkt, dvt, dq, atoms, qw, kw, vw, dmid, ak, ag, bk, bg, ck, cg,
        dk_in, dv_in, dqh, dqh_in, vec_own, vec_in, standard, normed, partial, beside_send, beside_recv,
        across_send, across_recv, grads, vec_all, load_sem, send_sem, recv_sem,
    ) = refs[:51]
    slots, width, full = dkt.shape
    here = dq.shape[0]
    rows, half = here // slots, width // 2
    bits = parts.bit_length() - 1
    short, tall = width // parts, hidden // parts
    row, dp = lax.axis_index("rows"), lax.axis_index("dp")
    core, y = row % 2, row // 2
    beside, across = (dp, row + 1 - 2 * core), (dp, row + 2 - 4 * y)

    def partner(name):
        if name == "y":
            return across
        b = int(name[1:])
        return (xor(dp, 1 << b, bits), row)

    pieces = make_parts(parts, width, hidden)
    at = 51
    for piece in pieces:
        n = len(piece.scratch())
        piece.bind(refs[at : at + n], partner)
        at += n
    pa, pb, pc, pq, pk, pv, ps = pieces

    pairs = (
        (ak, a_keep), (ag, a_got), (bk, b_keep), (bg, b_got), (ck, c_keep), (cg, c_got), (dq, dq_in),
        (dkt, dkt_in), (dvt, dvt_in), (atoms, all_in), (kw, key_w), (vw, value_w), (qw, query_w), (dmid, dmid_in),
    )
    loads = {}
    for i, (vmem, hbm) in enumerate(pairs):
        loads[id(vmem)] = pltpu.make_async_copy(hbm, vmem, load_sem.at[i])
        loads[id(vmem)].start()
    ready = lambda *which: [loads[id(ref)].wait() for ref in which]
    meet([beside, across] + [partner("d%d" % b) for b in range(bits)])
    other = pl.ds(pl.multiple_of((1 - core) * half, half), half)
    mine = pl.ds(pl.multiple_of(core * half, half), half)
    ready(dkt, dvt, dq)
    to_sibling = [
        remote(dkt.at[:, other, :], dk_in, send_sem.at[0], recv_sem.at[0], beside),
        remote(dvt.at[:, other, :], dv_in, send_sem.at[1], recv_sem.at[1], beside),
    ]
    dq_low = dq[...]
    dqh[0] = dq_low[:, :half]
    dqh[1] = dq_low[:, half:]
    to_sibling.append(remote(dqh.at[1 - core], dqh_in, send_sem.at[2], recv_sem.at[2], beside))
    ready(ak, ag, bk, bg, ck, cg)
    for piece, keep, got in ((pa, ak, ag), (pb, bk, bg), (pc, ck, cg)):
        piece.state[...] = keep[...] + got[...].astype(f32)
        piece.go(0)

    gain, shift = wide(gain_ref), wide(shift_ref)
    down = lambda value: jnp.sum(value, axis=0, keepdims=True)
    ready(atoms, kw, vw)
    gain_grad = shift_grad = value_bias = 0.0
    send_on = []
    for s in range(slots):
        standard[s] = standardize(atoms[s].astype(f32))[0]
        normed[s] = (standard[s] * gain + shift).astype(bf16)
        dv = dvt[s].T
        grad = times_transposed(dkt[s].T, kw[...]) + times_transposed(dv, vw[...])
        value_bias = value_bias + down(dv.astype(f32))
        gain_grad = gain_grad + down(grad * standard[s])
        shift_grad = shift_grad + down(grad)
        for i in range(full // rows):
            to = xor(row, i, 2)
            partial[to, s] = grad[rows * i : rows * (i + 1)]
        beside_send[s, 0] = partial[1, s].astype(bf16)
        beside_send[s, 1] = partial[3, s].astype(bf16)
        send_on.append(remote(beside_send.at[s], beside_recv.at[s], send_sem.at[3 + s], recv_sem.at[3 + s], beside))
    ready(qw)
    own = pl.ds(pl.multiple_of(row * rows, rows), rows)
    next_to = pl.ds(pl.multiple_of((row + 1 - 2 * core) * rows, rows), rows)
    rows_of = lambda ref, which: jnp.concatenate([ref[s, which, :] for s in range(slots)], axis=0)
    standard_own = rows_of(standard, own)
    query_grad = times_transposed(dq_low, qw[...]) * scale
    vec_own[0:1, :] = gain_grad + down(query_grad * standard_own)
    vec_own[1:2, :] = shift_grad + down(query_grad)
    vec_own[2:3, :] = down(dq_low.astype(f32)) * scale
    vec_own[3:4, :] = value_bias
    vec_own[4:12, :] = vec_ref[...]
    vec_own[12:16, :] = jnp.zeros((4, width), f32)
    n = 3 + slots
    to_sibling.append(remote(vec_own, vec_in, send_sem.at[n], recv_sem.at[n], beside))

    for piece in (pa, pb, pc):
        piece.come(0)
        piece.go(1)

    for copy in to_sibling[:3]:
        copy.wait()
    grads[0] = (
        outer_sum(rows_of(normed, own), dqh[core]) + outer_sum(rows_of(normed, next_to), dqh_in[...])
    ) * scale
    key_total = value_total = 0.0
    add = lambda left, right: (left.astype(f32) + right.astype(f32)).astype(bf16)
    for s in range(slots):
        turned = normed[s].T
        key_total = key_total + times_transposed(turned, add(dkt[s, mine, :], dk_in[s]))
        value_total = value_total + times_transposed(turned, add(dvt[s, mine, :], dv_in[s]))
    grads[1] = key_total
    grads[2] = value_total
    to_sibling[3].wait()
    vec = vec_own[...] + vec_in[...]
    vec_all[...] = jnp.zeros_like(vec_all)
    for j in range(parts):
        vec_all[j, 0:4, :short] = vec[0:4, short * j : short * (j + 1)]
        vec_all[j, 4:8, :short] = vec[8:12, short * j : short * (j + 1)]
        start = tall * j
        vec_all[j, 8:9, :tall] = vec[4 + start // width : 5 + start // width, start % width : start % width + tall]
    for p in range(parts):
        j = xor(dp, p, bits)
        for r in range(2):
            lanes = pl.ds(pl.multiple_of(other_bit(y, 0, r) * 128, 128), 128)
            for i, piece in enumerate((pq, pk, pv)):
                piece.state[2 * p + r] = grads[i, pl.ds(pl.multiple_of(j * short, short), short), lanes]
            ps.state[2 * p + r] = vec_all[j, :, lanes]
    late = (pq, pk, pv, ps)
    for piece in late:
        piece.go(0)

    for s in range(slots):
        send_on[s].wait()
        across_send[s] = (partial[2, s] + beside_recv[s, 1].astype(f32)).astype(bf16)
    n = 4 + slots
    over = remote(across_send, across_recv, send_sem.at[n], recv_sem.at[n], across)

    steps = len(pa.steps)
    for piece in (pa, pb, pc):
        piece.come(1)
        piece.go(2)
    for piece in late:
        piece.come(0)
        piece.go(1)
    over.wait()
    ready(dmid)
    for s in range(slots):
        some = slice(rows * s, rows * (s + 1))
        grad = partial[0, s] + beside_recv[s, 0].astype(f32) + across_recv[s].astype(f32) + query_grad[some]
        stand, inverse = standardize(atoms[s, own, :].astype(f32))
        out_ref[some, :] = (dmid[some, :] + norm_back(grad * gain, stand, inverse)).astype(bf16)
    for n in range(2, steps):
        for piece in (pa, pb, pc):
            piece.come(n)
            if n + 1 < steps:
                piece.go(n + 1)
        for piece in late:
            piece.come(n - 1)
            piece.go(n)
    at = 0
    places = []
    for piece in (pa, pc, pb, pq, pk, pv, ps):
        places.append((piece, at))
        at += piece.rows
    for piece, at in places[:3]:
        piece.share(total, core, y, at)
    for n in range(steps - 1, len(pq.steps)):
        for piece in late:
            piece.come(n)
            if n + 1 < len(pq.steps):
                piece.go(n + 1)
    for piece, at in places[3:]:
        piece.share(total, core, y, at)
    for piece, at in places:
        piece.shared(total, core, y, at)
    n = 5 + slots
    remote(total.at[core], total.at[core], send_sem.at[n], recv_sem.at[n], beside).wait()


def tail(parts, scale, dkt, dvt, dq, all_atoms, query_w, key_w, value_w, dmid, vectors, vec, pieces):
    slots, width, full = dkt.shape
    here = dq.shape[0]
    hidden = width * 4
    rows, half = here // slots, width // 2
    vm = pl.BlockSpec(memory_space=pltpu.VMEM)
    hbm = pl.BlockSpec(memory_space=pl.ANY)
    far = pl.BlockSpec(memory_space=pltpu.HBM)
    kinds = make_parts(parts, width, hidden)
    count = sum(piece.rows for piece in kinds)
    same = lambda array: pltpu.VMEM(array.shape, array.dtype)
    loaded = [dkt, dvt, dq, all_atoms, query_w, key_w, value_w, dmid] + list(pieces)
    transfers = 6 + slots
    scratch = [same(array) for array in loaded] + [
        pltpu.VMEM((slots, half, full), bf16),
        pltpu.VMEM((slots, half, full), bf16),
        pltpu.VMEM((2, here, half), bf16),
        pltpu.VMEM((here, half), bf16),
        pltpu.VMEM((16, width), f32),
        pltpu.VMEM((16, width), f32),
        pltpu.VMEM((slots, full, width), f32),
        pltpu.VMEM((slots, full, width), bf16),
        pltpu.VMEM((4, slots, rows, width), f32),
        pltpu.VMEM((slots, 2, rows, width), bf16),
        pltpu.VMEM((slots, 2, rows, width), bf16),
        pltpu.VMEM((slots, rows, width), bf16),
        pltpu.VMEM((slots, rows, width), bf16),
        pltpu.VMEM((3, width, half), f32),
        pltpu.VMEM((parts, 16, half), f32),
        pltpu.SemaphoreType.DMA((len(loaded),)),
        pltpu.SemaphoreType.DMA((transfers,)),
        pltpu.SemaphoreType.DMA((transfers,)),
    ]
    for piece in kinds:
        scratch += piece.scratch()
    return pl.pallas_call(
        functools.partial(tail_kernel, parts, scale, hidden),
        in_specs=[hbm] * 4 + [far] * 3 + [hbm] + [vm] * 3 + [hbm] * 6,
        out_specs=[vm, vm],
        out_shape=[
            jax.ShapeDtypeStruct((here, width), bf16),
            jax.ShapeDtypeStruct((2, count, half), f32),
        ],
        scratch_shapes=scratch,
        name="tail",
        cost_estimate=pl.CostEstimate(
            flops=10 * slots * full * width * width, transcendentals=0, bytes_accessed=12 << 20
        ),
        compiler_params=pltpu.CompilerParams(vmem_limit_bytes=26 << 20, collective_id=2, has_side_effects=True),
    )(dkt, dvt, dq, all_atoms, query_w, key_w, value_w, dmid, *vectors, vec, *pieces)


def last_kernel(
    total, grad_ref, made_ref, grad_out, made_out, uw, ow, iw, qw, kw, vw, again, ashift, qb, vb, ob, fgain, fshift, ub, ib
):
    half = total.shape[2]
    grad_out[...] = grad_ref[...]
    made_out[...] = made_ref[...]
    short = ow.shape[0]
    at = 0
    for ref in (uw, ow):
        n = ref.shape[0]
        for c in range(2):
            ref[:, half * c : half * (c + 1)] = total[c, at : at + n, :]
        at += n
    blocks = iw.shape[1] // 2 // half
    for k in range(blocks):
        for c in range(2):
            n = c * blocks + k
            iw[:, half * n : half * (n + 1)] = total[c, at : at + short, :]
        at += short
    for ref in (qw, kw, vw):
        for c in range(2):
            ref[:, half * c : half * (c + 1)] = total[c, at : at + short, :]
        at += short
    vec = total[0, at : at + 16, :]
    for i, ref in enumerate((again, ashift, qb, vb, ob, fgain, fshift, ub)):
        ref[...] = vec[i : i + 1, :short]
    ib[...] = vec[8:9, : ib.shape[1]]


def last(parts, total, grad, made, hidden):
    here, width = grad.shape
    short, tall = width // parts, hidden // parts
    vm = pl.BlockSpec(memory_space=pltpu.VMEM)
    like = lambda *shape: jax.ShapeDtypeStruct(shape, f32)
    out_shape = [jax.ShapeDtypeStruct(grad.shape, bf16)] * 2
    out_shape += [like(tall, width), like(short, width), like(short, hidden)] + [like(short, width)] * 3
    out_shape += [like(1, short)] * 8 + [like(1, tall)]
    return pl.pallas_call(
        last_kernel,
        in_specs=[vm] * 3,
        out_specs=[vm] * len(out_shape),
        out_shape=out_shape,
        name="last",
        compiler_params=pltpu.CompilerParams(vmem_limit_bytes=16 << 20),
    )(total, grad, made)


def make_swap(parts, group):
    def swap(array, dp_bit=None, row_bit=None):
        pairs = []
        for d in range(parts):
            for r in range(group):
                e = d if dp_bit is None else d ^ (1 << dp_bit)
                t = r if row_bit is None else r ^ (1 << row_bit)
                pairs.append((d * group + r, e * group + t))
        return lax.ppermute(array, ("dp", "rows"), pairs)

    return swap


def local(
    parts,
    group,
    atoms,
    pair_bias,
    mol_counts,
    attn_gain,
    attn_shift,
    query_weight,
    query_bias,
    key_weight,
    value_weight,
    value_bias,
    out_weight,
    out_bias,
    ffn_gain,
    ffn_shift,
    inner_weight,
    inner_bias,
    outer_weight,
    outer_bias,
    atoms_cotangent,
    pair_cotangent,
):
    slots, part_rows, width = atoms.shape
    heads = pair_bias.shape[1]
    full = pair_bias.shape[3]
    scale = (width // heads) ** (-0.5)
    here = slots * part_rows
    hidden = inner_weight.shape[1]
    swap = make_swap(parts, group)
    flat = lambda array: array.reshape(here, width)
    all_atoms, mask, q, qt, k, kt, v, vt = front(
        scale, full, atoms, mol_counts, (attn_gain, attn_shift, query_bias, value_bias), query_weight, key_weight, value_weight
    )
    pair_out, weights, mixed, inverse_sum = attention_forward(q, kt, v, pair_bias, mask)
    atoms_out, a_keep, a_send, b_keep, b_send, c_keep, c_send, scaled, centre, scaled_turned, grad_middle, vec = middle(
        parts,
        flat(mixed),
        flat(inverse_sum),
        flat(atoms),
        flat(atoms_cotangent),
        (out_bias, ffn_gain, ffn_shift, outer_bias, inner_bias),
        out_weight,
        inner_weight,
        outer_weight,
        slots,
    )
    a_got, b_got, c_got = swap(a_send, dp_bit=0), swap(b_send, row_bit=1), swap(c_send, dp_bit=1)
    pair_grad, dq, dkt, dvt = attention_backward(
        qt, scaled.reshape(q.shape), scaled_turned, centre.reshape(q.shape), k, vt, weights, pair_cotangent
    )
    grad, total = tail(
        parts,
        scale,
        dkt,
        dvt,
        flat(dq),
        all_atoms,
        query_weight,
        key_weight,
        value_weight,
        grad_middle,
        (attn_gain, attn_shift),
        vec,
        (a_keep, a_got, b_keep, b_got, c_keep, c_got),
    )
    grad, made, uw, ow, iw, qw, kw, vw, again, ashift, qb, vb, ob, fgain, fshift, ub, ib = last(
        parts, total, grad, atoms_out, hidden
    )
    line = lambda array: array.reshape(-1)
    return (
        made.reshape(atoms.shape),
        pair_out,
        grad.reshape(atoms.shape),
        pair_grad,
        line(again),
        line(ashift),
        qw,
        line(qb),
        kw,
        vw,
        line(vb),
        ow,
        line(ob),
        line(fgain),
        line(fshift),
        iw,
        line(ib),
        uw,
        line(ub),
    )


def solution(mesh):
    one, two = P("dp"), P("dp", None)
    atoms_spec, pair_spec = P("dp", "rows", None), P("dp", None, "rows", None)
    in_specs = (atoms_spec, pair_spec, two) + (P(),) * 15 + (atoms_spec, pair_spec)
    out_specs = (
        (atoms_spec, pair_spec, atoms_spec, pair_spec, one, one, two, one, two, two, one, two)
        + (one, one, one, two, one, two, one)
    )
    run = functools.partial(local, mesh.shape["dp"], mesh.shape["rows"])
    return jax.shard_map(run, mesh=mesh, in_specs=in_specs, out_specs=out_specs, check_vma=False)
```

```python
import functools

import jax
import jax.numpy as jnp
from jax import lax
from jax.experimental import pallas as pl
from jax.experimental.pallas import tpu as pltpu
from jax.sharding import PartitionSpec as P

f32, bf16 = jnp.float32, jnp.bfloat16
BIG = 1e9
HPL = 16
CHUNK = 8
STEP = 32
VMEM_PAIR = 16 << 20
VMEM_BACK = 26 << 20
MESH = pl.DeviceIdType.MESH
PIECES = (
    ("d0", (("outer", 0), ("outer", 1))),
    ("y", (("outer", 2),)),
    ("d1", (("outer", 3),)),
    ("d0", (("inner", 0),)),
    ("y", (("inner", 1), ("inner", 2))),
    ("d1", (("inner", 3), ("out", 0))),
)


def standardize(value):
    centred = value - jnp.mean(value, axis=-1, keepdims=True)
    inverse = lax.rsqrt(jnp.mean(centred * centred, axis=-1, keepdims=True) + 1e-05)
    return (centred * inverse, inverse)


def norm_back(grad_normed, standard, inverse):
    return inverse * (
        grad_normed
        - jnp.mean(grad_normed, axis=-1, keepdims=True)
        - standard * jnp.mean(grad_normed * standard, axis=-1, keepdims=True)
    )


def matmul(left, right):
    return jnp.dot(left, right, preferred_element_type=f32)


def times_transposed(left, right):
    return lax.dot_general(left, right, (((1,), (1,)), ((), ())), preferred_element_type=f32)


def outer_sum(left, right):
    return lax.dot_general(left, right, (((0,), (0,)), ((), ())), preferred_element_type=f32)


def other_bit(index, bit, const):
    own = (index // (1 << bit)) % 2
    return 1 - own if (const >> bit) & 1 else own


def xor(index, const, bits):
    return sum(other_bit(index, b, const) * (1 << b) for b in range(bits))


def remote(source, target, send_sem, recv_sem, device):
    copy = pltpu.make_async_remote_copy(
        src_ref=source, dst_ref=target, send_sem=send_sem, recv_sem=recv_sem, device_id=device, device_id_type=MESH
    )
    copy.start()
    return copy


def meet(devices):
    barrier = pltpu.get_barrier_semaphore()
    for device in devices:
        pl.semaphore_signal(barrier, inc=1, device_id=device, device_id_type=MESH)
    pl.semaphore_wait(barrier, len(devices))


def wide(ref):
    return ref[...].astype(f32).reshape(1, -1)


def front_kernel(
    scale,
    atoms_ref,
    counts_ref,
    gain_ref,
    shift_ref,
    query_b,
    value_b,
    query_w,
    key_w,
    value_w,
    all_ref,
    mask_ref,
    q_ref,
    qt_ref,
    k_ref,
    kt_ref,
    v_ref,
    vt_ref,
    qw,
    kw,
    vw,
    load_sem,
    send_sem,
    recv_sem,
):
    slots, rows, width = atoms_ref.shape
    full = mask_ref.shape[2]
    row, dp = lax.axis_index("rows"), lax.axis_index("dp")
    core, y = row % 2, row // 2
    beside, across = row + 1 - 2 * core, row + 2 - 4 * y
    loads = [
        pltpu.make_async_copy(hbm, vmem, load_sem.at[i])
        for i, (hbm, vmem) in enumerate(((query_w, qw), (key_w, kw), (value_w, vw)))
    ]
    for copy in loads:
        copy.start()
    meet([(dp, beside), (dp, across)])
    at = lambda r: pl.ds(pl.multiple_of(r * rows, rows), rows)
    here = lambda s: all_ref.at[s, at(row), :]
    there = lambda s: all_ref.at[s, at(across), :]
    far = [remote(atoms_ref.at[s], here(s), send_sem.at[s], recv_sem.at[s], (dp, across)) for s in range(slots)]
    near = [
        remote(atoms_ref.at[s], here(s), send_sem.at[slots + s], recv_sem.at[slots + s], (dp, beside))
        for s in range(slots)
    ]
    gain, shift = wide(gain_ref), wide(shift_ref)
    bias = wide(value_b)
    for s in range(slots):
        all_ref[s, at(row), :] = atoms_ref[s]
    own = atoms_ref[...].reshape(slots * rows, width).astype(f32)
    normed = (standardize(own)[0] * gain + shift).astype(bf16)
    loads[0].wait()
    queries = ((matmul(normed, qw[...]) + wide(query_b)) * scale).astype(bf16)
    for s in range(slots):
        part = queries[rows * s : rows * (s + 1)]
        q_ref[s] = part
        qt_ref[s] = part.T
    loads[1].wait()
    loads[2].wait()

    def project(s, chip):
        some = pl.ds(pl.multiple_of(chip * 2 * rows, 2 * rows), 2 * rows)
        normed = (standardize(all_ref[s, some, :].astype(f32))[0] * gain + shift).astype(bf16)
        keys = matmul(normed, kw[...]).astype(bf16)
        k_ref[s, some, :] = keys
        kt_ref[s, :, some] = keys.T
        values = (matmul(normed, vw[...]) + bias).astype(bf16)
        v_ref[s, some, :] = values
        vt_ref[s, :, some] = values.T

    def masks(s):
        ends = [counts_ref[s, 0]]
        for m in range(1, counts_ref.shape[1]):
            ends.append(ends[-1] + counts_ref[s, m])
        keys_at = lax.broadcasted_iota(jnp.int32, (1, full), 1)
        queries_at = lax.broadcasted_iota(jnp.int32, (rows, 1), 0) + row * rows
        count = lambda at: sum((end <= at).astype(jnp.int32) for end in ends)
        mask_ref[s] = jnp.where(count(keys_at) == count(queries_at), 0.0, -BIG)

    forward = []
    for s in range(slots):
        near[s].wait()
        project(s, y)
        far[s].wait()
        n = 2 * slots + s
        forward.append(remote(there(s), there(s), send_sem.at[n], recv_sem.at[n], (dp, beside)))
        masks(s)
        if s:
            forward[s - 1].wait()
            project(s - 1, 1 - y)
    forward[-1].wait()
    project(slots - 1, 1 - y)


def front(scale, full, atoms, counts, vectors, query_w, key_w, value_w):
    slots, rows, width = atoms.shape
    vm = pl.BlockSpec(memory_space=pltpu.VMEM)
    hbm = pl.BlockSpec(memory_space=pltpu.HBM)
    like = lambda *shape: jax.ShapeDtypeStruct(shape, bf16)
    out_shape = [
        like(slots, full, width),
        jax.ShapeDtypeStruct((slots, rows, full), f32),
        like(slots, rows, width),
        like(slots, width, rows),
        like(slots, full, width),
        like(slots, width, full),
        like(slots, full, width),
        like(slots, width, full),
    ]
    return pl.pallas_call(
        functools.partial(front_kernel, scale),
        in_specs=[vm, pl.BlockSpec(memory_space=pltpu.SMEM)] + [vm] * 4 + [hbm] * 3,
        out_specs=[vm] * len(out_shape),
        out_shape=out_shape,
        scratch_shapes=[pltpu.VMEM((width, width), bf16)] * 3
        + [
            pltpu.SemaphoreType.DMA((3,)),
            pltpu.SemaphoreType.DMA((3 * slots,)),
            pltpu.SemaphoreType.DMA((3 * slots,)),
        ],
        name="front",
        cost_estimate=pl.CostEstimate(
            flops=48 * slots * full * width * width, transcendentals=0, bytes_accessed=32 << 20
        ),
        compiler_params=pltpu.CompilerParams(vmem_limit_bytes=18 << 20, collective_id=0, has_side_effects=True),
    )(*(pltpu.with_memory_space_constraint(array, pltpu.HBM) for array in (atoms, counts, *vectors, query_w, key_w, value_w)))


def forward_kernel(q_ref, kt_ref, v_ref, bias_ref, mask_ref, out_ref, e_ref, mix_ref, rl_ref):
    _, heads, rows, full = bias_ref.shape
    lane_head = lax.broadcasted_iota(jnp.int32, (rows, 128), 1) // 8
    mask = mask_ref[0]
    ones = jnp.ones((full, 128), bf16)
    for b in range(heads // HPL):
        cols = slice(128 * b, 128 * b + 128)
        q = q_ref[0, :, cols].astype(f32)
        kt = kt_ref[0, cols, :]
        v = jnp.concatenate([v_ref[0, :, cols], ones], axis=1)
        mixed = jnp.zeros((rows, 128), f32)
        total = jnp.zeros((rows, 128), f32)
        for c in range(HPL // CHUNK):
            own = [lane_head == CHUNK * c + i for i in range(CHUNK)]
            left = jnp.concatenate([jnp.where(o, q, 0.0).astype(bf16) for o in own], axis=0)
            scores = matmul(left, kt).reshape(CHUNK, rows, full)
            hs = slice(HPL * b + CHUNK * c, HPL * b + CHUNK * (c + 1))
            scores = scores + bias_ref[0, hs].astype(f32)
            out_ref[0, hs] = scores.astype(bf16)
            scores = scores + mask[None]
            highest = jnp.max(scores, axis=-1, keepdims=True)
            e = jnp.exp(scores - highest).astype(bf16)
            e_ref[0, hs] = e
            sums = matmul(e.reshape(CHUNK * rows, full), v)
            for i, o in enumerate(own):
                mixed = jnp.where(o, sums[rows * i : rows * (i + 1), :128], mixed)
                total = jnp.where(o, sums[rows * i : rows * (i + 1), 128:], total)
        inverse = 1.0 / total
        mix_ref[0, :, cols] = mixed * inverse
        rl_ref[0, :, cols] = inverse


def attention_forward(q, kt, v, bias, mask):
    slots, heads, rows, full = bias.shape
    step = min(STEP, heads)
    width = step * 8
    natural = lambda n: pl.BlockSpec((1, n, width), lambda s, h: (s, 0, h))
    pair = pl.BlockSpec((1, step, rows, full), lambda s, h: (s, h, 0, 0))
    return pl.pallas_call(
        forward_kernel,
        grid=(slots, heads // step),
        in_specs=[
            natural(rows),
            pl.BlockSpec((1, width, full), lambda s, h: (s, h, 0)),
            natural(full),
            pair,
            pl.BlockSpec((1, rows, full), lambda s, h: (s, 0, 0)),
        ],
        out_specs=[pair, pair, natural(rows), natural(rows)],
        out_shape=[
            jax.ShapeDtypeStruct(bias.shape, bf16),
            jax.ShapeDtypeStruct(bias.shape, bf16),
            jax.ShapeDtypeStruct(q.shape, f32),
            jax.ShapeDtypeStruct(q.shape, f32),
        ],
        name="attention_forward",
        cost_estimate=pl.CostEstimate(
            flops=2 * bias.size * 512, transcendentals=bias.size, bytes_accessed=bias.size * 6
        ),
        compiler_params=pltpu.CompilerParams(vmem_limit_bytes=VMEM_PAIR),
    )(q, kt, v, bias, mask)


def attention_backward(s, b, qt_ref, dm_ref, dmt_ref, nm_ref, k_ref, vt_ref, e_ref, cot_ref, pg_ref, dq_ref, dkt_ref, dvt_ref):
    _, heads, rows, full = cot_ref.shape
    lane_head = lax.broadcasted_iota(jnp.int32, (rows, 128), 1) // 8
    shape = (8 * CHUNK, CHUNK * rows)
    same = lax.broadcasted_iota(jnp.int32, shape, 0) // 8 == lax.broadcasted_iota(jnp.int32, shape, 1) // rows
    ones = jnp.ones((128, full), bf16)
    cols = pl.ds(pl.multiple_of(128 * b, 128), 128)
    dm = dm_ref[s, :, cols].astype(f32)
    nm = nm_ref[s, :, cols].astype(f32)
    vt = jnp.concatenate([vt_ref[s, cols, :], ones], axis=0)
    k = k_ref[s, :, cols]
    dq = jnp.zeros((rows, 128), f32)
    for c in range(HPL // CHUNK):
        own = [lane_head == CHUNK * c + i for i in range(CHUNK)]
        left = jnp.concatenate(
            [
                jnp.concatenate([jnp.where(o, dm, 0.0), jnp.where(o, nm, 0.0)], axis=1).astype(bf16)
                for o in own
            ],
            axis=0,
        )
        centred = matmul(left, vt).reshape(CHUNK, rows, full)
        hs = pl.ds(HPL * b + CHUNK * c, CHUNK)
        e = e_ref[s, hs]
        grad = (e.astype(f32) * centred + cot_ref[s, hs].astype(f32)).astype(bf16)
        pg_ref[s, hs] = grad
        grad = grad.reshape(CHUNK * rows, full)
        sums = matmul(grad, k)
        for i, o in enumerate(own):
            dq = jnp.where(o, sums[rows * i : rows * (i + 1)], dq)
        rs = pl.ds(pl.multiple_of(128 * b + 8 * CHUNK * c, 8 * CHUNK), 8 * CHUNK)
        spread = lambda ref: jnp.where(
            same, jnp.concatenate([ref[s, rs, :].astype(f32)] * CHUNK, axis=1), 0.0
        ).astype(bf16)
        dkt_ref[s, rs, :] = matmul(spread(qt_ref), grad).astype(bf16)
        dvt_ref[s, rs, :] = matmul(spread(dmt_ref), e.reshape(CHUNK * rows, full)).astype(bf16)
    dq_ref[s, :, cols] = dq.astype(bf16)


def middle_kernel(
    parts,
    mix_ref,
    rl_ref,
    atoms_ref,
    dy_ref,
    out_b,
    gain_ref,
    shift_ref,
    outer_b,
    bias_ref,
    out_w,
    inner_w,
    outer_w,
    out_ref,
    *refs,
):
    pieces, refs = refs[: 2 * len(PIECES)], refs[2 * len(PIECES) :]
    (
    dm_ref,
    nm_ref,
    dmt_ref,
    dmid_ref,
    vec_ref,
    ow,
    iw,
    uw,
    act,
    dpre,
    dpre_in,
    inner,
    mixed,
    branch,
    branch_in,
    dyh,
    dy_in,
    grads,
    load_sem,
    send_sem,
    recv_sem,
    ) = refs
    here, width = atoms_ref.shape
    half = width // 2
    blocks = act.shape[1]
    slots, _, rows = dmt_ref.shape
    bits = parts.bit_length() - 1
    row = lax.axis_index("rows")
    dp = lax.axis_index("dp")
    core = row % 2
    y = row // 2
    sibling = (dp, row + 1 - 2 * core)

    loads = [
        pltpu.make_async_copy(hbm, vmem, load_sem.at[i])
        for i, (hbm, vmem) in enumerate(((out_w, ow), (inner_w, iw), (outer_w, uw)))
    ]
    for copy in loads:
        copy.start()
    barrier = pltpu.get_barrier_semaphore()
    pl.semaphore_signal(barrier, inc=1, device_id=sibling, device_id_type=pl.DeviceIdType.MESH)
    pl.semaphore_wait(barrier, 1)
    sent = []

    def send(source, target):
        n = len(sent)
        copy = pltpu.make_async_remote_copy(
            src_ref=source,
            dst_ref=target,
            send_sem=send_sem.at[n],
            recv_sem=recv_sem.at[n],
            device_id=sibling,
            device_id_type=pl.DeviceIdType.MESH,
        )
        copy.start()
        sent.append(copy)

    dy = dy_ref[...]
    dyh[0] = dy[:, :half]
    dyh[1] = dy[:, half:]
    send(dyh.at[1 - core], dy_in)
    mix = mix_ref[...]
    mixed[0] = mix.astype(bf16)
    send(mixed.at[0], mixed.at[1])
    loads[0].wait()
    middle = atoms_ref[...].astype(f32) + matmul(mixed[0], ow[...]) + wide(out_b)
    standard, inverse = standardize(middle)
    gain = wide(gain_ref)
    inner[0] = (standard * gain + wide(shift_ref)).astype(bf16)
    send(inner.at[0], inner.at[1])
    loads[1].wait()
    loads[2].wait()
    result = middle + wide(outer_b)
    bias = wide(bias_ref)
    grad_inner = jnp.zeros((here, width), f32)
    for b in range(blocks):
        cols = slice(width * b, width * (b + 1))
        pre = matmul(inner[0], iw[:, cols]) + bias[:, cols]
        cdf = 0.5 + 0.5 * lax.erf(pre * (0.5**0.5))
        low = (pre * cdf).astype(bf16)
        act[0, b] = low
        send(act.at[0, b], act.at[1, b])
        slope = cdf + pre * (jnp.exp(-0.5 * pre * pre) * 0.3989422804014327)
        grad = (times_transposed(dy, uw[cols, :]) * slope).astype(bf16)
        dpre[b] = grad
        result = result + matmul(low, uw[cols, :])
        grad_inner = grad_inner + times_transposed(grad, iw[:, cols])
        vec_ref[b : b + 1, :] = jnp.sum(grad.astype(f32), axis=0, keepdims=True)
    for i in range(blocks // 2):
        send(dpre.at[(blocks // 2) * (1 - core) + i], dpre_in.at[i])
    out_ref[...] = result.astype(bf16)
    dy_wide = dy.astype(f32)
    grad_middle = dy_wide + norm_back(grad_inner * gain, standard, inverse)
    dmid_ref[...] = grad_middle
    low = grad_middle.astype(bf16)
    branch[0] = low[:, :half]
    branch[1] = low[:, half:]
    send(branch.at[1 - core], branch_in)
    down = lambda value: jnp.sum(value, axis=0, keepdims=True)
    vec_ref[blocks : blocks + 1, :] = down(low.astype(f32))
    vec_ref[blocks + 1 : blocks + 2, :] = down(grad_inner * standard)
    vec_ref[blocks + 2 : blocks + 3, :] = down(grad_inner)
    vec_ref[blocks + 3 : blocks + 4, :] = down(dy_wide)
    scaled = times_transposed(low, ow[...]).astype(bf16).astype(f32) * rl_ref[...]
    nm_ref[...] = (-scaled * mix).astype(bf16)
    scaled = scaled.astype(bf16)
    dm_ref[...] = scaled
    for s in range(slots):
        dmt_ref[s] = scaled[rows * s : rows * (s + 1)].astype(f32).T.astype(bf16)

    for copy in sent:
        copy.wait()
    tall, short = blocks * width // parts, width // parts
    dy_own = dyh[core]
    for b in range(blocks):
        grads[width * b : width * (b + 1), :] = outer_sum(act[0, b], dy_own) + outer_sum(act[1, b], dy_in[...])
    base = blocks * width
    for i in range(blocks // 2):
        grad = outer_sum(inner[0], dpre[(blocks // 2) * core + i]) + outer_sum(inner[1], dpre_in[i])
        for k in range(2):
            grads[base + width * (2 * i + k) : base + width * (2 * i + k + 1), :] = grad[:, half * k : half * (k + 1)]
    last = base + width * blocks
    grads[last:, :] = outer_sum(mixed[0], branch[core]) + outer_sum(mixed[1], branch_in[...])

    def at(start, n, h):
        return grads[pl.ds(pl.multiple_of(start, 8), n), pl.ds(pl.multiple_of(h * 128, 128), 128)]

    start = {"outer": (0, tall), "inner": (base, short), "out": (last, short)}
    step = {"outer": short, "inner": width, "out": 0}
    for p in range(parts):
        j = xor(dp, p, bits)
        for r in range(2):
            h = other_bit(y, 0, r)
            for n, (opening, parts_of) in enumerate(PIECES):
                if opening == "y":
                    gone, q = r, p
                elif opening == "d0":
                    gone, q = p & 1, 2 * (p >> 1) + r
                else:
                    gone, q = (p >> 1) & 1, 2 * ((p >> 2) * 2 + (p & 1)) + r
                ref = pieces[2 * n + gone]
                for i, (kind, k) in enumerate(parts_of):
                    first, per = start[kind]
                    ref[q, short * i : short * (i + 1)] = at(first + step[kind] * k + per * j, short, h).astype(ref.dtype)


def middle(parts, mix, rl, atoms, dy, vectors, out_w, inner_w, outer_w, slots):
    here, width = atoms.shape
    hidden = inner_w.shape[1]
    blocks, half, rows = hidden // width, width // 2, here // slots
    tall, short = hidden // parts, width // parts
    assert hidden == 4 * width
    vm = pl.BlockSpec(memory_space=pltpu.VMEM)
    hbm = pl.BlockSpec(memory_space=pltpu.HBM)
    like = jax.ShapeDtypeStruct
    out_shape = [
        like((here, width), bf16),
        *(like((parts, len(blocks_of) * short, 128), kind) for _, blocks_of in PIECES for kind in (f32, bf16)),
        like((here, width), bf16),
        like((here, width), bf16),
        like((slots, width, rows), bf16),
        like((here, width), f32),
        like((blocks + 4, width), f32),
    ]
    transfers = 3 + blocks + blocks // 2 + 1
    return pl.pallas_call(
        functools.partial(middle_kernel, parts),
        in_specs=[vm] * 9 + [hbm] * 3,
        out_specs=[vm] * len(out_shape),
        out_shape=out_shape,
        scratch_shapes=[
            pltpu.VMEM((width, width), bf16),
            pltpu.VMEM((width, hidden), bf16),
            pltpu.VMEM((hidden, width), bf16),
            pltpu.VMEM((2, blocks, here, width), bf16),
            pltpu.VMEM((blocks, here, width), bf16),
            pltpu.VMEM((blocks // 2, here, width), bf16),
            pltpu.VMEM((2, here, width), bf16),
            pltpu.VMEM((2, here, width), bf16),
            pltpu.VMEM((2, here, half), bf16),
            pltpu.VMEM((here, half), bf16),
            pltpu.VMEM((2, here, half), bf16),
            pltpu.VMEM((here, half), bf16),
            pltpu.VMEM((2 * hidden + width, half), f32),
            pltpu.SemaphoreType.DMA((3,)),
            pltpu.SemaphoreType.DMA((transfers,)),
            pltpu.SemaphoreType.DMA((transfers,)),
        ],
        name="middle",
        cost_estimate=pl.CostEstimate(
            flops=12 * here * width * hidden, transcendentals=2 * here * hidden, bytes_accessed=12 << 20
        ),
        compiler_params=pltpu.CompilerParams(
            vmem_limit_bytes=20 << 20, collective_id=1, has_side_effects=True
        ),
    )(
        mix, rl, atoms, dy, *vectors,
        *(pltpu.with_memory_space_constraint(array, pltpu.HBM) for array in (out_w, inner_w, outer_w)),
    )


class Part:
    def __init__(self, names, order, rows, dtype=bf16, opening=None):
        self.opening = opening
        self.names, self.order, self.rows, self.dtype = names, order, rows, dtype
        self.steps, left = [], list(names)
        for name in order:
            others = [n for n in left if n != name]
            spots = []
            for q in range(1 << len(others)):
                base = sum(
                    self.stride(n) for i, n in enumerate(others) if (q >> (len(others) - 1 - i)) & 1
                )
                spots.append((base, base + self.stride(name)))
            self.steps.append((name, spots))
            left = others

    def stride(self, name):
        return 1 << (len(self.names) - 1 - self.names.index(name))

    def scratch(self):
        shapes = [pltpu.VMEM((1 << len(self.names), self.rows, 128), f32)]
        if self.opening:
            shapes.append(pltpu.VMEM((1 << len(self.names), self.rows, 128), self.dtype))
        for _, spots in self.steps:
            shapes += [pltpu.VMEM((len(spots), self.rows, 128), self.dtype)] * 2
        n = len(self.steps) + 1
        return shapes + [pltpu.SemaphoreType.DMA((n,)), pltpu.SemaphoreType.DMA((n,))]

    def bind(self, refs, partner):
        self.state, refs = refs[0], refs[1:]
        if self.opening:
            self.first, refs = refs[0], refs[1:]
        self.sends, self.recvs = refs[0:-2:2], refs[1:-2:2]
        self.send_sem, self.recv_sem, self.partner = refs[-2], refs[-1], partner

    def open(self, send):
        n = len(self.steps)
        self.copy = remote(send, self.first, self.send_sem.at[n], self.recv_sem.at[n], self.partner(self.opening))

    def opened(self, keep):
        self.copy.wait()
        self.state[...] = keep[...] + self.first[...].astype(f32)

    def go(self, n):
        name, spots = self.steps[n]
        for q, (_, far) in enumerate(spots):
            self.sends[n][q] = self.state[far].astype(self.dtype)
        self.copy = remote(
            self.sends[n], self.recvs[n], self.send_sem.at[n], self.recv_sem.at[n], self.partner(name)
        )

    def come(self, n):
        self.copy.wait()
        for q, (near, _) in enumerate(self.steps[n][1]):
            self.state[near] = self.state[near] + self.recvs[n][q].astype(f32)

    def share(self, ref):
        ref[...] = self.state[0].astype(ref.dtype)


def make_parts(parts, width, hidden):
    bits = ["d%d" % b for b in range(parts.bit_length() - 1)]
    high = bits[::-1]
    short = width // parts
    without = lambda name: [n for n in high if n != name]
    kinds = {
        "d0": (without("d0") + ["y"], ["y", "d1"]),
        "y": (high, ["d1", "d0"]),
        "d1": (without("d1") + ["y"], ["d0", "y"]),
    }
    early = [
        Part(kinds[opening][0], kinds[opening][1] + bits[2:], len(blocks) * short, opening=opening)
        for opening, blocks in PIECES
    ]
    q = Part(high + ["y"], ["d0", "y", "d1"] + bits[2:], short)
    k = Part(high + ["y"], ["y", "d1", "d0"] + bits[2:], short)
    v = Part(high + ["y"], ["d1", "d0", "y"] + bits[2:], short)
    s = Part(high + ["y"], ["d1", "d0", "y"] + bits[2:], 16, f32)
    return early, [q, k, v, s]


def back_kernel(parts, scale, hidden, *refs):
    (
        qt, dm, dmt, nm, k_ref, vt, e_ref, cot, atoms, dmid, gain_ref, shift_ref, vec_ref,
        *refs,
    ) = refs
    made, refs = refs[: 2 * len(PIECES)], refs[2 * len(PIECES) :]
    (
        query_w, key_w, value_w,
        pg, out_ref, total,
        dkt, dvt, dq, qw, kw, vw,
        dk_in, dv_in, dqh, dqh_in, vec_own, vec_in, standard, normed, partial, beside_send, beside_recv,
        across_send, across_recv, grads, vec_all, load_sem, send_sem, recv_sem,
        *refs,
    ) = refs
    slots, width, full = dkt.shape
    rows, half = dq.shape[1], width // 2
    bits = parts.bit_length() - 1
    short, tall = width // parts, hidden // parts
    row, dp = lax.axis_index("rows"), lax.axis_index("dp")
    core, y = row % 2, row // 2
    beside, across = (dp, row + 1 - 2 * core), (dp, row + 2 - 4 * y)

    def partner(name):
        if name == "y":
            return across
        b = int(name[1:])
        return (xor(dp, 1 << b, bits), row)

    early, late = make_parts(parts, width, hidden)
    for piece in early + late:
        n = len(piece.scratch())
        piece.bind(refs[:n], partner)
        refs = refs[n:]
    one, two = early[:3], early[3:]
    steps, late_steps = len(early[0].steps), len(late[0].steps)

    def opened(group):
        for piece in group:
            piece.opened(made[2 * early.index(piece)])
            piece.go(0)

    def advance(group, n):
        for piece in group:
            piece.come(n)
            if n + 1 < len(piece.steps):
                piece.go(n + 1)

    loads = [
        pltpu.make_async_copy(hbm, vmem, load_sem.at[i])
        for i, (hbm, vmem) in enumerate(((query_w, qw), (key_w, kw), (value_w, vw)))
    ]
    for copy in loads:
        copy.start()
    corner = (dp, 3 - row)
    meet([beside, across, corner] + [partner("d%d" % b) for b in range(bits)])
    for n, piece in enumerate(early):
        piece.open(made[2 * n + 1])

    sent = 0

    def send(source, target, device):
        nonlocal sent
        sent += 1
        return remote(source, target, send_sem.at[sent - 1], recv_sem.at[sent - 1], device)

    other = pl.ds(pl.multiple_of((1 - core) * half, half), half)
    mine = pl.ds(pl.multiple_of(core * half, half), half)
    gain, shift = wide(gain_ref), wide(shift_ref)
    down = lambda value: jnp.sum(value, axis=0, keepdims=True)
    gain_grad = shift_grad = value_bias = 0.0
    send_on, to_sibling = [], []
    for s in range(slots):
        def block(b, carry):
            attention_backward(s, b, qt, dm, dmt, nm, k_ref, vt, e_ref, cot, pg, dq, dkt, dvt)
            return carry

        lax.fori_loop(0, width // 128, block, 0)
        to_sibling.append(send(dkt.at[s, other, :], dk_in.at[s], beside))
        to_sibling.append(send(dvt.at[s, other, :], dv_in.at[s], beside))
        if s == 0:
            for copy in loads:
                copy.wait()
        standard[s] = standardize(atoms[s].astype(f32))[0]
        normed[s] = (standard[s] * gain + shift).astype(bf16)
        dv = dvt[s].T
        grad = times_transposed(dkt[s].T, kw[...]) + times_transposed(dv, vw[...])
        value_bias = value_bias + down(dv.astype(f32))
        gain_grad = gain_grad + down(grad * standard[s])
        shift_grad = shift_grad + down(grad)
        for i in range(full // rows):
            partial[xor(row, i, 2), s] = grad[rows * i : rows * (i + 1)]
        beside_send[s, 0] = partial[1, s].astype(bf16)
        beside_send[s, 1] = partial[3, s].astype(bf16)
        send_on.append(send(beside_send.at[s], beside_recv.at[s], beside))
        if s == slots - 2:
            opened(one)
    opened(two)
    dq_low = jnp.concatenate([dq[s] for s in range(slots)], axis=0)
    dqh[0] = dq_low[:, :half]
    dqh[1] = dq_low[:, half:]
    to_sibling.append(send(dqh.at[1 - core], dqh_in, beside))
    own = pl.ds(pl.multiple_of(row * rows, rows), rows)
    next_to = pl.ds(pl.multiple_of((row + 1 - 2 * core) * rows, rows), rows)
    rows_of = lambda ref, which: jnp.concatenate([ref[s, which, :] for s in range(slots)], axis=0)
    query_grad = times_transposed(dq_low, qw[...]) * scale
    vec_own[0:1, :] = gain_grad + down(query_grad * rows_of(standard, own))
    vec_own[1:2, :] = shift_grad + down(query_grad)
    vec_own[2:3, :] = down(dq_low.astype(f32)) * scale
    vec_own[3:4, :] = value_bias
    vec_own[4:12, :] = vec_ref[...]
    vec_own[12:16, :] = jnp.zeros((4, width), f32)
    vec_sent = send(vec_own, vec_in, beside)

    advance(one, 0)
    for s in range(slots):
        send_on[s].wait()
        across_send[s] = (partial[2, s] + beside_recv[s, 1].astype(f32)).astype(bf16)
    over = send(across_send, across_recv, across)

    for copy in to_sibling:
        copy.wait()
    grads[0] = (
        outer_sum(rows_of(normed, own), dqh[core]) + outer_sum(rows_of(normed, next_to), dqh_in[...])
    ) * scale
    key_total = value_total = 0.0
    add = lambda left, right: (left.astype(f32) + right.astype(f32)).astype(bf16)
    for s in range(slots):
        turned = normed[s].T
        key_total = key_total + times_transposed(turned, add(dkt[s, mine, :], dk_in[s]))
        value_total = value_total + times_transposed(turned, add(dvt[s, mine, :], dv_in[s]))
    grads[1] = key_total
    grads[2] = value_total
    vec_sent.wait()
    vec = vec_own[...] + vec_in[...]
    vec_all[...] = jnp.zeros_like(vec_all)
    for j in range(parts):
        vec_all[j, 0:4, :short] = vec[0:4, short * j : short * (j + 1)]
        vec_all[j, 4:8, :short] = vec[8:12, short * j : short * (j + 1)]
        start = tall * j
        vec_all[j, 8:9, :tall] = vec[4 + start // width : 5 + start // width, start % width : start % width + tall]
    for p in range(parts):
        j = xor(dp, p, bits)
        for r in range(2):
            lanes = pl.ds(pl.multiple_of(other_bit(y, 0, r) * 128, 128), 128)
            for i, piece in enumerate(late[:3]):
                piece.state[2 * p + r] = grads[i, pl.ds(pl.multiple_of(j * short, short), short), lanes]
            late[3].state[2 * p + r] = vec_all[j, :, lanes]
    for piece in late:
        piece.go(0)

    advance(two, 0)
    advance(one, 1)
    advance(late, 0)
    advance(two, 1)
    over.wait()
    for s in range(slots):
        some = slice(rows * s, rows * (s + 1))
        grad = partial[0, s] + beside_recv[s, 0].astype(f32) + across_recv[s].astype(f32) + query_grad[some]
        stand, inverse = standardize(atoms[s, own, :].astype(f32))
        out_ref[some, :] = (dmid[some, :] + norm_back(grad * gain, stand, inverse)).astype(bf16)
    for n in range(2, steps):
        advance(one, n)
        advance(late, n - 1)
        advance(two, n)

    def place(group, at):
        for piece in group:
            piece.share(total.at[row, at : at + piece.rows])
            at += piece.rows
        return at

    cut = place(early, 0)
    mine, theirs = total.at[row, :cut], total.at[across[1], :cut]
    arrive = send(mine, mine, across)
    ends = [send(mine, mine, beside)]
    for n in range(steps - 1, late_steps):
        advance(late, n)
    place(late, cut)
    rest = total.at[row, cut:]
    ends += [send(rest, rest, device) for device in (across, corner, beside)]
    arrive.wait()
    ends.append(send(theirs, theirs, beside))
    for copy in ends:
        copy.wait()


def back(parts, scale, qt, dm, dmt, nm, k, vt, weights, cot, atoms, dmid, vectors, vec, pieces, query_w, key_w, value_w):
    slots, width, full = vt.shape
    rows, half = qt.shape[2], width // 2
    here, hidden = slots * rows, width * 4
    vm = pl.BlockSpec(memory_space=pltpu.VMEM)
    far = pl.BlockSpec(memory_space=pltpu.HBM)
    kinds = sum(make_parts(parts, width, hidden), [])
    count = sum(piece.rows for piece in kinds)
    transfers = 3 * slots + 9
    scratch = [
        pltpu.VMEM((slots, width, full), bf16),
        pltpu.VMEM((slots, width, full), bf16),
        pltpu.VMEM((slots, rows, width), bf16),
        pltpu.VMEM((width, width), bf16),
        pltpu.VMEM((width, width), bf16),
        pltpu.VMEM((width, width), bf16),
        pltpu.VMEM((slots, half, full), bf16),
        pltpu.VMEM((slots, half, full), bf16),
        pltpu.VMEM((2, here, half), bf16),
        pltpu.VMEM((here, half), bf16),
        pltpu.VMEM((16, width), f32),
        pltpu.VMEM((16, width), f32),
        pltpu.VMEM((slots, full, width), f32),
        pltpu.VMEM((slots, full, width), bf16),
        pltpu.VMEM((4, slots, rows, width), f32),
        pltpu.VMEM((slots, 2, rows, width), bf16),
        pltpu.VMEM((slots, 2, rows, width), bf16),
        pltpu.VMEM((slots, rows, width), bf16),
        pltpu.VMEM((slots, rows, width), bf16),
        pltpu.VMEM((3, width, half), f32),
        pltpu.VMEM((parts, 16, half), f32),
        pltpu.SemaphoreType.DMA((3,)),
        pltpu.SemaphoreType.DMA((transfers,)),
        pltpu.SemaphoreType.DMA((transfers,)),
    ]
    for piece in kinds:
        scratch += piece.scratch()
    return pl.pallas_call(
        functools.partial(back_kernel, parts, scale, hidden),
        in_specs=[vm] * (13 + 2 * len(PIECES)) + [far] * 3,
        out_specs=[vm] * 3,
        out_shape=[
            jax.ShapeDtypeStruct(cot.shape, bf16),
            jax.ShapeDtypeStruct((here, width), bf16),
            jax.ShapeDtypeStruct((4, count, 128), bf16),
        ],
        scratch_shapes=scratch,
        name="back",
        cost_estimate=pl.CostEstimate(
            flops=40 * slots * full * width * width, transcendentals=0, bytes_accessed=32 << 20
        ),
        compiler_params=pltpu.CompilerParams(vmem_limit_bytes=VMEM_BACK, collective_id=2, has_side_effects=True),
    )(
        qt, dm, dmt, nm, k, vt, weights, cot, atoms, dmid, *vectors, vec, *pieces,
        *(pltpu.with_memory_space_constraint(array, pltpu.HBM) for array in (query_w, key_w, value_w)),
    )


def last_kernel(
    total, grad_ref, made_ref, pair, grad_out, made_out, uw, ow, iw, qw, kw, vw, again, ashift, qb, vb, ob, fgain,
    fshift, ub, ib, pair_out, sem,
):
    copy = pltpu.make_async_copy(pair, pair_out, sem)
    copy.start()
    grad_out[...] = grad_ref[...]
    made_out[...] = made_ref[...]
    short = ow.shape[0]
    blocks = iw.shape[1] // 2 // 256
    spots = [spot for _, of in PIECES for spot in of] + [("query", 0), ("key", 0), ("value", 0)]
    refs = {"outer": uw, "inner": iw, "out": ow, "query": qw, "key": kw, "value": vw}
    at = 0
    for name, k in spots:
        ref = refs[name]
        first = short * k if name == "outer" else 0
        for r in range(4):
            core, y = r % 2, r // 2
            col = 256 * (core * blocks + k if name == "inner" else core) + 128 * y
            ref[first : first + short, col : col + 128] = total[r, at : at + short, :].astype(f32)
        at += short
    for i, ref in enumerate((again, ashift, qb, vb, ob, fgain, fshift, ub)):
        ref[...] = total[0, at : at + 16, :].astype(f32)[i : i + 1, :short]
    for y in range(2):
        n = min(128, ib.shape[1] - 128 * y)
        if n > 0:
            ib[:, 128 * y : 128 * y + n] = total[2 * y, at : at + 16, :].astype(f32)[8:9, :n]
    copy.wait()


def last(parts, total, grad, made, pair, hidden):
    here, width = grad.shape
    short, tall = width // parts, hidden // parts
    vm = pl.BlockSpec(memory_space=pltpu.VMEM)
    like = lambda *shape: jax.ShapeDtypeStruct(shape, f32)
    out_shape = [jax.ShapeDtypeStruct(grad.shape, bf16)] * 2
    out_shape += [like(tall, width), like(short, width), like(short, hidden)] + [like(short, width)] * 3
    out_shape += [like(1, short)] * 8 + [like(1, tall), jax.ShapeDtypeStruct(pair.shape, bf16)]
    return pl.pallas_call(
        last_kernel,
        in_specs=[vm] * 3 + [pl.BlockSpec(memory_space=pl.ANY)],
        out_specs=[vm] * (len(out_shape) - 1) + [pl.BlockSpec(memory_space=pl.ANY)],
        out_shape=out_shape,
        scratch_shapes=[pltpu.SemaphoreType.DMA],
        name="last",
        compiler_params=pltpu.CompilerParams(vmem_limit_bytes=16 << 20),
    )(total, grad, made, pair)


def local(
    parts,
    group,
    atoms,
    pair_bias,
    mol_counts,
    attn_gain,
    attn_shift,
    query_weight,
    query_bias,
    key_weight,
    value_weight,
    value_bias,
    out_weight,
    out_bias,
    ffn_gain,
    ffn_shift,
    inner_weight,
    inner_bias,
    outer_weight,
    outer_bias,
    atoms_cotangent,
    pair_cotangent,
):
    slots, part_rows, width = atoms.shape
    heads = pair_bias.shape[1]
    full = pair_bias.shape[3]
    scale = (width // heads) ** (-0.5)
    here = slots * part_rows
    hidden = inner_weight.shape[1]
    flat = lambda array: array.reshape(here, width)
    all_atoms, mask, q, qt, k, kt, v, vt = front(
        scale, full, atoms, mol_counts, (attn_gain, attn_shift, query_bias, value_bias), query_weight, key_weight, value_weight
    )
    pair_out, weights, mixed, inverse_sum = attention_forward(q, kt, v, pair_bias, mask)
    atoms_out, *pieces, scaled, centre, scaled_turned, grad_middle, vec = middle(
        parts,
        flat(mixed),
        flat(inverse_sum),
        flat(atoms),
        flat(atoms_cotangent),
        (out_bias, ffn_gain, ffn_shift, outer_bias, inner_bias),
        out_weight,
        inner_weight,
        outer_weight,
        slots,
    )
    pair_grad, grad, total = back(
        parts,
        scale,
        qt,
        scaled.reshape(q.shape),
        scaled_turned,
        centre.reshape(q.shape),
        k,
        vt,
        weights,
        pair_cotangent,
        all_atoms,
        grad_middle,
        (attn_gain, attn_shift),
        vec,
        pieces,
        query_weight,
        key_weight,
        value_weight,
    )
    grad, made, uw, ow, iw, qw, kw, vw, again, ashift, qb, vb, ob, fgain, fshift, ub, ib, pair_grad = last(
        parts, total, grad, atoms_out, pair_grad, hidden
    )
    line = lambda array: array.reshape(-1)
    return (
        made.reshape(atoms.shape),
        pair_out,
        grad.reshape(atoms.shape),
        pair_grad,
        line(again),
        line(ashift),
        qw,
        line(qb),
        kw,
        vw,
        line(vb),
        ow,
        line(ob),
        line(fgain),
        line(fshift),
        iw,
        line(ib),
        uw,
        line(ub),
    )


def solution(mesh):
    one, two = P("dp"), P("dp", None)
    atoms_spec, pair_spec = P("dp", "rows", None), P("dp", None, "rows", None)
    in_specs = (atoms_spec, pair_spec, two) + (P(),) * 15 + (atoms_spec, pair_spec)
    out_specs = (
        (atoms_spec, pair_spec, atoms_spec, pair_spec, one, one, two, one, two, two, one, two)
        + (one, one, one, two, one, two, one)
    )
    run = functools.partial(local, mesh.shape["dp"], mesh.shape["rows"])
    return jax.shard_map(run, mesh=mesh, in_specs=in_specs, out_specs=out_specs, check_vma=False)
```

```python
import functools

import jax
import jax.numpy as jnp
from jax import lax
from jax.experimental import pallas as pl
from jax.experimental.pallas import tpu as pltpu
from jax.sharding import PartitionSpec as P

f32, bf16 = jnp.float32, jnp.bfloat16
BIG = 1e9
HPL = 16
CHUNK = 8
STEP = 32
VMEM_PAIR = 16 << 20
VMEM_BACK = 26 << 20
MESH = pl.DeviceIdType.MESH
PIECES = (
    ("d0", (("outer", 0), ("outer", 1))),
    ("y", (("outer", 2),)),
    ("d1", (("outer", 3),)),
    ("d0", (("inner", 0),)),
    ("y", (("inner", 1), ("inner", 2))),
    ("d1", (("inner", 3), ("out", 0))),
)


def standardize(value):
    centred = value - jnp.mean(value, axis=-1, keepdims=True)
    inverse = lax.rsqrt(jnp.mean(centred * centred, axis=-1, keepdims=True) + 1e-05)
    return (centred * inverse, inverse)


def norm_back(grad_normed, standard, inverse):
    return inverse * (
        grad_normed
        - jnp.mean(grad_normed, axis=-1, keepdims=True)
        - standard * jnp.mean(grad_normed * standard, axis=-1, keepdims=True)
    )


def matmul(left, right):
    return jnp.dot(left, right, preferred_element_type=f32)


def times_transposed(left, right):
    return lax.dot_general(left, right, (((1,), (1,)), ((), ())), preferred_element_type=f32)


def outer_sum(left, right):
    return lax.dot_general(left, right, (((0,), (0,)), ((), ())), preferred_element_type=f32)


def other_bit(index, bit, const):
    own = (index // (1 << bit)) % 2
    return 1 - own if (const >> bit) & 1 else own


def xor(index, const, bits):
    return sum(other_bit(index, b, const) * (1 << b) for b in range(bits))


def remote(source, target, send_sem, recv_sem, device):
    copy = pltpu.make_async_remote_copy(
        src_ref=source, dst_ref=target, send_sem=send_sem, recv_sem=recv_sem, device_id=device, device_id_type=MESH
    )
    copy.start()
    return copy


def meet(devices):
    barrier = pltpu.get_barrier_semaphore()
    for device in devices:
        pl.semaphore_signal(barrier, inc=1, device_id=device, device_id_type=MESH)
    pl.semaphore_wait(barrier, len(devices))


def wide(ref):
    return ref[...].astype(f32).reshape(1, -1)


def front_kernel(
    scale,
    atoms_ref,
    counts_ref,
    gain_ref,
    shift_ref,
    query_b,
    value_b,
    query_w,
    key_w,
    value_w,
    all_ref,
    mask_ref,
    q_ref,
    qt_ref,
    k_ref,
    kt_ref,
    v_ref,
    vt_ref,
    qw,
    kw,
    vw,
    load_sem,
    send_sem,
    recv_sem,
):
    slots, rows, width = atoms_ref.shape
    full = mask_ref.shape[2]
    row, dp = lax.axis_index("rows"), lax.axis_index("dp")
    core, y = row % 2, row // 2
    beside, across = row + 1 - 2 * core, row + 2 - 4 * y
    loads = [
        pltpu.make_async_copy(hbm, vmem, load_sem.at[i])
        for i, (hbm, vmem) in enumerate(((query_w, qw), (key_w, kw), (value_w, vw)))
    ]
    for copy in loads:
        copy.start()
    meet([(dp, beside), (dp, across)])
    at = lambda r: pl.ds(pl.multiple_of(r * rows, rows), rows)
    here = lambda s: all_ref.at[s, at(row), :]
    there = lambda s: all_ref.at[s, at(across), :]
    far = [remote(atoms_ref.at[s], here(s), send_sem.at[s], recv_sem.at[s], (dp, across)) for s in range(slots)]
    near = [
        remote(atoms_ref.at[s], here(s), send_sem.at[slots + s], recv_sem.at[slots + s], (dp, beside))
        for s in range(slots)
    ]
    gain, shift = wide(gain_ref), wide(shift_ref)
    bias = wide(value_b)
    for s in range(slots):
        all_ref[s, at(row), :] = atoms_ref[s]
    own = atoms_ref[...].reshape(slots * rows, width).astype(f32)
    normed = (standardize(own)[0] * gain + shift).astype(bf16)
    loads[0].wait()
    queries = ((matmul(normed, qw[...]) + wide(query_b)) * scale).astype(bf16)
    for s in range(slots):
        part = queries[rows * s : rows * (s + 1)]
        q_ref[s] = part
        qt_ref[s] = part.T
    loads[1].wait()
    loads[2].wait()

    def project(s, chip):
        some = pl.ds(pl.multiple_of(chip * 2 * rows, 2 * rows), 2 * rows)
        normed = (standardize(all_ref[s, some, :].astype(f32))[0] * gain + shift).astype(bf16)
        keys = matmul(normed, kw[...]).astype(bf16)
        k_ref[s, some, :] = keys
        kt_ref[s, :, some] = keys.T
        values = (matmul(normed, vw[...]) + bias).astype(bf16)
        v_ref[s, some, :] = values
        vt_ref[s, :, some] = values.T

    def masks(s):
        ends = [counts_ref[s, 0]]
        for m in range(1, counts_ref.shape[1]):
            ends.append(ends[-1] + counts_ref[s, m])
        keys_at = lax.broadcasted_iota(jnp.int32, (1, full), 1)
        queries_at = lax.broadcasted_iota(jnp.int32, (rows, 1), 0) + row * rows
        count = lambda at: sum((end <= at).astype(jnp.int32) for end in ends)
        mask_ref[s] = jnp.where(count(keys_at) == count(queries_at), 0.0, -BIG)

    forward = []
    for s in range(slots):
        near[s].wait()
        project(s, y)
        far[s].wait()
        n = 2 * slots + s
        forward.append(remote(there(s), there(s), send_sem.at[n], recv_sem.at[n], (dp, beside)))
        masks(s)
        if s:
            forward[s - 1].wait()
            project(s - 1, 1 - y)
    forward[-1].wait()
    project(slots - 1, 1 - y)


def front(scale, full, atoms, counts, vectors, query_w, key_w, value_w):
    slots, rows, width = atoms.shape
    vm = pl.BlockSpec(memory_space=pltpu.VMEM)
    hbm = pl.BlockSpec(memory_space=pltpu.HBM)
    like = lambda *shape: jax.ShapeDtypeStruct(shape, bf16)
    out_shape = [
        like(slots, full, width),
        jax.ShapeDtypeStruct((slots, rows, full), f32),
        like(slots, rows, width),
        like(slots, width, rows),
        like(slots, full, width),
        like(slots, width, full),
        like(slots, full, width),
        like(slots, width, full),
    ]
    return pl.pallas_call(
        functools.partial(front_kernel, scale),
        in_specs=[vm, pl.BlockSpec(memory_space=pltpu.SMEM)] + [vm] * 4 + [hbm] * 3,
        out_specs=[vm] * len(out_shape),
        out_shape=out_shape,
        scratch_shapes=[pltpu.VMEM((width, width), bf16)] * 3
        + [
            pltpu.SemaphoreType.DMA((3,)),
            pltpu.SemaphoreType.DMA((3 * slots,)),
            pltpu.SemaphoreType.DMA((3 * slots,)),
        ],
        name="front",
        cost_estimate=pl.CostEstimate(
            flops=48 * slots * full * width * width, transcendentals=0, bytes_accessed=32 << 20
        ),
        compiler_params=pltpu.CompilerParams(vmem_limit_bytes=18 << 20, collective_id=0, has_side_effects=True),
    )(*(pltpu.with_memory_space_constraint(array, pltpu.HBM) for array in (atoms, counts, *vectors, query_w, key_w, value_w)))


def forward_kernel(q_ref, kt_ref, v_ref, bias_ref, mask_ref, out_ref, e_ref, mix_ref, rl_ref):
    _, heads, rows, full = bias_ref.shape
    lane_head = lax.broadcasted_iota(jnp.int32, (rows, 128), 1) // 8
    mask = mask_ref[0]
    ones = jnp.ones((full, 128), bf16)
    for b in range(heads // HPL):
        cols = slice(128 * b, 128 * b + 128)
        q = q_ref[0, :, cols].astype(f32)
        kt = kt_ref[0, cols, :]
        v = jnp.concatenate([v_ref[0, :, cols], ones], axis=1)
        mixed = jnp.zeros((rows, 128), f32)
        total = jnp.zeros((rows, 128), f32)
        for c in range(HPL // CHUNK):
            own = [lane_head == CHUNK * c + i for i in range(CHUNK)]
            left = jnp.concatenate([jnp.where(o, q, 0.0).astype(bf16) for o in own], axis=0)
            scores = matmul(left, kt).reshape(CHUNK, rows, full)
            hs = slice(HPL * b + CHUNK * c, HPL * b + CHUNK * (c + 1))
            scores = scores + bias_ref[0, hs].astype(f32)
            out_ref[0, hs] = scores.astype(bf16)
            scores = scores + mask[None]
            highest = jnp.max(scores, axis=-1, keepdims=True)
            e = jnp.exp(scores - highest).astype(bf16)
            e_ref[0, hs] = e
            sums = matmul(e.reshape(CHUNK * rows, full), v)
            for i, o in enumerate(own):
                mixed = jnp.where(o, sums[rows * i : rows * (i + 1), :128], mixed)
                total = jnp.where(o, sums[rows * i : rows * (i + 1), 128:], total)
        inverse = 1.0 / total
        mix_ref[0, :, cols] = mixed * inverse
        rl_ref[0, :, cols] = inverse


def attention_forward(q, kt, v, bias, mask):
    slots, heads, rows, full = bias.shape
    step = min(STEP, heads)
    width = step * 8
    natural = lambda n: pl.BlockSpec((1, n, width), lambda s, h: (s, 0, h))
    pair = pl.BlockSpec((1, step, rows, full), lambda s, h: (s, h, 0, 0))
    return pl.pallas_call(
        forward_kernel,
        grid=(slots, heads // step),
        in_specs=[
            natural(rows),
            pl.BlockSpec((1, width, full), lambda s, h: (s, h, 0)),
            natural(full),
            pair,
            pl.BlockSpec((1, rows, full), lambda s, h: (s, 0, 0)),
        ],
        out_specs=[pair, pair, natural(rows), natural(rows)],
        out_shape=[
            jax.ShapeDtypeStruct(bias.shape, bf16),
            jax.ShapeDtypeStruct(bias.shape, bf16),
            jax.ShapeDtypeStruct(q.shape, f32),
            jax.ShapeDtypeStruct(q.shape, f32),
        ],
        name="attention_forward",
        cost_estimate=pl.CostEstimate(
            flops=2 * bias.size * 512, transcendentals=bias.size, bytes_accessed=bias.size * 6
        ),
        compiler_params=pltpu.CompilerParams(vmem_limit_bytes=VMEM_PAIR),
    )(q, kt, v, bias, mask)


def attention_backward(s, b, qt_ref, dm_ref, dmt_ref, nm_ref, k_ref, vt_ref, e_ref, cot_ref, pg_ref, dq_ref, dkt_ref, dvt_ref):
    _, heads, rows, full = cot_ref.shape
    lane_head = lax.broadcasted_iota(jnp.int32, (rows, 128), 1) // 8
    shape = (8 * CHUNK, CHUNK * rows)
    same = lax.broadcasted_iota(jnp.int32, shape, 0) // 8 == lax.broadcasted_iota(jnp.int32, shape, 1) // rows
    ones = jnp.ones((128, full), bf16)
    cols = pl.ds(pl.multiple_of(128 * b, 128), 128)
    dm = dm_ref[s, :, cols].astype(f32)
    nm = nm_ref[s, :, cols].astype(f32)
    vt = jnp.concatenate([vt_ref[s, cols, :], ones], axis=0)
    k = k_ref[s, :, cols]
    dq = jnp.zeros((rows, 128), f32)
    for c in range(HPL // CHUNK):
        own = [lane_head == CHUNK * c + i for i in range(CHUNK)]
        left = jnp.concatenate(
            [
                jnp.concatenate([jnp.where(o, dm, 0.0), jnp.where(o, nm, 0.0)], axis=1).astype(bf16)
                for o in own
            ],
            axis=0,
        )
        centred = matmul(left, vt).reshape(CHUNK, rows, full)
        hs = pl.ds(HPL * b + CHUNK * c, CHUNK)
        e = e_ref[s, hs]
        grad = (e.astype(f32) * centred + cot_ref[s, hs].astype(f32)).astype(bf16)
        pg_ref[s, hs] = grad
        grad = grad.reshape(CHUNK * rows, full)
        sums = matmul(grad, k)
        for i, o in enumerate(own):
            dq = jnp.where(o, sums[rows * i : rows * (i + 1)], dq)
        rs = pl.ds(pl.multiple_of(128 * b + 8 * CHUNK * c, 8 * CHUNK), 8 * CHUNK)
        spread = lambda ref: jnp.where(
            same, jnp.concatenate([ref[s, rs, :].astype(f32)] * CHUNK, axis=1), 0.0
        ).astype(bf16)
        dkt_ref[s, rs, :] = matmul(spread(qt_ref), grad).astype(bf16)
        dvt_ref[s, rs, :] = matmul(spread(dmt_ref), e.reshape(CHUNK * rows, full)).astype(bf16)
    dq_ref[s, :, cols] = dq.astype(bf16)


def middle_kernel(
    parts,
    mix_ref,
    rl_ref,
    atoms_ref,
    dy_ref,
    out_b,
    gain_ref,
    shift_ref,
    outer_b,
    bias_ref,
    out_w,
    inner_w,
    outer_w,
    out_ref,
    *refs,
):
    pieces, refs = refs[: 2 * len(PIECES)], refs[2 * len(PIECES) :]
    (
    dm_ref,
    nm_ref,
    dmt_ref,
    dmid_ref,
    vec_ref,
    ow,
    iw,
    uw,
    act,
    dpre,
    dpre_in,
    inner,
    mixed,
    branch,
    branch_in,
    dyh,
    dy_in,
    grads,
    load_sem,
    send_sem,
    recv_sem,
    ) = refs
    here, width = atoms_ref.shape
    half = width // 2
    blocks = act.shape[1]
    slots, _, rows = dmt_ref.shape
    bits = parts.bit_length() - 1
    row = lax.axis_index("rows")
    dp = lax.axis_index("dp")
    core = row % 2
    y = row // 2
    sibling = (dp, row + 1 - 2 * core)

    loads = [
        pltpu.make_async_copy(hbm, vmem, load_sem.at[i])
        for i, (hbm, vmem) in enumerate(((out_w, ow), (inner_w, iw), (outer_w, uw)))
    ]
    for copy in loads:
        copy.start()
    barrier = pltpu.get_barrier_semaphore()
    pl.semaphore_signal(barrier, inc=1, device_id=sibling, device_id_type=pl.DeviceIdType.MESH)
    pl.semaphore_wait(barrier, 1)
    sent = []

    def send(source, target):
        n = len(sent)
        copy = pltpu.make_async_remote_copy(
            src_ref=source,
            dst_ref=target,
            send_sem=send_sem.at[n],
            recv_sem=recv_sem.at[n],
            device_id=sibling,
            device_id_type=pl.DeviceIdType.MESH,
        )
        copy.start()
        sent.append(copy)

    dy = dy_ref[...]
    dyh[0] = dy[:, :half]
    dyh[1] = dy[:, half:]
    send(dyh.at[1 - core], dy_in)
    mix = mix_ref[...]
    mixed[0] = mix.astype(bf16)
    send(mixed.at[0], mixed.at[1])
    loads[0].wait()
    middle = atoms_ref[...].astype(f32) + matmul(mixed[0], ow[...]) + wide(out_b)
    standard, inverse = standardize(middle)
    gain = wide(gain_ref)
    inner[0] = (standard * gain + wide(shift_ref)).astype(bf16)
    send(inner.at[0], inner.at[1])
    loads[1].wait()
    loads[2].wait()
    result = middle + wide(outer_b)
    bias = wide(bias_ref)
    grad_inner = jnp.zeros((here, width), f32)
    for b in range(blocks):
        cols = slice(width * b, width * (b + 1))
        pre = matmul(inner[0], iw[:, cols]) + bias[:, cols]
        cdf = 0.5 + 0.5 * lax.erf(pre * (0.5**0.5))
        low = (pre * cdf).astype(bf16)
        act[0, b] = low
        send(act.at[0, b], act.at[1, b])
        slope = cdf + pre * (jnp.exp(-0.5 * pre * pre) * 0.3989422804014327)
        grad = (times_transposed(dy, uw[cols, :]) * slope).astype(bf16)
        dpre[b] = grad
        result = result + matmul(low, uw[cols, :])
        grad_inner = grad_inner + times_transposed(grad, iw[:, cols])
        vec_ref[b : b + 1, :] = jnp.sum(grad.astype(f32), axis=0, keepdims=True)
    for i in range(blocks // 2):
        send(dpre.at[(blocks // 2) * (1 - core) + i], dpre_in.at[i])
    out_ref[...] = result.astype(bf16)
    dy_wide = dy.astype(f32)
    grad_middle = dy_wide + norm_back(grad_inner * gain, standard, inverse)
    dmid_ref[...] = grad_middle
    low = grad_middle.astype(bf16)
    branch[0] = low[:, :half]
    branch[1] = low[:, half:]
    send(branch.at[1 - core], branch_in)
    down = lambda value: jnp.sum(value, axis=0, keepdims=True)
    vec_ref[blocks : blocks + 1, :] = down(low.astype(f32))
    vec_ref[blocks + 1 : blocks + 2, :] = down(grad_inner * standard)
    vec_ref[blocks + 2 : blocks + 3, :] = down(grad_inner)
    vec_ref[blocks + 3 : blocks + 4, :] = down(dy_wide)
    scaled = times_transposed(low, ow[...]).astype(bf16).astype(f32) * rl_ref[...]
    nm_ref[...] = (-scaled * mix).astype(bf16)
    scaled = scaled.astype(bf16)
    dm_ref[...] = scaled
    for s in range(slots):
        dmt_ref[s] = scaled[rows * s : rows * (s + 1)].astype(f32).T.astype(bf16)

    for copy in sent:
        copy.wait()
    tall, short = blocks * width // parts, width // parts
    dy_own = dyh[core]
    for b in range(blocks):
        grads[width * b : width * (b + 1), :] = outer_sum(act[0, b], dy_own) + outer_sum(act[1, b], dy_in[...])
    base = blocks * width
    for i in range(blocks // 2):
        grad = outer_sum(inner[0], dpre[(blocks // 2) * core + i]) + outer_sum(inner[1], dpre_in[i])
        for k in range(2):
            grads[base + width * (2 * i + k) : base + width * (2 * i + k + 1), :] = grad[:, half * k : half * (k + 1)]
    last = base + width * blocks
    grads[last:, :] = outer_sum(mixed[0], branch[core]) + outer_sum(mixed[1], branch_in[...])

    def at(start, n, h):
        return grads[pl.ds(pl.multiple_of(start, 8), n), pl.ds(pl.multiple_of(h * 128, 128), 128)]

    start = {"outer": (0, tall), "inner": (base, short), "out": (last, short)}
    step = {"outer": short, "inner": width, "out": 0}
    for p in range(parts):
        j = xor(dp, p, bits)
        for r in range(2):
            h = other_bit(y, 0, r)
            for n, (opening, parts_of) in enumerate(PIECES):
                if opening == "y":
                    gone, q = r, p
                elif opening == "d0":
                    gone, q = p & 1, 2 * (p >> 1) + r
                else:
                    gone, q = (p >> 1) & 1, 2 * ((p >> 2) * 2 + (p & 1)) + r
                ref = pieces[2 * n + gone]
                for i, (kind, k) in enumerate(parts_of):
                    first, per = start[kind]
                    ref[q, short * i : short * (i + 1)] = at(first + step[kind] * k + per * j, short, h).astype(ref.dtype)


def middle(parts, mix, rl, atoms, dy, vectors, out_w, inner_w, outer_w, slots):
    here, width = atoms.shape
    hidden = inner_w.shape[1]
    blocks, half, rows = hidden // width, width // 2, here // slots
    tall, short = hidden // parts, width // parts
    assert hidden == 4 * width
    vm = pl.BlockSpec(memory_space=pltpu.VMEM)
    hbm = pl.BlockSpec(memory_space=pltpu.HBM)
    like = jax.ShapeDtypeStruct
    out_shape = [
        like((here, width), bf16),
        *(like((parts, len(blocks_of) * short, 128), kind) for _, blocks_of in PIECES for kind in (f32, bf16)),
        like((here, width), bf16),
        like((here, width), bf16),
        like((slots, width, rows), bf16),
        like((here, width), f32),
        like((blocks + 4, width), f32),
    ]
    transfers = 3 + blocks + blocks // 2 + 1
    return pl.pallas_call(
        functools.partial(middle_kernel, parts),
        in_specs=[vm] * 9 + [hbm] * 3,
        out_specs=[vm] * len(out_shape),
        out_shape=out_shape,
        scratch_shapes=[
            pltpu.VMEM((width, width), bf16),
            pltpu.VMEM((width, hidden), bf16),
            pltpu.VMEM((hidden, width), bf16),
            pltpu.VMEM((2, blocks, here, width), bf16),
            pltpu.VMEM((blocks, here, width), bf16),
            pltpu.VMEM((blocks // 2, here, width), bf16),
            pltpu.VMEM((2, here, width), bf16),
            pltpu.VMEM((2, here, width), bf16),
            pltpu.VMEM((2, here, half), bf16),
            pltpu.VMEM((here, half), bf16),
            pltpu.VMEM((2, here, half), bf16),
            pltpu.VMEM((here, half), bf16),
            pltpu.VMEM((2 * hidden + width, half), f32),
            pltpu.SemaphoreType.DMA((3,)),
            pltpu.SemaphoreType.DMA((transfers,)),
            pltpu.SemaphoreType.DMA((transfers,)),
        ],
        name="middle",
        cost_estimate=pl.CostEstimate(
            flops=12 * here * width * hidden, transcendentals=2 * here * hidden, bytes_accessed=12 << 20
        ),
        compiler_params=pltpu.CompilerParams(
            vmem_limit_bytes=20 << 20, collective_id=1, has_side_effects=True
        ),
    )(
        mix, rl, atoms, dy, *vectors, out_w, inner_w, outer_w,
    )


class Part:
    def __init__(self, names, order, rows, dtype=bf16, opening=None):
        self.opening = opening
        self.names, self.order, self.rows, self.dtype = names, order, rows, dtype
        self.steps, left = [], list(names)
        for name in order:
            others = [n for n in left if n != name]
            spots = []
            for q in range(1 << len(others)):
                base = sum(
                    self.stride(n) for i, n in enumerate(others) if (q >> (len(others) - 1 - i)) & 1
                )
                spots.append((base, base + self.stride(name)))
            self.steps.append((name, spots))
            left = others

    def stride(self, name):
        return 1 << (len(self.names) - 1 - self.names.index(name))

    def scratch(self):
        shapes = [pltpu.VMEM((1 << len(self.names), self.rows, 128), f32)]
        if self.opening:
            shapes.append(pltpu.VMEM((1 << len(self.names), self.rows, 128), self.dtype))
        for _, spots in self.steps:
            shapes += [pltpu.VMEM((len(spots), self.rows, 128), self.dtype)] * 2
        n = len(self.steps) + 1
        return shapes + [pltpu.SemaphoreType.DMA((n,)), pltpu.SemaphoreType.DMA((n,))]

    def bind(self, refs, partner):
        self.state, refs = refs[0], refs[1:]
        if self.opening:
            self.first, refs = refs[0], refs[1:]
        self.sends, self.recvs = refs[0:-2:2], refs[1:-2:2]
        self.send_sem, self.recv_sem, self.partner = refs[-2], refs[-1], partner

    def open(self, send):
        n = len(self.steps)
        self.copy = remote(send, self.first, self.send_sem.at[n], self.recv_sem.at[n], self.partner(self.opening))

    def opened(self, keep):
        self.copy.wait()
        self.state[...] = keep[...] + self.first[...].astype(f32)

    def go(self, n):
        name, spots = self.steps[n]
        for q, (_, far) in enumerate(spots):
            self.sends[n][q] = self.state[far].astype(self.dtype)
        self.copy = remote(
            self.sends[n], self.recvs[n], self.send_sem.at[n], self.recv_sem.at[n], self.partner(name)
        )

    def come(self, n):
        self.copy.wait()
        for q, (near, _) in enumerate(self.steps[n][1]):
            self.state[near] = self.state[near] + self.recvs[n][q].astype(f32)

    def share(self, ref):
        ref[...] = self.state[0].astype(ref.dtype)


def make_parts(parts, width, hidden):
    bits = ["d%d" % b for b in range(parts.bit_length() - 1)]
    high = bits[::-1]
    short = width // parts
    without = lambda name: [n for n in high if n != name]
    kinds = {
        "d0": (without("d0") + ["y"], ["y", "d1"]),
        "y": (high, ["d1", "d0"]),
        "d1": (without("d1") + ["y"], ["d0", "y"]),
    }
    early = [
        Part(kinds[opening][0], kinds[opening][1] + bits[2:], len(blocks) * short, opening=opening)
        for opening, blocks in PIECES
    ]
    q = Part(high + ["y"], ["d0", "y", "d1"] + bits[2:], short)
    k = Part(high + ["y"], ["y", "d1", "d0"] + bits[2:], short)
    v = Part(high + ["y"], ["d1", "d0", "y"] + bits[2:], short)
    s = Part(high + ["y"], ["d1", "d0", "y"] + bits[2:], 16, f32)
    return early, [q, k, v, s]


def back_kernel(parts, scale, hidden, *refs):
    (
        qt, dm, dmt, nm, k_ref, vt, e_ref, cot, atoms, dmid, gain_ref, shift_ref, vec_ref,
        *refs,
    ) = refs
    made, refs = refs[: 2 * len(PIECES)], refs[2 * len(PIECES) :]
    (
        query_w, key_w, value_w,
        pg, out_ref, total,
        dkt, dvt, dq, qw, kw, vw,
        dk_in, dv_in, dqh, dqh_in, vec_own, vec_in, standard, normed, partial, beside_send, beside_recv,
        across_send, across_recv, grads, vec_all, load_sem, send_sem, recv_sem,
        *refs,
    ) = refs
    slots, width, full = dkt.shape
    rows, half = dq.shape[1], width // 2
    bits = parts.bit_length() - 1
    short, tall = width // parts, hidden // parts
    row, dp = lax.axis_index("rows"), lax.axis_index("dp")
    core, y = row % 2, row // 2
    beside, across = (dp, row + 1 - 2 * core), (dp, row + 2 - 4 * y)

    def partner(name):
        if name == "y":
            return across
        b = int(name[1:])
        return (xor(dp, 1 << b, bits), row)

    early, late = make_parts(parts, width, hidden)
    for piece in early + late:
        n = len(piece.scratch())
        piece.bind(refs[:n], partner)
        refs = refs[n:]
    one, two = early[:3], early[3:]
    steps, late_steps = len(early[0].steps), len(late[0].steps)

    def opened(group):
        for piece in group:
            piece.opened(made[2 * early.index(piece)])
            piece.go(0)

    def advance(group, n):
        for piece in group:
            piece.come(n)
            if n + 1 < len(piece.steps):
                piece.go(n + 1)

    loads = [
        pltpu.make_async_copy(hbm, vmem, load_sem.at[i])
        for i, (hbm, vmem) in enumerate(((query_w, qw), (key_w, kw), (value_w, vw)))
    ]
    for copy in loads:
        copy.start()
    corner = (dp, 3 - row)
    meet([beside, across, corner] + [partner("d%d" % b) for b in range(bits)])
    for n, piece in enumerate(early):
        piece.open(made[2 * n + 1])

    sent = 0

    def send(source, target, device):
        nonlocal sent
        sent += 1
        return remote(source, target, send_sem.at[sent - 1], recv_sem.at[sent - 1], device)

    other = pl.ds(pl.multiple_of((1 - core) * half, half), half)
    mine = pl.ds(pl.multiple_of(core * half, half), half)
    gain, shift = wide(gain_ref), wide(shift_ref)
    down = lambda value: jnp.sum(value, axis=0, keepdims=True)
    gain_grad = shift_grad = value_bias = 0.0
    send_on, to_sibling = [], []
    for s in range(slots):
        def block(b, carry):
            attention_backward(s, b, qt, dm, dmt, nm, k_ref, vt, e_ref, cot, pg, dq, dkt, dvt)
            return carry

        lax.fori_loop(0, width // 128, block, 0)
        to_sibling.append(send(dkt.at[s, other, :], dk_in.at[s], beside))
        to_sibling.append(send(dvt.at[s, other, :], dv_in.at[s], beside))
        if s == 0:
            for copy in loads:
                copy.wait()
        standard[s] = standardize(atoms[s].astype(f32))[0]
        normed[s] = (standard[s] * gain + shift).astype(bf16)
        dv = dvt[s].T
        grad = times_transposed(dkt[s].T, kw[...]) + times_transposed(dv, vw[...])
        value_bias = value_bias + down(dv.astype(f32))
        gain_grad = gain_grad + down(grad * standard[s])
        shift_grad = shift_grad + down(grad)
        for i in range(full // rows):
            partial[xor(row, i, 2), s] = grad[rows * i : rows * (i + 1)]
        beside_send[s, 0] = partial[1, s].astype(bf16)
        beside_send[s, 1] = partial[3, s].astype(bf16)
        send_on.append(send(beside_send.at[s], beside_recv.at[s], beside))
        if s == slots - 2:
            opened(one)
    opened(two)
    dq_low = jnp.concatenate([dq[s] for s in range(slots)], axis=0)
    dqh[0] = dq_low[:, :half]
    dqh[1] = dq_low[:, half:]
    to_sibling.append(send(dqh.at[1 - core], dqh_in, beside))
    own = pl.ds(pl.multiple_of(row * rows, rows), rows)
    next_to = pl.ds(pl.multiple_of((row + 1 - 2 * core) * rows, rows), rows)
    rows_of = lambda ref, which: jnp.concatenate([ref[s, which, :] for s in range(slots)], axis=0)
    query_grad = times_transposed(dq_low, qw[...]) * scale
    vec_own[0:1, :] = gain_grad + down(query_grad * rows_of(standard, own))
    vec_own[1:2, :] = shift_grad + down(query_grad)
    vec_own[2:3, :] = down(dq_low.astype(f32)) * scale
    vec_own[3:4, :] = value_bias
    vec_own[4:12, :] = vec_ref[...]
    vec_own[12:16, :] = jnp.zeros((4, width), f32)
    vec_sent = send(vec_own, vec_in, beside)

    advance(one, 0)
    for s in range(slots):
        send_on[s].wait()
        across_send[s] = (partial[2, s] + beside_recv[s, 1].astype(f32)).astype(bf16)
    over = send(across_send, across_recv, across)

    for copy in to_sibling:
        copy.wait()
    grads[0] = (
        outer_sum(rows_of(normed, own), dqh[core]) + outer_sum(rows_of(normed, next_to), dqh_in[...])
    ) * scale
    key_total = value_total = 0.0
    add = lambda left, right: (left.astype(f32) + right.astype(f32)).astype(bf16)
    for s in range(slots):
        turned = normed[s].T
        key_total = key_total + times_transposed(turned, add(dkt[s, mine, :], dk_in[s]))
        value_total = value_total + times_transposed(turned, add(dvt[s, mine, :], dv_in[s]))
    grads[1] = key_total
    grads[2] = value_total
    vec_sent.wait()
    vec = vec_own[...] + vec_in[...]
    vec_all[...] = jnp.zeros_like(vec_all)
    for j in range(parts):
        vec_all[j, 0:4, :short] = vec[0:4, short * j : short * (j + 1)]
        vec_all[j, 4:8, :short] = vec[8:12, short * j : short * (j + 1)]
        start = tall * j
        vec_all[j, 8:9, :tall] = vec[4 + start // width : 5 + start // width, start % width : start % width + tall]
    for p in range(parts):
        j = xor(dp, p, bits)
        for r in range(2):
            lanes = pl.ds(pl.multiple_of(other_bit(y, 0, r) * 128, 128), 128)
            for i, piece in enumerate(late[:3]):
                piece.state[2 * p + r] = grads[i, pl.ds(pl.multiple_of(j * short, short), short), lanes]
            late[3].state[2 * p + r] = vec_all[j, :, lanes]
    for piece in late:
        piece.go(0)

    advance(two, 0)
    advance(one, 1)
    advance(late, 0)
    advance(two, 1)
    over.wait()
    for s in range(slots):
        some = slice(rows * s, rows * (s + 1))
        grad = partial[0, s] + beside_recv[s, 0].astype(f32) + across_recv[s].astype(f32) + query_grad[some]
        stand, inverse = standardize(atoms[s, own, :].astype(f32))
        out_ref[some, :] = (dmid[some, :] + norm_back(grad * gain, stand, inverse)).astype(bf16)
    for n in range(2, steps):
        advance(one, n)
        advance(late, n - 1)
        advance(two, n)

    def place(group, at):
        for piece in group:
            piece.share(total.at[row, at : at + piece.rows])
            at += piece.rows
        return at

    cut = place(early, 0)
    mine, theirs = total.at[row, :cut], total.at[across[1], :cut]
    arrive = send(mine, mine, across)
    ends = [send(mine, mine, beside)]
    for n in range(steps - 1, late_steps):
        advance(late, n)
    place(late, cut)
    rest = total.at[row, cut:]
    ends += [send(rest, rest, device) for device in (across, corner, beside)]
    arrive.wait()
    ends.append(send(theirs, theirs, beside))
    for copy in ends:
        copy.wait()


def back(parts, scale, qt, dm, dmt, nm, k, vt, weights, cot, atoms, dmid, vectors, vec, pieces, query_w, key_w, value_w):
    slots, width, full = vt.shape
    rows, half = qt.shape[2], width // 2
    here, hidden = slots * rows, width * 4
    vm = pl.BlockSpec(memory_space=pltpu.VMEM)
    far = pl.BlockSpec(memory_space=pltpu.HBM)
    kinds = sum(make_parts(parts, width, hidden), [])
    count = sum(piece.rows for piece in kinds)
    transfers = 3 * slots + 9
    scratch = [
        pltpu.VMEM((slots, width, full), bf16),
        pltpu.VMEM((slots, width, full), bf16),
        pltpu.VMEM((slots, rows, width), bf16),
        pltpu.VMEM((width, width), bf16),
        pltpu.VMEM((width, width), bf16),
        pltpu.VMEM((width, width), bf16),
        pltpu.VMEM((slots, half, full), bf16),
        pltpu.VMEM((slots, half, full), bf16),
        pltpu.VMEM((2, here, half), bf16),
        pltpu.VMEM((here, half), bf16),
        pltpu.VMEM((16, width), f32),
        pltpu.VMEM((16, width), f32),
        pltpu.VMEM((slots, full, width), f32),
        pltpu.VMEM((slots, full, width), bf16),
        pltpu.VMEM((4, slots, rows, width), f32),
        pltpu.VMEM((slots, 2, rows, width), bf16),
        pltpu.VMEM((slots, 2, rows, width), bf16),
        pltpu.VMEM((slots, rows, width), bf16),
        pltpu.VMEM((slots, rows, width), bf16),
        pltpu.VMEM((3, width, half), f32),
        pltpu.VMEM((parts, 16, half), f32),
        pltpu.SemaphoreType.DMA((3,)),
        pltpu.SemaphoreType.DMA((transfers,)),
        pltpu.SemaphoreType.DMA((transfers,)),
    ]
    for piece in kinds:
        scratch += piece.scratch()
    return pl.pallas_call(
        functools.partial(back_kernel, parts, scale, hidden),
        in_specs=[vm] * (13 + 2 * len(PIECES)) + [far] * 3,
        out_specs=[vm] * 3,
        out_shape=[
            jax.ShapeDtypeStruct(cot.shape, bf16),
            jax.ShapeDtypeStruct((here, width), bf16),
            jax.ShapeDtypeStruct((4, count, 128), bf16),
        ],
        scratch_shapes=scratch,
        name="back",
        cost_estimate=pl.CostEstimate(
            flops=40 * slots * full * width * width, transcendentals=0, bytes_accessed=32 << 20
        ),
        compiler_params=pltpu.CompilerParams(vmem_limit_bytes=VMEM_BACK, collective_id=2, has_side_effects=True),
    )(
        qt, dm, dmt, nm, k, vt, weights, cot, atoms, dmid, *vectors, vec, *pieces,
        *(pltpu.with_memory_space_constraint(array, pltpu.HBM) for array in (query_w, key_w, value_w)),
    )


def last_kernel(total, grad_ref, made_ref, pair, *refs):
    count = 18
    outs, refs = refs[:count], refs[count:]
    (grad_out, made_out, *_, pair_out), (uw, ow, iw, qw, kw, vw), small, sem = outs, refs[:6], refs[6:15], refs[15]
    copies = []

    def move(source, target):
        copy = pltpu.make_async_copy(source, target, sem.at[len(copies)])
        copy.start()
        copies.append(copy)

    move(pair, pair_out)
    move(grad_ref, grad_out)
    move(made_ref, made_out)
    short = ow.shape[0]
    blocks = iw.shape[1] // 2 // 256
    spots = [spot for _, of in PIECES for spot in of] + [("query", 0), ("key", 0), ("value", 0)]
    refs = {"outer": uw, "inner": iw, "out": ow, "query": qw, "key": kw, "value": vw}
    at = 0
    for name, k in spots:
        ref = refs[name]
        first = short * k if name == "outer" else 0
        for r in range(4):
            core, y = r % 2, r // 2
            col = 256 * (core * blocks + k if name == "inner" else core) + 128 * y
            ref[first : first + short, col : col + 128] = total[r, at : at + short, :].astype(f32)
        at += short
    for ref, out in zip((uw, ow, iw, qw, kw, vw), outs[2:8]):
        move(ref, out)
    for i, ref in enumerate(small[:8]):
        ref[...] = total[0, at : at + 16, :].astype(f32)[i : i + 1, :short]
    ib = small[8]
    for y in range(2):
        n = min(128, ib.shape[1] - 128 * y)
        if n > 0:
            ib[:, 128 * y : 128 * y + n] = total[2 * y, at : at + 16, :].astype(f32)[8:9, :n]
    for ref, out in zip(small, outs[8:17]):
        move(ref, out)
    for copy in copies:
        copy.wait()


def last(parts, total, grad, made, pair, hidden):
    here, width = grad.shape
    short, tall = width // parts, hidden // parts
    vm = pl.BlockSpec(memory_space=pltpu.VMEM)
    hbm = pl.BlockSpec(memory_space=pl.ANY)
    shapes = [(tall, width), (short, width), (short, hidden)] + [(short, width)] * 3
    shapes += [(1, short)] * 8 + [(1, tall)]
    out_shape = [jax.ShapeDtypeStruct(grad.shape, bf16)] * 2
    out_shape += [jax.ShapeDtypeStruct(shape, f32) for shape in shapes]
    out_shape.append(jax.ShapeDtypeStruct(pair.shape, bf16))
    return pl.pallas_call(
        last_kernel,
        in_specs=[vm] + [hbm] * 3,
        out_specs=[hbm] * len(out_shape),
        out_shape=out_shape,
        scratch_shapes=[pltpu.VMEM(shape, f32) for shape in shapes] + [pltpu.SemaphoreType.DMA((len(out_shape),))],
        name="last",
        compiler_params=pltpu.CompilerParams(vmem_limit_bytes=16 << 20),
    )(total, grad, made, pair)


def local(
    parts,
    group,
    atoms,
    pair_bias,
    mol_counts,
    attn_gain,
    attn_shift,
    query_weight,
    query_bias,
    key_weight,
    value_weight,
    value_bias,
    out_weight,
    out_bias,
    ffn_gain,
    ffn_shift,
    inner_weight,
    inner_bias,
    outer_weight,
    outer_bias,
    atoms_cotangent,
    pair_cotangent,
):
    slots, part_rows, width = atoms.shape
    heads = pair_bias.shape[1]
    full = pair_bias.shape[3]
    scale = (width // heads) ** (-0.5)
    here = slots * part_rows
    hidden = inner_weight.shape[1]
    flat = lambda array: array.reshape(here, width)
    all_atoms, mask, q, qt, k, kt, v, vt = front(
        scale, full, atoms, mol_counts, (attn_gain, attn_shift, query_bias, value_bias), query_weight, key_weight, value_weight
    )
    pair_out, weights, mixed, inverse_sum = attention_forward(q, kt, v, pair_bias, mask)
    atoms_out, *pieces, scaled, centre, scaled_turned, grad_middle, vec = middle(
        parts,
        flat(mixed),
        flat(inverse_sum),
        flat(atoms),
        flat(atoms_cotangent),
        (out_bias, ffn_gain, ffn_shift, outer_bias, inner_bias),
        out_weight,
        inner_weight,
        outer_weight,
        slots,
    )
    pair_grad, grad, total = back(
        parts,
        scale,
        qt,
        scaled.reshape(q.shape),
        scaled_turned,
        centre.reshape(q.shape),
        k,
        vt,
        weights,
        pair_cotangent,
        all_atoms,
        grad_middle,
        (attn_gain, attn_shift),
        vec,
        pieces,
        query_weight,
        key_weight,
        value_weight,
    )
    grad, made, uw, ow, iw, qw, kw, vw, again, ashift, qb, vb, ob, fgain, fshift, ub, ib, pair_grad = last(
        parts, total, grad, atoms_out, pair_grad, hidden
    )
    line = lambda array: array.reshape(-1)
    return (
        made.reshape(atoms.shape),
        pair_out,
        grad.reshape(atoms.shape),
        pair_grad,
        line(again),
        line(ashift),
        qw,
        line(qb),
        kw,
        vw,
        line(vb),
        ow,
        line(ob),
        line(fgain),
        line(fshift),
        iw,
        line(ib),
        uw,
        line(ub),
    )


def solution(mesh):
    one, two = P("dp"), P("dp", None)
    atoms_spec, pair_spec = P("dp", "rows", None), P("dp", None, "rows", None)
    in_specs = (atoms_spec, pair_spec, two) + (P(),) * 15 + (atoms_spec, pair_spec)
    out_specs = (
        (atoms_spec, pair_spec, atoms_spec, pair_spec, one, one, two, one, two, two, one, two)
        + (one, one, one, two, one, two, one)
    )
    run = functools.partial(local, mesh.shape["dp"], mesh.shape["rows"])
    return jax.shard_map(run, mesh=mesh, in_specs=in_specs, out_specs=out_specs, check_vma=False)
```

```python
import functools

import jax
import jax.numpy as jnp
from jax import lax
from jax.experimental import pallas as pl
from jax.experimental.pallas import tpu as pltpu
from jax.sharding import PartitionSpec as P

f32, bf16 = jnp.float32, jnp.bfloat16
BIG = 1e9
HPL = 16
CHUNK = 8
STEP = 32
VMEM_PAIR = 16 << 20
VMEM_BACK = 26 << 20
MESH = pl.DeviceIdType.MESH
PIECES = (
    ("d0", (("outer", 0), ("outer", 1))),
    ("y", (("outer", 2),)),
    ("d1", (("outer", 3),)),
    ("d0", (("inner", 0),)),
    ("y", (("inner", 1), ("inner", 2))),
    ("d1", (("inner", 3), ("out", 0))),
)


def standardize(value):
    centred = value - jnp.mean(value, axis=-1, keepdims=True)
    inverse = lax.rsqrt(jnp.mean(centred * centred, axis=-1, keepdims=True) + 1e-05)
    return (centred * inverse, inverse)


def norm_back(grad_normed, standard, inverse):
    return inverse * (
        grad_normed
        - jnp.mean(grad_normed, axis=-1, keepdims=True)
        - standard * jnp.mean(grad_normed * standard, axis=-1, keepdims=True)
    )


def matmul(left, right):
    return jnp.dot(left, right, preferred_element_type=f32)


def times_transposed(left, right):
    return lax.dot_general(left, right, (((1,), (1,)), ((), ())), preferred_element_type=f32)


def outer_sum(left, right):
    return lax.dot_general(left, right, (((0,), (0,)), ((), ())), preferred_element_type=f32)


def other_bit(index, bit, const):
    own = (index // (1 << bit)) % 2
    return 1 - own if (const >> bit) & 1 else own


def xor(index, const, bits):
    return sum(other_bit(index, b, const) * (1 << b) for b in range(bits))


def remote(source, target, send_sem, recv_sem, device):
    copy = pltpu.make_async_remote_copy(
        src_ref=source, dst_ref=target, send_sem=send_sem, recv_sem=recv_sem, device_id=device, device_id_type=MESH
    )
    copy.start()
    return copy


def meet(devices):
    barrier = pltpu.get_barrier_semaphore()
    for device in devices:
        pl.semaphore_signal(barrier, inc=1, device_id=device, device_id_type=MESH)
    pl.semaphore_wait(barrier, len(devices))


def wide(ref):
    return ref[...].astype(f32).reshape(1, -1)


def front_kernel(
    scale,
    atoms_ref,
    counts_ref,
    gain_ref,
    shift_ref,
    query_b,
    value_b,
    query_w,
    key_w,
    value_w,
    all_ref,
    mask_ref,
    q_ref,
    qt_ref,
    k_ref,
    kt_ref,
    v_ref,
    vt_ref,
    qw,
    kw,
    vw,
    load_sem,
    send_sem,
    recv_sem,
):
    slots, rows, width = atoms_ref.shape
    full = mask_ref.shape[2]
    row, dp = lax.axis_index("rows"), lax.axis_index("dp")
    core, y = row % 2, row // 2
    beside, across = row + 1 - 2 * core, row + 2 - 4 * y
    loads = [
        pltpu.make_async_copy(hbm, vmem, load_sem.at[i])
        for i, (hbm, vmem) in enumerate(((query_w, qw), (key_w, kw), (value_w, vw)))
    ]
    for copy in loads:
        copy.start()
    meet([(dp, beside), (dp, across)])
    at = lambda r: pl.ds(pl.multiple_of(r * rows, rows), rows)
    here = lambda s: all_ref.at[s, at(row), :]
    there = lambda s: all_ref.at[s, at(across), :]
    far = [remote(atoms_ref.at[s], here(s), send_sem.at[s], recv_sem.at[s], (dp, across)) for s in range(slots)]
    near = [
        remote(atoms_ref.at[s], here(s), send_sem.at[slots + s], recv_sem.at[slots + s], (dp, beside))
        for s in range(slots)
    ]
    gain, shift = wide(gain_ref), wide(shift_ref)
    bias = wide(value_b)
    for s in range(slots):
        all_ref[s, at(row), :] = atoms_ref[s]
    own = atoms_ref[...].reshape(slots * rows, width).astype(f32)
    normed = (standardize(own)[0] * gain + shift).astype(bf16)
    loads[0].wait()
    queries = ((matmul(normed, qw[...]) + wide(query_b)) * scale).astype(bf16)
    for s in range(slots):
        part = queries[rows * s : rows * (s + 1)]
        q_ref[s] = part
        qt_ref[s] = part.T
    loads[1].wait()
    loads[2].wait()

    def project(s, chip):
        some = pl.ds(pl.multiple_of(chip * 2 * rows, 2 * rows), 2 * rows)
        normed = (standardize(all_ref[s, some, :].astype(f32))[0] * gain + shift).astype(bf16)
        keys = matmul(normed, kw[...]).astype(bf16)
        k_ref[s, some, :] = keys
        kt_ref[s, :, some] = keys.T
        values = (matmul(normed, vw[...]) + bias).astype(bf16)
        v_ref[s, some, :] = values
        vt_ref[s, :, some] = values.T

    def masks(s):
        ends = [counts_ref[s, 0]]
        for m in range(1, counts_ref.shape[1]):
            ends.append(ends[-1] + counts_ref[s, m])
        keys_at = lax.broadcasted_iota(jnp.int32, (1, full), 1)
        queries_at = lax.broadcasted_iota(jnp.int32, (rows, 1), 0) + row * rows
        count = lambda at: sum((end <= at).astype(jnp.int32) for end in ends)
        mask_ref[s] = jnp.where(count(keys_at) == count(queries_at), 0.0, -BIG)

    forward = []

    def pass_on(s):
        far[s].wait()
        n = 2 * slots + s
        forward.append(remote(there(s), there(s), send_sem.at[n], recv_sem.at[n], (dp, beside)))

    for s in range(slots):
        if s == slots - 1:
            pass_on(0)
        near[s].wait()
        project(s, y)
    for s in range(slots):
        masks(s)
    for s in range(1, slots):
        pass_on(s)
        forward[s - 1].wait()
        project(s - 1, 1 - y)
    forward[-1].wait()
    project(slots - 1, 1 - y)


def front(scale, full, atoms, counts, vectors, query_w, key_w, value_w):
    slots, rows, width = atoms.shape
    vm = pl.BlockSpec(memory_space=pltpu.VMEM)
    hbm = pl.BlockSpec(memory_space=pltpu.HBM)
    like = lambda *shape: jax.ShapeDtypeStruct(shape, bf16)
    out_shape = [
        like(slots, full, width),
        jax.ShapeDtypeStruct((slots, rows, full), f32),
        like(slots, rows, width),
        like(slots, width, rows),
        like(slots, full, width),
        like(slots, width, full),
        like(slots, full, width),
        like(slots, width, full),
    ]
    return pl.pallas_call(
        functools.partial(front_kernel, scale),
        in_specs=[vm, pl.BlockSpec(memory_space=pltpu.SMEM)] + [vm] * 4 + [hbm] * 3,
        out_specs=[vm] * len(out_shape),
        out_shape=out_shape,
        scratch_shapes=[pltpu.VMEM((width, width), bf16)] * 3
        + [
            pltpu.SemaphoreType.DMA((3,)),
            pltpu.SemaphoreType.DMA((3 * slots,)),
            pltpu.SemaphoreType.DMA((3 * slots,)),
        ],
        name="front",
        cost_estimate=pl.CostEstimate(
            flops=48 * slots * full * width * width, transcendentals=0, bytes_accessed=32 << 20
        ),
        compiler_params=pltpu.CompilerParams(vmem_limit_bytes=18 << 20, collective_id=0, has_side_effects=True),
    )(*(pltpu.with_memory_space_constraint(array, pltpu.HBM) for array in (atoms, counts, *vectors, query_w, key_w, value_w)))


def forward_kernel(q_ref, kt_ref, v_ref, bias_ref, mask_ref, out_ref, e_ref, mix_ref, rl_ref):
    _, heads, rows, full = bias_ref.shape
    lane_head = lax.broadcasted_iota(jnp.int32, (rows, 128), 1) // 8
    mask = mask_ref[0]
    ones = jnp.ones((full, 128), bf16)
    for b in range(heads // HPL):
        cols = slice(128 * b, 128 * b + 128)
        q = q_ref[0, :, cols].astype(f32)
        kt = kt_ref[0, cols, :]
        v = jnp.concatenate([v_ref[0, :, cols], ones], axis=1)
        mixed = jnp.zeros((rows, 128), f32)
        total = jnp.zeros((rows, 128), f32)
        for c in range(HPL // CHUNK):
            own = [lane_head == CHUNK * c + i for i in range(CHUNK)]
            left = jnp.concatenate([jnp.where(o, q, 0.0).astype(bf16) for o in own], axis=0)
            scores = matmul(left, kt).reshape(CHUNK, rows, full)
            hs = slice(HPL * b + CHUNK * c, HPL * b + CHUNK * (c + 1))
            scores = scores + bias_ref[0, hs].astype(f32)
            out_ref[0, hs] = scores.astype(bf16)
            scores = scores + mask[None]
            highest = jnp.max(scores, axis=-1, keepdims=True)
            e = jnp.exp(scores - highest).astype(bf16)
            e_ref[0, hs] = e
            sums = matmul(e.reshape(CHUNK * rows, full), v)
            for i, o in enumerate(own):
                mixed = jnp.where(o, sums[rows * i : rows * (i + 1), :128], mixed)
                total = jnp.where(o, sums[rows * i : rows * (i + 1), 128:], total)
        inverse = 1.0 / total
        mix_ref[0, :, cols] = mixed * inverse
        rl_ref[0, :, cols] = inverse


def attention_forward(q, kt, v, bias, mask):
    slots, heads, rows, full = bias.shape
    step = min(STEP, heads)
    width = step * 8
    natural = lambda n: pl.BlockSpec((1, n, width), lambda s, h: (s, 0, h))
    pair = pl.BlockSpec((1, step, rows, full), lambda s, h: (s, h, 0, 0))
    return pl.pallas_call(
        forward_kernel,
        grid=(slots, heads // step),
        in_specs=[
            natural(rows),
            pl.BlockSpec((1, width, full), lambda s, h: (s, h, 0)),
            natural(full),
            pair,
            pl.BlockSpec((1, rows, full), lambda s, h: (s, 0, 0)),
        ],
        out_specs=[pair, pair, natural(rows), natural(rows)],
        out_shape=[
            jax.ShapeDtypeStruct(bias.shape, bf16),
            jax.ShapeDtypeStruct(bias.shape, bf16),
            jax.ShapeDtypeStruct(q.shape, f32),
            jax.ShapeDtypeStruct(q.shape, f32),
        ],
        name="attention_forward",
        cost_estimate=pl.CostEstimate(
            flops=2 * bias.size * 512, transcendentals=bias.size, bytes_accessed=bias.size * 6
        ),
        compiler_params=pltpu.CompilerParams(vmem_limit_bytes=VMEM_PAIR),
    )(q, kt, v, bias, mask)


def attention_backward(s, b, qt_ref, dm_ref, dmt_ref, nm_ref, k_ref, vt_ref, e_ref, cot_ref, pg_ref, dq_ref, dkt_ref, dvt_ref):
    _, heads, rows, full = cot_ref.shape
    lane_head = lax.broadcasted_iota(jnp.int32, (rows, 128), 1) // 8
    shape = (8 * CHUNK, CHUNK * rows)
    same = lax.broadcasted_iota(jnp.int32, shape, 0) // 8 == lax.broadcasted_iota(jnp.int32, shape, 1) // rows
    ones = jnp.ones((128, full), bf16)
    cols = pl.ds(pl.multiple_of(128 * b, 128), 128)
    dm = dm_ref[s, :, cols].astype(f32)
    nm = nm_ref[s, :, cols].astype(f32)
    vt = jnp.concatenate([vt_ref[s, cols, :], ones], axis=0)
    k = k_ref[s, :, cols]
    dq = jnp.zeros((rows, 128), f32)
    for c in range(HPL // CHUNK):
        own = [lane_head == CHUNK * c + i for i in range(CHUNK)]
        left = jnp.concatenate(
            [
                jnp.concatenate([jnp.where(o, dm, 0.0), jnp.where(o, nm, 0.0)], axis=1).astype(bf16)
                for o in own
            ],
            axis=0,
        )
        centred = matmul(left, vt).reshape(CHUNK, rows, full)
        hs = pl.ds(HPL * b + CHUNK * c, CHUNK)
        e = e_ref[s, hs]
        grad = (e.astype(f32) * centred + cot_ref[s, hs].astype(f32)).astype(bf16)
        pg_ref[s, hs] = grad
        grad = grad.reshape(CHUNK * rows, full)
        sums = matmul(grad, k)
        for i, o in enumerate(own):
            dq = jnp.where(o, sums[rows * i : rows * (i + 1)], dq)
        rs = pl.ds(pl.multiple_of(128 * b + 8 * CHUNK * c, 8 * CHUNK), 8 * CHUNK)
        spread = lambda ref: jnp.where(
            same, jnp.concatenate([ref[s, rs, :].astype(f32)] * CHUNK, axis=1), 0.0
        ).astype(bf16)
        dkt_ref[s, rs, :] = matmul(spread(qt_ref), grad).astype(bf16)
        dvt_ref[s, rs, :] = matmul(spread(dmt_ref), e.reshape(CHUNK * rows, full)).astype(bf16)
    dq_ref[s, :, cols] = dq.astype(bf16)


def middle_kernel(
    parts,
    mix_ref,
    rl_ref,
    atoms_ref,
    dy_ref,
    out_b,
    gain_ref,
    shift_ref,
    outer_b,
    bias_ref,
    ow,
    iw,
    uw,
    out_ref,
    *refs,
):
    pieces, refs = refs[: 2 * len(PIECES)], refs[2 * len(PIECES) :]
    (
    dm_ref,
    nm_ref,
    dmt_ref,
    dmid_ref,
    vec_ref,
    act,
    dpre,
    dpre_in,
    inner,
    mixed,
    branch,
    branch_in,
    dyh,
    dy_in,
    grads,
    send_sem,
    recv_sem,
    ) = refs
    here, width = atoms_ref.shape
    half = width // 2
    blocks = act.shape[1]
    slots, _, rows = dmt_ref.shape
    bits = parts.bit_length() - 1
    row = lax.axis_index("rows")
    dp = lax.axis_index("dp")
    core = row % 2
    y = row // 2
    sibling = (dp, row + 1 - 2 * core)

    barrier = pltpu.get_barrier_semaphore()
    pl.semaphore_signal(barrier, inc=1, device_id=sibling, device_id_type=pl.DeviceIdType.MESH)
    sent = []

    def send(source, target):
        n = len(sent)
        copy = pltpu.make_async_remote_copy(
            src_ref=source,
            dst_ref=target,
            send_sem=send_sem.at[n],
            recv_sem=recv_sem.at[n],
            device_id=sibling,
            device_id_type=pl.DeviceIdType.MESH,
        )
        copy.start()
        sent.append(copy)

    dy = dy_ref[...]
    dyh[0] = dy[:, :half]
    dyh[1] = dy[:, half:]
    mix = mix_ref[...]
    mixed[0] = mix.astype(bf16)
    middle = atoms_ref[...].astype(f32) + matmul(mixed[0], ow[...]) + wide(out_b)
    standard, inverse = standardize(middle)
    gain = wide(gain_ref)
    inner[0] = (standard * gain + wide(shift_ref)).astype(bf16)
    pl.semaphore_wait(barrier, 1)
    send(dyh.at[1 - core], dy_in)
    send(mixed.at[0], mixed.at[1])
    send(inner.at[0], inner.at[1])
    result = middle + wide(outer_b)
    bias = wide(bias_ref)
    grad_inner = jnp.zeros((here, width), f32)
    for b in range(blocks):
        cols = slice(width * b, width * (b + 1))
        pre = matmul(inner[0], iw[:, cols]) + bias[:, cols]
        cdf = 0.5 + 0.5 * lax.erf(pre * (0.5**0.5))
        low = (pre * cdf).astype(bf16)
        act[0, b] = low
        send(act.at[0, b], act.at[1, b])
        slope = cdf + pre * (jnp.exp(-0.5 * pre * pre) * 0.3989422804014327)
        grad = (times_transposed(dy, uw[cols, :]) * slope).astype(bf16)
        dpre[b] = grad
        result = result + matmul(low, uw[cols, :])
        grad_inner = grad_inner + times_transposed(grad, iw[:, cols])
        vec_ref[b : b + 1, :] = jnp.sum(grad.astype(f32), axis=0, keepdims=True)
    for i in range(blocks // 2):
        send(dpre.at[(blocks // 2) * (1 - core) + i], dpre_in.at[i])
    out_ref[...] = result.astype(bf16)
    dy_wide = dy.astype(f32)
    grad_middle = dy_wide + norm_back(grad_inner * gain, standard, inverse)
    dmid_ref[...] = grad_middle
    low = grad_middle.astype(bf16)
    branch[0] = low[:, :half]
    branch[1] = low[:, half:]
    send(branch.at[1 - core], branch_in)
    down = lambda value: jnp.sum(value, axis=0, keepdims=True)
    vec_ref[blocks : blocks + 1, :] = down(low.astype(f32))
    vec_ref[blocks + 1 : blocks + 2, :] = down(grad_inner * standard)
    vec_ref[blocks + 2 : blocks + 3, :] = down(grad_inner)
    vec_ref[blocks + 3 : blocks + 4, :] = down(dy_wide)
    scaled = times_transposed(low, ow[...]).astype(bf16).astype(f32) * rl_ref[...]
    nm_ref[...] = (-scaled * mix).astype(bf16)
    scaled = scaled.astype(bf16)
    dm_ref[...] = scaled
    for s in range(slots):
        dmt_ref[s] = scaled[rows * s : rows * (s + 1)].astype(f32).T.astype(bf16)

    for copy in sent:
        copy.wait()
    tall, short = blocks * width // parts, width // parts
    dy_own = dyh[core]
    for b in range(blocks):
        grads[width * b : width * (b + 1), :] = outer_sum(act[0, b], dy_own) + outer_sum(act[1, b], dy_in[...])
    base = blocks * width
    for i in range(blocks // 2):
        grad = outer_sum(inner[0], dpre[(blocks // 2) * core + i]) + outer_sum(inner[1], dpre_in[i])
        for k in range(2):
            grads[base + width * (2 * i + k) : base + width * (2 * i + k + 1), :] = grad[:, half * k : half * (k + 1)]
    last = base + width * blocks
    grads[last:, :] = outer_sum(mixed[0], branch[core]) + outer_sum(mixed[1], branch_in[...])

    def at(start, n, h):
        return grads[pl.ds(pl.multiple_of(start, 8), n), pl.ds(pl.multiple_of(h * 128, 128), 128)]

    start = {"outer": (0, tall), "inner": (base, short), "out": (last, short)}
    step = {"outer": short, "inner": width, "out": 0}
    for p in range(parts):
        j = xor(dp, p, bits)
        for r in range(2):
            h = other_bit(y, 0, r)
            for n, (opening, parts_of) in enumerate(PIECES):
                if opening == "y":
                    gone, q = r, p
                elif opening == "d0":
                    gone, q = p & 1, 2 * (p >> 1) + r
                else:
                    gone, q = (p >> 1) & 1, 2 * ((p >> 2) * 2 + (p & 1)) + r
                ref = pieces[2 * n + gone]
                for i, (kind, k) in enumerate(parts_of):
                    first, per = start[kind]
                    ref[q, short * i : short * (i + 1)] = at(first + step[kind] * k + per * j, short, h).astype(ref.dtype)


def middle(parts, mix, rl, atoms, dy, vectors, out_w, inner_w, outer_w, slots):
    here, width = atoms.shape
    hidden = inner_w.shape[1]
    blocks, half, rows = hidden // width, width // 2, here // slots
    tall, short = hidden // parts, width // parts
    assert hidden == 4 * width
    vm = pl.BlockSpec(memory_space=pltpu.VMEM)
    like = jax.ShapeDtypeStruct
    out_shape = [
        like((here, width), bf16),
        *(like((parts, len(blocks_of) * short, 128), kind) for _, blocks_of in PIECES for kind in (f32, bf16)),
        like((here, width), bf16),
        like((here, width), bf16),
        like((slots, width, rows), bf16),
        like((here, width), f32),
        like((blocks + 4, width), f32),
    ]
    transfers = 3 + blocks + blocks // 2 + 1
    return pl.pallas_call(
        functools.partial(middle_kernel, parts),
        in_specs=[vm] * 12,
        out_specs=[vm] * len(out_shape),
        out_shape=out_shape,
        scratch_shapes=[
            pltpu.VMEM((2, blocks, here, width), bf16),
            pltpu.VMEM((blocks, here, width), bf16),
            pltpu.VMEM((blocks // 2, here, width), bf16),
            pltpu.VMEM((2, here, width), bf16),
            pltpu.VMEM((2, here, width), bf16),
            pltpu.VMEM((2, here, half), bf16),
            pltpu.VMEM((here, half), bf16),
            pltpu.VMEM((2, here, half), bf16),
            pltpu.VMEM((here, half), bf16),
            pltpu.VMEM((2 * hidden + width, half), f32),
            pltpu.SemaphoreType.DMA((transfers,)),
            pltpu.SemaphoreType.DMA((transfers,)),
        ],
        name="middle",
        cost_estimate=pl.CostEstimate(
            flops=12 * here * width * hidden, transcendentals=2 * here * hidden, bytes_accessed=12 << 20
        ),
        compiler_params=pltpu.CompilerParams(
            vmem_limit_bytes=20 << 20, collective_id=1, has_side_effects=True
        ),
    )(
        mix, rl, atoms, dy, *vectors, out_w, inner_w, outer_w,
    )


class Part:
    def __init__(self, names, order, rows, dtype=bf16, opening=None):
        self.opening = opening
        self.names, self.order, self.rows, self.dtype = names, order, rows, dtype
        self.steps, left = [], list(names)
        for name in order:
            others = [n for n in left if n != name]
            spots = []
            for q in range(1 << len(others)):
                base = sum(
                    self.stride(n) for i, n in enumerate(others) if (q >> (len(others) - 1 - i)) & 1
                )
                spots.append((base, base + self.stride(name)))
            self.steps.append((name, spots))
            left = others

    def stride(self, name):
        return 1 << (len(self.names) - 1 - self.names.index(name))

    def scratch(self):
        shapes = [pltpu.VMEM((1 << len(self.names), self.rows, 128), f32)]
        if self.opening:
            shapes.append(pltpu.VMEM((1 << len(self.names), self.rows, 128), self.dtype))
        for _, spots in self.steps:
            shapes += [pltpu.VMEM((len(spots), self.rows, 128), self.dtype)] * 2
        n = len(self.steps) + 1
        return shapes + [pltpu.SemaphoreType.DMA((n,)), pltpu.SemaphoreType.DMA((n,))]

    def bind(self, refs, partner):
        self.state, refs = refs[0], refs[1:]
        if self.opening:
            self.first, refs = refs[0], refs[1:]
        self.sends, self.recvs = refs[0:-2:2], refs[1:-2:2]
        self.send_sem, self.recv_sem, self.partner = refs[-2], refs[-1], partner

    def open(self, send):
        n = len(self.steps)
        self.copy = remote(send, self.first, self.send_sem.at[n], self.recv_sem.at[n], self.partner(self.opening))

    def opened(self, keep):
        self.copy.wait()
        self.state[...] = keep[...] + self.first[...].astype(f32)

    def go(self, n):
        name, spots = self.steps[n]
        for q, (_, far) in enumerate(spots):
            self.sends[n][q] = self.state[far].astype(self.dtype)
        self.copy = remote(
            self.sends[n], self.recvs[n], self.send_sem.at[n], self.recv_sem.at[n], self.partner(name)
        )

    def come(self, n):
        self.copy.wait()
        for q, (near, _) in enumerate(self.steps[n][1]):
            self.state[near] = self.state[near] + self.recvs[n][q].astype(f32)

    def share(self, ref):
        ref[...] = self.state[0].astype(ref.dtype)


def make_parts(parts, width, hidden):
    bits = ["d%d" % b for b in range(parts.bit_length() - 1)]
    high = bits[::-1]
    short = width // parts
    without = lambda name: [n for n in high if n != name]
    kinds = {
        "d0": (without("d0") + ["y"], ["y", "d1"]),
        "y": (high, ["d1", "d0"]),
        "d1": (without("d1") + ["y"], ["d0", "y"]),
    }
    early = [
        Part(kinds[opening][0], kinds[opening][1] + bits[2:], len(blocks) * short, opening=opening)
        for opening, blocks in PIECES
    ]
    q = Part(high + ["y"], ["d0", "y", "d1"] + bits[2:], short)
    k = Part(high + ["y"], ["y", "d1", "d0"] + bits[2:], short)
    v = Part(high + ["y"], ["d1", "d0", "y"] + bits[2:], short)
    s = Part(high + ["y"], ["d1", "d0", "y"] + bits[2:], 16, f32)
    return early, [q, k, v, s]


def back_kernel(parts, scale, hidden, *refs):
    (
        qt, dm, dmt, nm, k_ref, vt, e_ref, cot, atoms, dmid, gain_ref, shift_ref, vec_ref,
        *refs,
    ) = refs
    made, refs = refs[: 2 * len(PIECES)], refs[2 * len(PIECES) :]
    (
        query_w, key_w, value_w,
        pg, out_ref, total,
        dkt, dvt, dq, qw, kw, vw,
        dk_in, dv_in, dqh, dqh_in, vec_own, vec_in, standard, normed, partial, beside_send, beside_recv,
        across_send, across_recv, grads, vec_all, load_sem, send_sem, recv_sem,
        *refs,
    ) = refs
    slots, width, full = dkt.shape
    rows, half = dq.shape[1], width // 2
    bits = parts.bit_length() - 1
    short, tall = width // parts, hidden // parts
    row, dp = lax.axis_index("rows"), lax.axis_index("dp")
    core, y = row % 2, row // 2
    beside, across = (dp, row + 1 - 2 * core), (dp, row + 2 - 4 * y)

    def partner(name):
        if name == "y":
            return across
        b = int(name[1:])
        return (xor(dp, 1 << b, bits), row)

    early, late = make_parts(parts, width, hidden)
    for piece in early + late:
        n = len(piece.scratch())
        piece.bind(refs[:n], partner)
        refs = refs[n:]
    one, two = early[:3], early[3:]
    steps, late_steps = len(early[0].steps), len(late[0].steps)

    def opened(group):
        for piece in group:
            piece.opened(made[2 * early.index(piece)])
            piece.go(0)

    def advance(group, n):
        for piece in group:
            piece.come(n)
            if n + 1 < len(piece.steps):
                piece.go(n + 1)

    loads = [
        pltpu.make_async_copy(hbm, vmem, load_sem.at[i])
        for i, (hbm, vmem) in enumerate(((query_w, qw), (key_w, kw), (value_w, vw)))
    ]
    for copy in loads:
        copy.start()
    corner = (dp, 3 - row)
    meet([beside, across, corner] + [partner("d%d" % b) for b in range(bits)])
    for n, piece in enumerate(early):
        piece.open(made[2 * n + 1])

    sent = 0

    def send(source, target, device):
        nonlocal sent
        sent += 1
        return remote(source, target, send_sem.at[sent - 1], recv_sem.at[sent - 1], device)

    other = pl.ds(pl.multiple_of((1 - core) * half, half), half)
    mine = pl.ds(pl.multiple_of(core * half, half), half)
    gain, shift = wide(gain_ref), wide(shift_ref)
    down = lambda value: jnp.sum(value, axis=0, keepdims=True)
    gain_grad = shift_grad = value_bias = 0.0
    send_on, to_sibling = [], []
    for s in range(slots):
        def block(b, carry):
            attention_backward(s, b, qt, dm, dmt, nm, k_ref, vt, e_ref, cot, pg, dq, dkt, dvt)
            return carry

        lax.fori_loop(0, width // 128, block, 0)
        to_sibling.append(send(dkt.at[s, other, :], dk_in.at[s], beside))
        to_sibling.append(send(dvt.at[s, other, :], dv_in.at[s], beside))
        if s == 0:
            for copy in loads:
                copy.wait()
        standard[s] = standardize(atoms[s].astype(f32))[0]
        normed[s] = (standard[s] * gain + shift).astype(bf16)
        dv = dvt[s].T
        grad = times_transposed(dkt[s].T, kw[...]) + times_transposed(dv, vw[...])
        value_bias = value_bias + down(dv.astype(f32))
        gain_grad = gain_grad + down(grad * standard[s])
        shift_grad = shift_grad + down(grad)
        for i in range(full // rows):
            partial[xor(row, i, 2), s] = grad[rows * i : rows * (i + 1)]
        beside_send[s, 0] = partial[1, s].astype(bf16)
        beside_send[s, 1] = partial[3, s].astype(bf16)
        send_on.append(send(beside_send.at[s], beside_recv.at[s], beside))
        if s == slots - 2:
            opened(one)
    opened(two)
    dq_low = jnp.concatenate([dq[s] for s in range(slots)], axis=0)
    dqh[0] = dq_low[:, :half]
    dqh[1] = dq_low[:, half:]
    to_sibling.append(send(dqh.at[1 - core], dqh_in, beside))
    own = pl.ds(pl.multiple_of(row * rows, rows), rows)
    next_to = pl.ds(pl.multiple_of((row + 1 - 2 * core) * rows, rows), rows)
    rows_of = lambda ref, which: jnp.concatenate([ref[s, which, :] for s in range(slots)], axis=0)
    query_grad = times_transposed(dq_low, qw[...]) * scale
    vec_own[0:1, :] = gain_grad + down(query_grad * rows_of(standard, own))
    vec_own[1:2, :] = shift_grad + down(query_grad)
    vec_own[2:3, :] = down(dq_low.astype(f32)) * scale
    vec_own[3:4, :] = value_bias
    vec_own[4:12, :] = vec_ref[...]
    vec_own[12:16, :] = jnp.zeros((4, width), f32)
    vec_sent = send(vec_own, vec_in, beside)

    advance(one, 0)
    for s in range(slots):
        send_on[s].wait()
        across_send[s] = (partial[2, s] + beside_recv[s, 1].astype(f32)).astype(bf16)
    over = send(across_send, across_recv, across)

    for copy in to_sibling:
        copy.wait()
    grads[0] = (
        outer_sum(rows_of(normed, own), dqh[core]) + outer_sum(rows_of(normed, next_to), dqh_in[...])
    ) * scale
    key_total = value_total = 0.0
    add = lambda left, right: (left.astype(f32) + right.astype(f32)).astype(bf16)
    for s in range(slots):
        turned = normed[s].T
        key_total = key_total + times_transposed(turned, add(dkt[s, mine, :], dk_in[s]))
        value_total = value_total + times_transposed(turned, add(dvt[s, mine, :], dv_in[s]))
    grads[1] = key_total
    grads[2] = value_total
    vec_sent.wait()
    vec = vec_own[...] + vec_in[...]
    vec_all[...] = jnp.zeros_like(vec_all)
    for j in range(parts):
        vec_all[j, 0:4, :short] = vec[0:4, short * j : short * (j + 1)]
        vec_all[j, 4:8, :short] = vec[8:12, short * j : short * (j + 1)]
        start = tall * j
        vec_all[j, 8:9, :tall] = vec[4 + start // width : 5 + start // width, start % width : start % width + tall]
    for p in range(parts):
        j = xor(dp, p, bits)
        for r in range(2):
            lanes = pl.ds(pl.multiple_of(other_bit(y, 0, r) * 128, 128), 128)
            for i, piece in enumerate(late[:3]):
                piece.state[2 * p + r] = grads[i, pl.ds(pl.multiple_of(j * short, short), short), lanes]
            late[3].state[2 * p + r] = vec_all[j, :, lanes]
    for piece in late:
        piece.go(0)

    advance(two, 0)
    advance(one, 1)
    advance(late, 0)
    advance(two, 1)
    over.wait()
    for s in range(slots):
        some = slice(rows * s, rows * (s + 1))
        grad = partial[0, s] + beside_recv[s, 0].astype(f32) + across_recv[s].astype(f32) + query_grad[some]
        stand, inverse = standardize(atoms[s, own, :].astype(f32))
        out_ref[some, :] = (dmid[some, :] + norm_back(grad * gain, stand, inverse)).astype(bf16)
    for n in range(2, steps):
        advance(one, n)
        advance(late, n - 1)
        advance(two, n)

    def place(group, at):
        for piece in group:
            piece.share(total.at[row, at : at + piece.rows])
            at += piece.rows
        return at

    cut = place(early, 0)
    mine, theirs = total.at[row, :cut], total.at[across[1], :cut]
    arrive = send(mine, mine, across)
    ends = [send(mine, mine, beside)]
    for n in range(steps - 1, late_steps):
        advance(late, n)
    place(late, cut)
    rest = total.at[row, cut:]
    ends += [send(rest, rest, device) for device in (across, corner, beside)]
    arrive.wait()
    ends.append(send(theirs, theirs, beside))
    for copy in ends:
        copy.wait()


def back(parts, scale, qt, dm, dmt, nm, k, vt, weights, cot, atoms, dmid, vectors, vec, pieces, query_w, key_w, value_w):
    slots, width, full = vt.shape
    rows, half = qt.shape[2], width // 2
    here, hidden = slots * rows, width * 4
    vm = pl.BlockSpec(memory_space=pltpu.VMEM)
    far = pl.BlockSpec(memory_space=pltpu.HBM)
    kinds = sum(make_parts(parts, width, hidden), [])
    count = sum(piece.rows for piece in kinds)
    transfers = 3 * slots + 9
    scratch = [
        pltpu.VMEM((slots, width, full), bf16),
        pltpu.VMEM((slots, width, full), bf16),
        pltpu.VMEM((slots, rows, width), bf16),
        pltpu.VMEM((width, width), bf16),
        pltpu.VMEM((width, width), bf16),
        pltpu.VMEM((width, width), bf16),
        pltpu.VMEM((slots, half, full), bf16),
        pltpu.VMEM((slots, half, full), bf16),
        pltpu.VMEM((2, here, half), bf16),
        pltpu.VMEM((here, half), bf16),
        pltpu.VMEM((16, width), f32),
        pltpu.VMEM((16, width), f32),
        pltpu.VMEM((slots, full, width), f32),
        pltpu.VMEM((slots, full, width), bf16),
        pltpu.VMEM((4, slots, rows, width), f32),
        pltpu.VMEM((slots, 2, rows, width), bf16),
        pltpu.VMEM((slots, 2, rows, width), bf16),
        pltpu.VMEM((slots, rows, width), bf16),
        pltpu.VMEM((slots, rows, width), bf16),
        pltpu.VMEM((3, width, half), f32),
        pltpu.VMEM((parts, 16, half), f32),
        pltpu.SemaphoreType.DMA((3,)),
        pltpu.SemaphoreType.DMA((transfers,)),
        pltpu.SemaphoreType.DMA((transfers,)),
    ]
    for piece in kinds:
        scratch += piece.scratch()
    return pl.pallas_call(
        functools.partial(back_kernel, parts, scale, hidden),
        in_specs=[vm] * (13 + 2 * len(PIECES)) + [far] * 3,
        out_specs=[vm] * 3,
        out_shape=[
            jax.ShapeDtypeStruct(cot.shape, bf16),
            jax.ShapeDtypeStruct((here, width), bf16),
            jax.ShapeDtypeStruct((4, count, 128), bf16),
        ],
        scratch_shapes=scratch,
        name="back",
        cost_estimate=pl.CostEstimate(
            flops=40 * slots * full * width * width, transcendentals=0, bytes_accessed=32 << 20
        ),
        compiler_params=pltpu.CompilerParams(vmem_limit_bytes=VMEM_BACK, collective_id=2, has_side_effects=True),
    )(
        qt, dm, dmt, nm, k, vt, weights, cot, atoms, dmid, *vectors, vec, *pieces,
        *(pltpu.with_memory_space_constraint(array, pltpu.HBM) for array in (query_w, key_w, value_w)),
    )


def last_kernel(total, grad_ref, made_ref, pair, *refs):
    count = 18
    outs, refs = refs[:count], refs[count:]
    (grad_out, made_out, *_, pair_out), (uw, ow, iw, qw, kw, vw), small, sem = outs, refs[:6], refs[6:15], refs[15]
    copies = []

    def move(source, target):
        copy = pltpu.make_async_copy(source, target, sem.at[len(copies)])
        copy.start()
        copies.append(copy)

    move(pair, pair_out)
    move(grad_ref, grad_out)
    move(made_ref, made_out)
    short = ow.shape[0]
    blocks = iw.shape[1] // 2 // 256
    spots = [spot for _, of in PIECES for spot in of] + [("query", 0), ("key", 0), ("value", 0)]
    refs = {"outer": uw, "inner": iw, "out": ow, "query": qw, "key": kw, "value": vw}
    at = 0
    for name, k in spots:
        ref = refs[name]
        first = short * k if name == "outer" else 0
        for r in range(4):
            core, y = r % 2, r // 2
            col = 256 * (core * blocks + k if name == "inner" else core) + 128 * y
            ref[first : first + short, col : col + 128] = total[r, at : at + short, :].astype(f32)
        at += short
    for ref, out in zip((uw, ow, iw, qw, kw, vw), outs[2:8]):
        move(ref, out)
    for i, ref in enumerate(small[:8]):
        ref[...] = total[0, at : at + 16, :].astype(f32)[i : i + 1, :short]
    ib = small[8]
    for y in range(2):
        n = min(128, ib.shape[1] - 128 * y)
        if n > 0:
            ib[:, 128 * y : 128 * y + n] = total[2 * y, at : at + 16, :].astype(f32)[8:9, :n]
    for ref, out in zip(small, outs[8:17]):
        move(ref, out)
    for copy in copies:
        copy.wait()


def last(parts, total, grad, made, pair, hidden):
    here, width = grad.shape
    short, tall = width // parts, hidden // parts
    vm = pl.BlockSpec(memory_space=pltpu.VMEM)
    hbm = pl.BlockSpec(memory_space=pl.ANY)
    shapes = [(tall, width), (short, width), (short, hidden)] + [(short, width)] * 3
    shapes += [(1, short)] * 8 + [(1, tall)]
    out_shape = [jax.ShapeDtypeStruct(grad.shape, bf16)] * 2
    out_shape += [jax.ShapeDtypeStruct(shape, f32) for shape in shapes]
    out_shape.append(jax.ShapeDtypeStruct(pair.shape, bf16))
    return pl.pallas_call(
        last_kernel,
        in_specs=[vm] + [hbm] * 3,
        out_specs=[hbm] * len(out_shape),
        out_shape=out_shape,
        scratch_shapes=[pltpu.VMEM(shape, f32) for shape in shapes] + [pltpu.SemaphoreType.DMA((len(out_shape),))],
        name="last",
        compiler_params=pltpu.CompilerParams(vmem_limit_bytes=16 << 20),
    )(total, grad, made, pair)


def local(
    parts,
    group,
    atoms,
    pair_bias,
    mol_counts,
    attn_gain,
    attn_shift,
    query_weight,
    query_bias,
    key_weight,
    value_weight,
    value_bias,
    out_weight,
    out_bias,
    ffn_gain,
    ffn_shift,
    inner_weight,
    inner_bias,
    outer_weight,
    outer_bias,
    atoms_cotangent,
    pair_cotangent,
):
    slots, part_rows, width = atoms.shape
    heads = pair_bias.shape[1]
    full = pair_bias.shape[3]
    scale = (width // heads) ** (-0.5)
    here = slots * part_rows
    hidden = inner_weight.shape[1]
    flat = lambda array: array.reshape(here, width)
    all_atoms, mask, q, qt, k, kt, v, vt = front(
        scale, full, atoms, mol_counts, (attn_gain, attn_shift, query_bias, value_bias), query_weight, key_weight, value_weight
    )
    pair_out, weights, mixed, inverse_sum = attention_forward(q, kt, v, pair_bias, mask)
    atoms_out, *pieces, scaled, centre, scaled_turned, grad_middle, vec = middle(
        parts,
        flat(mixed),
        flat(inverse_sum),
        flat(atoms),
        flat(atoms_cotangent),
        (out_bias, ffn_gain, ffn_shift, outer_bias, inner_bias),
        out_weight,
        inner_weight,
        outer_weight,
        slots,
    )
    pair_grad, grad, total = back(
        parts,
        scale,
        qt,
        scaled.reshape(q.shape),
        scaled_turned,
        centre.reshape(q.shape),
        k,
        vt,
        weights,
        pair_cotangent,
        all_atoms,
        grad_middle,
        (attn_gain, attn_shift),
        vec,
        pieces,
        query_weight,
        key_weight,
        value_weight,
    )
    grad, made, uw, ow, iw, qw, kw, vw, again, ashift, qb, vb, ob, fgain, fshift, ub, ib, pair_grad = last(
        parts, total, grad, atoms_out, pair_grad, hidden
    )
    line = lambda array: array.reshape(-1)
    return (
        made.reshape(atoms.shape),
        pair_out,
        grad.reshape(atoms.shape),
        pair_grad,
        line(again),
        line(ashift),
        qw,
        line(qb),
        kw,
        vw,
        line(vb),
        ow,
        line(ob),
        line(fgain),
        line(fshift),
        iw,
        line(ib),
        uw,
        line(ub),
    )


def solution(mesh):
    one, two = P("dp"), P("dp", None)
    atoms_spec, pair_spec = P("dp", "rows", None), P("dp", None, "rows", None)
    in_specs = (atoms_spec, pair_spec, two) + (P(),) * 15 + (atoms_spec, pair_spec)
    out_specs = (
        (atoms_spec, pair_spec, atoms_spec, pair_spec, one, one, two, one, two, two, one, two)
        + (one, one, one, two, one, two, one)
    )
    run = functools.partial(local, mesh.shape["dp"], mesh.shape["rows"])
    return jax.shard_map(run, mesh=mesh, in_specs=in_specs, out_specs=out_specs, check_vma=False)
```

```python
import functools

import jax
import jax.numpy as jnp
from jax import lax
from jax.experimental import pallas as pl
from jax.experimental.pallas import tpu as pltpu
from jax.sharding import PartitionSpec as P

f32, bf16 = jnp.float32, jnp.bfloat16
BIG = 1e9
HPL = 16
CHUNK = 8
STEP = 64
VMEM_PAIR = 22 << 20
VMEM_BACK = 26 << 20
MESH = pl.DeviceIdType.MESH
PIECES = (
    ("d0", (("outer", 0), ("outer", 1))),
    ("y", (("outer", 2),)),
    ("d1", (("outer", 3),)),
    ("d0", (("inner", 0),)),
    ("y", (("inner", 1), ("inner", 2))),
    ("d1", (("inner", 3), ("out", 0))),
)


def standardize(value):
    centred = value - jnp.mean(value, axis=-1, keepdims=True)
    inverse = lax.rsqrt(jnp.mean(centred * centred, axis=-1, keepdims=True) + 1e-05)
    return (centred * inverse, inverse)


def norm_back(grad_normed, standard, inverse):
    return inverse * (
        grad_normed
        - jnp.mean(grad_normed, axis=-1, keepdims=True)
        - standard * jnp.mean(grad_normed * standard, axis=-1, keepdims=True)
    )


def matmul(left, right):
    return jnp.dot(left, right, preferred_element_type=f32)


def times_transposed(left, right):
    return lax.dot_general(left, right, (((1,), (1,)), ((), ())), preferred_element_type=f32)


def outer_sum(left, right):
    return lax.dot_general(left, right, (((0,), (0,)), ((), ())), preferred_element_type=f32)


def other_bit(index, bit, const):
    own = (index // (1 << bit)) % 2
    return 1 - own if (const >> bit) & 1 else own


def xor(index, const, bits):
    return sum(other_bit(index, b, const) * (1 << b) for b in range(bits))


def remote(source, target, send_sem, recv_sem, device):
    copy = pltpu.make_async_remote_copy(
        src_ref=source, dst_ref=target, send_sem=send_sem, recv_sem=recv_sem, device_id=device, device_id_type=MESH
    )
    copy.start()
    return copy


def meet(devices):
    barrier = pltpu.get_barrier_semaphore()
    for device in devices:
        pl.semaphore_signal(barrier, inc=1, device_id=device, device_id_type=MESH)
    pl.semaphore_wait(barrier, len(devices))


def wide(ref):
    return ref[...].astype(f32).reshape(1, -1)


def front_kernel(
    scale,
    atoms_ref,
    counts_ref,
    gain_ref,
    shift_ref,
    query_b,
    value_b,
    query_w,
    key_w,
    value_w,
    all_ref,
    mask_ref,
    q_ref,
    qt_ref,
    k_ref,
    kt_ref,
    v_ref,
    vt_ref,
    qw,
    kw,
    vw,
    load_sem,
    send_sem,
    recv_sem,
):
    slots, rows, width = atoms_ref.shape
    full = mask_ref.shape[2]
    row, dp = lax.axis_index("rows"), lax.axis_index("dp")
    core, y = row % 2, row // 2
    beside, across = row + 1 - 2 * core, row + 2 - 4 * y
    loads = [
        pltpu.make_async_copy(hbm, vmem, load_sem.at[i])
        for i, (hbm, vmem) in enumerate(((query_w, qw), (key_w, kw), (value_w, vw)))
    ]
    for copy in loads:
        copy.start()
    meet([(dp, beside), (dp, across)])
    at = lambda r: pl.ds(pl.multiple_of(r * rows, rows), rows)
    here = lambda s: all_ref.at[s, at(row), :]
    there = lambda s: all_ref.at[s, at(across), :]
    far = [remote(atoms_ref.at[s], here(s), send_sem.at[s], recv_sem.at[s], (dp, across)) for s in range(slots)]
    near = [
        remote(atoms_ref.at[s], here(s), send_sem.at[slots + s], recv_sem.at[slots + s], (dp, beside))
        for s in range(slots)
    ]
    gain, shift = wide(gain_ref), wide(shift_ref)
    bias = wide(value_b)
    for s in range(slots):
        all_ref[s, at(row), :] = atoms_ref[s]
    own = atoms_ref[...].reshape(slots * rows, width).astype(f32)
    normed = (standardize(own)[0] * gain + shift).astype(bf16)
    loads[0].wait()
    queries = ((matmul(normed, qw[...]) + wide(query_b)) * scale).astype(bf16)
    for s in range(slots):
        part = queries[rows * s : rows * (s + 1)]
        q_ref[s] = part
        qt_ref[s] = part.T
    loads[1].wait()
    loads[2].wait()

    def project(s, chip):
        some = pl.ds(pl.multiple_of(chip * 2 * rows, 2 * rows), 2 * rows)
        normed = (standardize(all_ref[s, some, :].astype(f32))[0] * gain + shift).astype(bf16)
        keys = matmul(normed, kw[...]).astype(bf16)
        k_ref[s, some, :] = keys
        kt_ref[s, :, some] = keys.T
        values = (matmul(normed, vw[...]) + bias).astype(bf16)
        v_ref[s, some, :] = values
        vt_ref[s, :, some] = values.T

    def masks(s):
        ends = [counts_ref[s, 0]]
        for m in range(1, counts_ref.shape[1]):
            ends.append(ends[-1] + counts_ref[s, m])
        keys_at = lax.broadcasted_iota(jnp.int32, (1, full), 1)
        queries_at = lax.broadcasted_iota(jnp.int32, (rows, 1), 0) + row * rows
        count = lambda at: sum((end <= at).astype(jnp.int32) for end in ends)
        mask_ref[s] = jnp.where(count(keys_at) == count(queries_at), 0.0, -BIG)

    forward = []

    def pass_on(s):
        far[s].wait()
        n = 2 * slots + s
        forward.append(remote(there(s), there(s), send_sem.at[n], recv_sem.at[n], (dp, beside)))

    for s in range(slots):
        if s == slots - 1:
            pass_on(0)
        near[s].wait()
        project(s, y)
    for s in range(slots):
        masks(s)
    for s in range(1, slots):
        pass_on(s)
        forward[s - 1].wait()
        project(s - 1, 1 - y)
    forward[-1].wait()
    project(slots - 1, 1 - y)


def front(scale, full, atoms, counts, vectors, query_w, key_w, value_w):
    slots, rows, width = atoms.shape
    vm = pl.BlockSpec(memory_space=pltpu.VMEM)
    hbm = pl.BlockSpec(memory_space=pltpu.HBM)
    like = lambda *shape: jax.ShapeDtypeStruct(shape, bf16)
    out_shape = [
        like(slots, full, width),
        jax.ShapeDtypeStruct((slots, rows, full), f32),
        like(slots, rows, width),
        like(slots, width, rows),
        like(slots, full, width),
        like(slots, width, full),
        like(slots, full, width),
        like(slots, width, full),
    ]
    return pl.pallas_call(
        functools.partial(front_kernel, scale),
        in_specs=[vm, pl.BlockSpec(memory_space=pltpu.SMEM)] + [vm] * 4 + [hbm] * 3,
        out_specs=[vm] * len(out_shape),
        out_shape=out_shape,
        scratch_shapes=[pltpu.VMEM((width, width), bf16)] * 3
        + [
            pltpu.SemaphoreType.DMA((3,)),
            pltpu.SemaphoreType.DMA((3 * slots,)),
            pltpu.SemaphoreType.DMA((3 * slots,)),
        ],
        name="front",
        cost_estimate=pl.CostEstimate(
            flops=48 * slots * full * width * width, transcendentals=0, bytes_accessed=32 << 20
        ),
        compiler_params=pltpu.CompilerParams(vmem_limit_bytes=18 << 20, collective_id=0, has_side_effects=True),
    )(*(pltpu.with_memory_space_constraint(array, pltpu.HBM) for array in (atoms, counts, *vectors, query_w, key_w, value_w)))


def forward_kernel(q_ref, kt_ref, v_ref, bias_ref, mask_ref, out_ref, e_ref, mix_ref, rl_ref):
    _, heads, rows, full = bias_ref.shape
    lane_head = lax.broadcasted_iota(jnp.int32, (rows, 128), 1) // 8
    mask = mask_ref[0]
    ones = jnp.ones((full, 128), bf16)
    for b in range(heads // HPL):
        cols = slice(128 * b, 128 * b + 128)
        q = q_ref[0, :, cols].astype(f32)
        kt = kt_ref[0, cols, :]
        v = jnp.concatenate([v_ref[0, :, cols], ones], axis=1)
        mixed = jnp.zeros((rows, 128), f32)
        total = jnp.zeros((rows, 128), f32)
        for c in range(HPL // CHUNK):
            own = [lane_head == CHUNK * c + i for i in range(CHUNK)]
            left = jnp.concatenate([jnp.where(o, q, 0.0).astype(bf16) for o in own], axis=0)
            scores = matmul(left, kt).reshape(CHUNK, rows, full)
            hs = slice(HPL * b + CHUNK * c, HPL * b + CHUNK * (c + 1))
            scores = scores + bias_ref[0, hs].astype(f32)
            out_ref[0, hs] = scores.astype(bf16)
            scores = scores + mask[None]
            highest = jnp.max(scores, axis=-1, keepdims=True)
            e = jnp.exp(scores - highest).astype(bf16)
            e_ref[0, hs] = e
            sums = matmul(e.reshape(CHUNK * rows, full), v)
            for i, o in enumerate(own):
                mixed = jnp.where(o, sums[rows * i : rows * (i + 1), :128], mixed)
                total = jnp.where(o, sums[rows * i : rows * (i + 1), 128:], total)
        inverse = 1.0 / total
        mix_ref[0, :, cols] = mixed * inverse
        rl_ref[0, :, cols] = inverse


def attention_forward(q, kt, v, bias, mask):
    slots, heads, rows, full = bias.shape
    step = min(STEP, heads)
    width = step * 8
    natural = lambda n: pl.BlockSpec((1, n, width), lambda s, h: (s, 0, h))
    pair = pl.BlockSpec((1, step, rows, full), lambda s, h: (s, h, 0, 0))
    return pl.pallas_call(
        forward_kernel,
        grid=(slots, heads // step),
        in_specs=[
            natural(rows),
            pl.BlockSpec((1, width, full), lambda s, h: (s, h, 0)),
            natural(full),
            pair,
            pl.BlockSpec((1, rows, full), lambda s, h: (s, 0, 0)),
        ],
        out_specs=[pair, pair, natural(rows), natural(rows)],
        out_shape=[
            jax.ShapeDtypeStruct(bias.shape, bf16),
            jax.ShapeDtypeStruct(bias.shape, bf16),
            jax.ShapeDtypeStruct(q.shape, f32),
            jax.ShapeDtypeStruct(q.shape, f32),
        ],
        name="attention_forward",
        cost_estimate=pl.CostEstimate(
            flops=2 * bias.size * 512, transcendentals=bias.size, bytes_accessed=bias.size * 6
        ),
        compiler_params=pltpu.CompilerParams(vmem_limit_bytes=VMEM_PAIR),
    )(q, kt, v, bias, mask)


def attention_backward(s, b, qt_ref, dm_ref, dmt_ref, nm_ref, k_ref, vt_ref, e_ref, cot_ref, pg_ref, dq_ref, dkt_ref, dvt_ref):
    _, heads, rows, full = cot_ref.shape
    lane_head = lax.broadcasted_iota(jnp.int32, (rows, 128), 1) // 8
    shape = (8 * CHUNK, CHUNK * rows)
    same = lax.broadcasted_iota(jnp.int32, shape, 0) // 8 == lax.broadcasted_iota(jnp.int32, shape, 1) // rows
    ones = jnp.ones((128, full), bf16)
    cols = pl.ds(pl.multiple_of(128 * b, 128), 128)
    dm = dm_ref[s, :, cols].astype(f32)
    nm = nm_ref[s, :, cols].astype(f32)
    vt = jnp.concatenate([vt_ref[s, cols, :], ones], axis=0)
    k = k_ref[s, :, cols]
    dq = jnp.zeros((rows, 128), f32)
    for c in range(HPL // CHUNK):
        own = [lane_head == CHUNK * c + i for i in range(CHUNK)]
        left = jnp.concatenate(
            [
                jnp.concatenate([jnp.where(o, dm, 0.0), jnp.where(o, nm, 0.0)], axis=1).astype(bf16)
                for o in own
            ],
            axis=0,
        )
        centred = matmul(left, vt).reshape(CHUNK, rows, full)
        hs = pl.ds(HPL * b + CHUNK * c, CHUNK)
        e = e_ref[s, hs]
        grad = (e.astype(f32) * centred + cot_ref[s, hs].astype(f32)).astype(bf16)
        pg_ref[s, hs] = grad
        grad = grad.reshape(CHUNK * rows, full)
        sums = matmul(grad, k)
        for i, o in enumerate(own):
            dq = jnp.where(o, sums[rows * i : rows * (i + 1)], dq)
        rs = pl.ds(pl.multiple_of(128 * b + 8 * CHUNK * c, 8 * CHUNK), 8 * CHUNK)
        spread = lambda ref: jnp.where(
            same, jnp.concatenate([ref[s, rs, :].astype(f32)] * CHUNK, axis=1), 0.0
        ).astype(bf16)
        dkt_ref[s, rs, :] = matmul(spread(qt_ref), grad).astype(bf16)
        dvt_ref[s, rs, :] = matmul(spread(dmt_ref), e.reshape(CHUNK * rows, full)).astype(bf16)
    dq_ref[s, :, cols] = dq.astype(bf16)


def middle_kernel(
    parts,
    mix_ref,
    rl_ref,
    atoms_ref,
    dy_ref,
    out_b,
    gain_ref,
    shift_ref,
    outer_b,
    bias_ref,
    ow,
    iw,
    uw,
    out_ref,
    *refs,
):
    pieces, refs = refs[: 2 * len(PIECES)], refs[2 * len(PIECES) :]
    (
    dm_ref,
    nm_ref,
    dmt_ref,
    dmid_ref,
    vec_ref,
    act,
    dpre,
    dpre_in,
    inner,
    mixed,
    branch,
    branch_in,
    dyh,
    dy_in,
    grads,
    send_sem,
    recv_sem,
    ) = refs
    here, width = atoms_ref.shape
    half = width // 2
    blocks = act.shape[1]
    slots, _, rows = dmt_ref.shape
    bits = parts.bit_length() - 1
    row = lax.axis_index("rows")
    dp = lax.axis_index("dp")
    core = row % 2
    y = row // 2
    sibling = (dp, row + 1 - 2 * core)

    barrier = pltpu.get_barrier_semaphore()
    pl.semaphore_signal(barrier, inc=1, device_id=sibling, device_id_type=pl.DeviceIdType.MESH)
    sent = []

    def send(source, target):
        n = len(sent)
        copy = pltpu.make_async_remote_copy(
            src_ref=source,
            dst_ref=target,
            send_sem=send_sem.at[n],
            recv_sem=recv_sem.at[n],
            device_id=sibling,
            device_id_type=pl.DeviceIdType.MESH,
        )
        copy.start()
        sent.append(copy)

    dy = dy_ref[...]
    dyh[0] = dy[:, :half]
    dyh[1] = dy[:, half:]
    mix = mix_ref[...]
    mixed[0] = mix.astype(bf16)
    middle = atoms_ref[...].astype(f32) + matmul(mixed[0], ow[...]) + wide(out_b)
    standard, inverse = standardize(middle)
    gain = wide(gain_ref)
    inner[0] = (standard * gain + wide(shift_ref)).astype(bf16)
    pl.semaphore_wait(barrier, 1)
    send(dyh.at[1 - core], dy_in)
    send(mixed.at[0], mixed.at[1])
    send(inner.at[0], inner.at[1])
    result = middle + wide(outer_b)
    bias = wide(bias_ref)
    grad_inner = jnp.zeros((here, width), f32)
    for b in range(blocks):
        cols = slice(width * b, width * (b + 1))
        pre = matmul(inner[0], iw[:, cols]) + bias[:, cols]
        cdf = 0.5 + 0.5 * lax.erf(pre * (0.5**0.5))
        low = (pre * cdf).astype(bf16)
        act[0, b] = low
        send(act.at[0, b], act.at[1, b])
        slope = cdf + pre * (jnp.exp(-0.5 * pre * pre) * 0.3989422804014327)
        grad = (times_transposed(dy, uw[cols, :]) * slope).astype(bf16)
        dpre[b] = grad
        result = result + matmul(low, uw[cols, :])
        grad_inner = grad_inner + times_transposed(grad, iw[:, cols])
        vec_ref[b : b + 1, :] = jnp.sum(grad.astype(f32), axis=0, keepdims=True)
    for i in range(blocks // 2):
        send(dpre.at[(blocks // 2) * (1 - core) + i], dpre_in.at[i])
    out_ref[...] = result.astype(bf16)
    dy_wide = dy.astype(f32)
    grad_middle = dy_wide + norm_back(grad_inner * gain, standard, inverse)
    dmid_ref[...] = grad_middle
    low = grad_middle.astype(bf16)
    branch[0] = low[:, :half]
    branch[1] = low[:, half:]
    send(branch.at[1 - core], branch_in)
    down = lambda value: jnp.sum(value, axis=0, keepdims=True)
    vec_ref[blocks : blocks + 1, :] = down(low.astype(f32))
    vec_ref[blocks + 1 : blocks + 2, :] = down(grad_inner * standard)
    vec_ref[blocks + 2 : blocks + 3, :] = down(grad_inner)
    vec_ref[blocks + 3 : blocks + 4, :] = down(dy_wide)
    scaled = times_transposed(low, ow[...]).astype(bf16).astype(f32) * rl_ref[...]
    nm_ref[...] = (-scaled * mix).astype(bf16)
    scaled = scaled.astype(bf16)
    dm_ref[...] = scaled
    for s in range(slots):
        dmt_ref[s] = scaled[rows * s : rows * (s + 1)].astype(f32).T.astype(bf16)

    for copy in sent:
        copy.wait()
    tall, short = blocks * width // parts, width // parts
    dy_own = dyh[core]
    for b in range(blocks):
        grads[width * b : width * (b + 1), :] = outer_sum(act[0, b], dy_own) + outer_sum(act[1, b], dy_in[...])
    base = blocks * width
    for i in range(blocks // 2):
        grad = outer_sum(inner[0], dpre[(blocks // 2) * core + i]) + outer_sum(inner[1], dpre_in[i])
        for k in range(2):
            grads[base + width * (2 * i + k) : base + width * (2 * i + k + 1), :] = grad[:, half * k : half * (k + 1)]
    last = base + width * blocks
    grads[last:, :] = outer_sum(mixed[0], branch[core]) + outer_sum(mixed[1], branch_in[...])

    def at(start, n, h):
        return grads[pl.ds(pl.multiple_of(start, 8), n), pl.ds(pl.multiple_of(h * 128, 128), 128)]

    start = {"outer": (0, tall), "inner": (base, short), "out": (last, short)}
    step = {"outer": short, "inner": width, "out": 0}
    for p in range(parts):
        j = xor(dp, p, bits)
        for r in range(2):
            h = other_bit(y, 0, r)
            for n, (opening, parts_of) in enumerate(PIECES):
                if opening == "y":
                    gone, q = r, p
                elif opening == "d0":
                    gone, q = p & 1, 2 * (p >> 1) + r
                else:
                    gone, q = (p >> 1) & 1, 2 * ((p >> 2) * 2 + (p & 1)) + r
                ref = pieces[2 * n + gone]
                for i, (kind, k) in enumerate(parts_of):
                    first, per = start[kind]
                    ref[q, short * i : short * (i + 1)] = at(first + step[kind] * k + per * j, short, h).astype(ref.dtype)


def middle(parts, mix, rl, atoms, dy, vectors, out_w, inner_w, outer_w, slots):
    here, width = atoms.shape
    hidden = inner_w.shape[1]
    blocks, half, rows = hidden // width, width // 2, here // slots
    tall, short = hidden // parts, width // parts
    assert hidden == 4 * width
    vm = pl.BlockSpec(memory_space=pltpu.VMEM)
    like = jax.ShapeDtypeStruct
    out_shape = [
        like((here, width), bf16),
        *(like((parts, len(blocks_of) * short, 128), kind) for _, blocks_of in PIECES for kind in (f32, bf16)),
        like((here, width), bf16),
        like((here, width), bf16),
        like((slots, width, rows), bf16),
        like((here, width), f32),
        like((blocks + 4, width), f32),
    ]
    transfers = 3 + blocks + blocks // 2 + 1
    return pl.pallas_call(
        functools.partial(middle_kernel, parts),
        in_specs=[vm] * 12,
        out_specs=[vm] * len(out_shape),
        out_shape=out_shape,
        scratch_shapes=[
            pltpu.VMEM((2, blocks, here, width), bf16),
            pltpu.VMEM((blocks, here, width), bf16),
            pltpu.VMEM((blocks // 2, here, width), bf16),
            pltpu.VMEM((2, here, width), bf16),
            pltpu.VMEM((2, here, width), bf16),
            pltpu.VMEM((2, here, half), bf16),
            pltpu.VMEM((here, half), bf16),
            pltpu.VMEM((2, here, half), bf16),
            pltpu.VMEM((here, half), bf16),
            pltpu.VMEM((2 * hidden + width, half), f32),
            pltpu.SemaphoreType.DMA((transfers,)),
            pltpu.SemaphoreType.DMA((transfers,)),
        ],
        name="middle",
        cost_estimate=pl.CostEstimate(
            flops=12 * here * width * hidden, transcendentals=2 * here * hidden, bytes_accessed=12 << 20
        ),
        compiler_params=pltpu.CompilerParams(
            vmem_limit_bytes=20 << 20, collective_id=1, has_side_effects=True
        ),
    )(
        mix, rl, atoms, dy, *vectors, out_w, inner_w, outer_w,
    )


class Part:
    def __init__(self, names, order, rows, dtype=bf16, opening=None):
        self.opening = opening
        self.names, self.order, self.rows, self.dtype = names, order, rows, dtype
        self.steps, left = [], list(names)
        for name in order:
            others = [n for n in left if n != name]
            spots = []
            for q in range(1 << len(others)):
                base = sum(
                    self.stride(n) for i, n in enumerate(others) if (q >> (len(others) - 1 - i)) & 1
                )
                spots.append((base, base + self.stride(name)))
            self.steps.append((name, spots))
            left = others

    def stride(self, name):
        return 1 << (len(self.names) - 1 - self.names.index(name))

    def scratch(self):
        shapes = [pltpu.VMEM((1 << len(self.names), self.rows, 128), f32)]
        if self.opening:
            shapes.append(pltpu.VMEM((1 << len(self.names), self.rows, 128), self.dtype))
        for _, spots in self.steps:
            shapes += [pltpu.VMEM((len(spots), self.rows, 128), self.dtype)] * 2
        n = len(self.steps) + 1
        return shapes + [pltpu.SemaphoreType.DMA((n,)), pltpu.SemaphoreType.DMA((n,))]

    def bind(self, refs, partner):
        self.state, refs = refs[0], refs[1:]
        if self.opening:
            self.first, refs = refs[0], refs[1:]
        self.sends, self.recvs = refs[0:-2:2], refs[1:-2:2]
        self.send_sem, self.recv_sem, self.partner = refs[-2], refs[-1], partner

    def open(self, send):
        n = len(self.steps)
        self.copy = remote(send, self.first, self.send_sem.at[n], self.recv_sem.at[n], self.partner(self.opening))

    def opened(self, keep):
        self.copy.wait()
        self.state[...] = keep[...] + self.first[...].astype(f32)

    def go(self, n):
        name, spots = self.steps[n]
        for q, (_, far) in enumerate(spots):
            self.sends[n][q] = self.state[far].astype(self.dtype)
        self.copy = remote(
            self.sends[n], self.recvs[n], self.send_sem.at[n], self.recv_sem.at[n], self.partner(name)
        )

    def come(self, n):
        self.copy.wait()
        for q, (near, _) in enumerate(self.steps[n][1]):
            self.state[near] = self.state[near] + self.recvs[n][q].astype(f32)

    def share(self, ref):
        ref[...] = self.state[0].astype(ref.dtype)


def make_parts(parts, width, hidden):
    bits = ["d%d" % b for b in range(parts.bit_length() - 1)]
    high = bits[::-1]
    short = width // parts
    without = lambda name: [n for n in high if n != name]
    kinds = {
        "d0": (without("d0") + ["y"], ["y", "d1"]),
        "y": (high, ["d1", "d0"]),
        "d1": (without("d1") + ["y"], ["d0", "y"]),
    }
    early = [
        Part(kinds[opening][0], kinds[opening][1] + bits[2:], len(blocks) * short, opening=opening)
        for opening, blocks in PIECES
    ]
    q = Part(high + ["y"], ["d0", "y", "d1"] + bits[2:], short)
    k = Part(high + ["y"], ["y", "d1", "d0"] + bits[2:], short)
    v = Part(high + ["y"], ["d1", "d0", "y"] + bits[2:], short)
    s = Part(high + ["y"], ["d1", "d0", "y"] + bits[2:], 16, f32)
    return early, [q, k, v, s]


def back_kernel(parts, scale, hidden, *refs):
    (
        qt, dm, dmt, nm, k_ref, vt, e_ref, cot, atoms, dmid, gain_ref, shift_ref, vec_ref,
        *refs,
    ) = refs
    made, refs = refs[: 2 * len(PIECES)], refs[2 * len(PIECES) :]
    (
        query_w, key_w, value_w,
        pg, out_ref, total,
        dkt, dvt, dq, qw, kw, vw,
        dk_in, dv_in, dqh, dqh_in, vec_own, vec_in, standard, normed, partial, beside_send, beside_recv,
        across_send, across_recv, grads, vec_all, load_sem, send_sem, recv_sem,
        *refs,
    ) = refs
    slots, width, full = dkt.shape
    rows, half = dq.shape[1], width // 2
    bits = parts.bit_length() - 1
    short, tall = width // parts, hidden // parts
    row, dp = lax.axis_index("rows"), lax.axis_index("dp")
    core, y = row % 2, row // 2
    beside, across = (dp, row + 1 - 2 * core), (dp, row + 2 - 4 * y)

    def partner(name):
        if name == "y":
            return across
        b = int(name[1:])
        return (xor(dp, 1 << b, bits), row)

    early, late = make_parts(parts, width, hidden)
    for piece in early + late:
        n = len(piece.scratch())
        piece.bind(refs[:n], partner)
        refs = refs[n:]
    one, two = early[:3], early[3:]
    steps, late_steps = len(early[0].steps), len(late[0].steps)

    def opened(group):
        for piece in group:
            piece.opened(made[2 * early.index(piece)])
            piece.go(0)

    def advance(group, n):
        for piece in group:
            piece.come(n)
            if n + 1 < len(piece.steps):
                piece.go(n + 1)

    loads = [
        pltpu.make_async_copy(hbm, vmem, load_sem.at[i])
        for i, (hbm, vmem) in enumerate(((query_w, qw), (key_w, kw), (value_w, vw)))
    ]
    for copy in loads:
        copy.start()
    corner = (dp, 3 - row)
    meet([beside, across, corner] + [partner("d%d" % b) for b in range(bits)])
    for n, piece in enumerate(early):
        piece.open(made[2 * n + 1])

    sent = 0

    def send(source, target, device):
        nonlocal sent
        sent += 1
        return remote(source, target, send_sem.at[sent - 1], recv_sem.at[sent - 1], device)

    other = pl.ds(pl.multiple_of((1 - core) * half, half), half)
    mine = pl.ds(pl.multiple_of(core * half, half), half)
    gain, shift = wide(gain_ref), wide(shift_ref)
    down = lambda value: jnp.sum(value, axis=0, keepdims=True)
    gain_grad = shift_grad = value_bias = 0.0
    send_on, to_sibling = [], []
    for s in range(slots):
        def block(b, carry):
            attention_backward(s, b, qt, dm, dmt, nm, k_ref, vt, e_ref, cot, pg, dq, dkt, dvt)
            return carry

        lax.fori_loop(0, width // 128, block, 0)
        to_sibling.append(send(dkt.at[s, other, :], dk_in.at[s], beside))
        to_sibling.append(send(dvt.at[s, other, :], dv_in.at[s], beside))
        if s == 0:
            for copy in loads:
                copy.wait()
        standard[s] = standardize(atoms[s].astype(f32))[0]
        normed[s] = (standard[s] * gain + shift).astype(bf16)
        dv = dvt[s].T
        grad = times_transposed(dkt[s].T, kw[...]) + times_transposed(dv, vw[...])
        value_bias = value_bias + down(dv.astype(f32))
        gain_grad = gain_grad + down(grad * standard[s])
        shift_grad = shift_grad + down(grad)
        for i in range(full // rows):
            partial[xor(row, i, 2), s] = grad[rows * i : rows * (i + 1)]
        beside_send[s, 0] = partial[1, s].astype(bf16)
        beside_send[s, 1] = partial[3, s].astype(bf16)
        send_on.append(send(beside_send.at[s], beside_recv.at[s], beside))
        if s == slots - 2:
            opened(one)
    opened(two)
    dq_low = jnp.concatenate([dq[s] for s in range(slots)], axis=0)
    dqh[0] = dq_low[:, :half]
    dqh[1] = dq_low[:, half:]
    to_sibling.append(send(dqh.at[1 - core], dqh_in, beside))
    own = pl.ds(pl.multiple_of(row * rows, rows), rows)
    next_to = pl.ds(pl.multiple_of((row + 1 - 2 * core) * rows, rows), rows)
    rows_of = lambda ref, which: jnp.concatenate([ref[s, which, :] for s in range(slots)], axis=0)
    query_grad = times_transposed(dq_low, qw[...]) * scale
    vec_own[0:1, :] = gain_grad + down(query_grad * rows_of(standard, own))
    vec_own[1:2, :] = shift_grad + down(query_grad)
    vec_own[2:3, :] = down(dq_low.astype(f32)) * scale
    vec_own[3:4, :] = value_bias
    vec_own[4:12, :] = vec_ref[...]
    vec_own[12:16, :] = jnp.zeros((4, width), f32)
    vec_sent = send(vec_own, vec_in, beside)

    advance(one, 0)
    for s in range(slots):
        send_on[s].wait()
        across_send[s] = (partial[2, s] + beside_recv[s, 1].astype(f32)).astype(bf16)
    over = send(across_send, across_recv, across)

    for copy in to_sibling:
        copy.wait()
    grads[0] = (
        outer_sum(rows_of(normed, own), dqh[core]) + outer_sum(rows_of(normed, next_to), dqh_in[...])
    ) * scale
    key_total = value_total = 0.0
    add = lambda left, right: (left.astype(f32) + right.astype(f32)).astype(bf16)
    for s in range(slots):
        turned = normed[s].T
        key_total = key_total + times_transposed(turned, add(dkt[s, mine, :], dk_in[s]))
        value_total = value_total + times_transposed(turned, add(dvt[s, mine, :], dv_in[s]))
    grads[1] = key_total
    grads[2] = value_total
    vec_sent.wait()
    vec = vec_own[...] + vec_in[...]
    vec_all[...] = jnp.zeros_like(vec_all)
    for j in range(parts):
        vec_all[j, 0:4, :short] = vec[0:4, short * j : short * (j + 1)]
        vec_all[j, 4:8, :short] = vec[8:12, short * j : short * (j + 1)]
        start = tall * j
        vec_all[j, 8:9, :tall] = vec[4 + start // width : 5 + start // width, start % width : start % width + tall]
    for p in range(parts):
        j = xor(dp, p, bits)
        for r in range(2):
            lanes = pl.ds(pl.multiple_of(other_bit(y, 0, r) * 128, 128), 128)
            for i, piece in enumerate(late[:3]):
                piece.state[2 * p + r] = grads[i, pl.ds(pl.multiple_of(j * short, short), short), lanes]
            late[3].state[2 * p + r] = vec_all[j, :, lanes]
    for piece in late:
        piece.go(0)

    advance(two, 0)
    advance(one, 1)
    advance(late, 0)
    advance(two, 1)
    over.wait()
    for s in range(slots):
        some = slice(rows * s, rows * (s + 1))
        grad = partial[0, s] + beside_recv[s, 0].astype(f32) + across_recv[s].astype(f32) + query_grad[some]
        stand, inverse = standardize(atoms[s, own, :].astype(f32))
        out_ref[some, :] = (dmid[some, :] + norm_back(grad * gain, stand, inverse)).astype(bf16)
    for n in range(2, steps):
        advance(one, n)
        advance(late, n - 1)
        advance(two, n)

    def place(group, at):
        for piece in group:
            piece.share(total.at[row, at : at + piece.rows])
            at += piece.rows
        return at

    cut = place(early, 0)
    mine, theirs = total.at[row, :cut], total.at[across[1], :cut]
    arrive = send(mine, mine, across)
    ends = [send(mine, mine, beside)]
    for n in range(steps - 1, late_steps):
        advance(late, n)
    place(late, cut)
    rest = total.at[row, cut:]
    ends += [send(rest, rest, device) for device in (across, corner, beside)]
    arrive.wait()
    ends.append(send(theirs, theirs, beside))
    for copy in ends:
        copy.wait()


def back(parts, scale, qt, dm, dmt, nm, k, vt, weights, cot, atoms, dmid, vectors, vec, pieces, query_w, key_w, value_w):
    slots, width, full = vt.shape
    rows, half = qt.shape[2], width // 2
    here, hidden = slots * rows, width * 4
    vm = pl.BlockSpec(memory_space=pltpu.VMEM)
    far = pl.BlockSpec(memory_space=pltpu.HBM)
    kinds = sum(make_parts(parts, width, hidden), [])
    count = sum(piece.rows for piece in kinds)
    transfers = 3 * slots + 9
    scratch = [
        pltpu.VMEM((slots, width, full), bf16),
        pltpu.VMEM((slots, width, full), bf16),
        pltpu.VMEM((slots, rows, width), bf16),
        pltpu.VMEM((width, width), bf16),
        pltpu.VMEM((width, width), bf16),
        pltpu.VMEM((width, width), bf16),
        pltpu.VMEM((slots, half, full), bf16),
        pltpu.VMEM((slots, half, full), bf16),
        pltpu.VMEM((2, here, half), bf16),
        pltpu.VMEM((here, half), bf16),
        pltpu.VMEM((16, width), f32),
        pltpu.VMEM((16, width), f32),
        pltpu.VMEM((slots, full, width), f32),
        pltpu.VMEM((slots, full, width), bf16),
        pltpu.VMEM((4, slots, rows, width), f32),
        pltpu.VMEM((slots, 2, rows, width), bf16),
        pltpu.VMEM((slots, 2, rows, width), bf16),
        pltpu.VMEM((slots, rows, width), bf16),
        pltpu.VMEM((slots, rows, width), bf16),
        pltpu.VMEM((3, width, half), f32),
        pltpu.VMEM((parts, 16, half), f32),
        pltpu.SemaphoreType.DMA((3,)),
        pltpu.SemaphoreType.DMA((transfers,)),
        pltpu.SemaphoreType.DMA((transfers,)),
    ]
    for piece in kinds:
        scratch += piece.scratch()
    return pl.pallas_call(
        functools.partial(back_kernel, parts, scale, hidden),
        in_specs=[vm] * (13 + 2 * len(PIECES)) + [far] * 3,
        out_specs=[vm] * 3,
        out_shape=[
            jax.ShapeDtypeStruct(cot.shape, bf16),
            jax.ShapeDtypeStruct((here, width), bf16),
            jax.ShapeDtypeStruct((4, count, 128), bf16),
        ],
        scratch_shapes=scratch,
        name="back",
        cost_estimate=pl.CostEstimate(
            flops=40 * slots * full * width * width, transcendentals=0, bytes_accessed=32 << 20
        ),
        compiler_params=pltpu.CompilerParams(vmem_limit_bytes=VMEM_BACK, collective_id=2, has_side_effects=True),
    )(
        qt, dm, dmt, nm, k, vt, weights, cot, atoms, dmid, *vectors, vec, *pieces,
        *(pltpu.with_memory_space_constraint(array, pltpu.HBM) for array in (query_w, key_w, value_w)),
    )


def last_kernel(total, grad_ref, made_ref, pair, *refs):
    count = 18
    outs, refs = refs[:count], refs[count:]
    (grad_out, made_out, *_, pair_out), (uw, ow, iw, qw, kw, vw), small, sem = outs, refs[:6], refs[6:15], refs[15]
    copies = []

    def move(source, target):
        copy = pltpu.make_async_copy(source, target, sem.at[len(copies)])
        copy.start()
        copies.append(copy)

    move(pair, pair_out)
    move(grad_ref, grad_out)
    move(made_ref, made_out)
    short = ow.shape[0]
    blocks = iw.shape[1] // 2 // 256
    spots = [spot for _, of in PIECES for spot in of] + [("query", 0), ("key", 0), ("value", 0)]
    refs = {"outer": uw, "inner": iw, "out": ow, "query": qw, "key": kw, "value": vw}
    at = 0
    for name, k in spots:
        ref = refs[name]
        first = short * k if name == "outer" else 0
        for r in range(4):
            core, y = r % 2, r // 2
            col = 256 * (core * blocks + k if name == "inner" else core) + 128 * y
            ref[first : first + short, col : col + 128] = total[r, at : at + short, :].astype(f32)
        at += short
    for ref, out in zip((uw, ow, iw, qw, kw, vw), outs[2:8]):
        move(ref, out)
    for i, ref in enumerate(small[:8]):
        ref[...] = total[0, at : at + 16, :].astype(f32)[i : i + 1, :short]
    ib = small[8]
    for y in range(2):
        n = min(128, ib.shape[1] - 128 * y)
        if n > 0:
            ib[:, 128 * y : 128 * y + n] = total[2 * y, at : at + 16, :].astype(f32)[8:9, :n]
    for ref, out in zip(small, outs[8:17]):
        move(ref, out)
    for copy in copies:
        copy.wait()


def last(parts, total, grad, made, pair, hidden):
    here, width = grad.shape
    short, tall = width // parts, hidden // parts
    vm = pl.BlockSpec(memory_space=pltpu.VMEM)
    hbm = pl.BlockSpec(memory_space=pl.ANY)
    shapes = [(tall, width), (short, width), (short, hidden)] + [(short, width)] * 3
    shapes += [(1, short)] * 8 + [(1, tall)]
    out_shape = [jax.ShapeDtypeStruct(grad.shape, bf16)] * 2
    out_shape += [jax.ShapeDtypeStruct(shape, f32) for shape in shapes]
    out_shape.append(jax.ShapeDtypeStruct(pair.shape, bf16))
    return pl.pallas_call(
        last_kernel,
        in_specs=[vm] + [hbm] * 3,
        out_specs=[hbm] * len(out_shape),
        out_shape=out_shape,
        scratch_shapes=[pltpu.VMEM(shape, f32) for shape in shapes] + [pltpu.SemaphoreType.DMA((len(out_shape),))],
        name="last",
        compiler_params=pltpu.CompilerParams(vmem_limit_bytes=16 << 20),
    )(total, grad, made, pair)


def local(
    parts,
    group,
    atoms,
    pair_bias,
    mol_counts,
    attn_gain,
    attn_shift,
    query_weight,
    query_bias,
    key_weight,
    value_weight,
    value_bias,
    out_weight,
    out_bias,
    ffn_gain,
    ffn_shift,
    inner_weight,
    inner_bias,
    outer_weight,
    outer_bias,
    atoms_cotangent,
    pair_cotangent,
):
    slots, part_rows, width = atoms.shape
    heads = pair_bias.shape[1]
    full = pair_bias.shape[3]
    scale = (width // heads) ** (-0.5)
    here = slots * part_rows
    hidden = inner_weight.shape[1]
    flat = lambda array: array.reshape(here, width)
    all_atoms, mask, q, qt, k, kt, v, vt = front(
        scale, full, atoms, mol_counts, (attn_gain, attn_shift, query_bias, value_bias), query_weight, key_weight, value_weight
    )
    pair_out, weights, mixed, inverse_sum = attention_forward(q, kt, v, pair_bias, mask)
    atoms_out, *pieces, scaled, centre, scaled_turned, grad_middle, vec = middle(
        parts,
        flat(mixed),
        flat(inverse_sum),
        flat(atoms),
        flat(atoms_cotangent),
        (out_bias, ffn_gain, ffn_shift, outer_bias, inner_bias),
        out_weight,
        inner_weight,
        outer_weight,
        slots,
    )
    pair_grad, grad, total = back(
        parts,
        scale,
        qt,
        scaled.reshape(q.shape),
        scaled_turned,
        centre.reshape(q.shape),
        k,
        vt,
        weights,
        pair_cotangent,
        all_atoms,
        grad_middle,
        (attn_gain, attn_shift),
        vec,
        pieces,
        query_weight,
        key_weight,
        value_weight,
    )
    grad, made, uw, ow, iw, qw, kw, vw, again, ashift, qb, vb, ob, fgain, fshift, ub, ib, pair_grad = last(
        parts, total, grad, atoms_out, pair_grad, hidden
    )
    line = lambda array: array.reshape(-1)
    return (
        made.reshape(atoms.shape),
        pair_out,
        grad.reshape(atoms.shape),
        pair_grad,
        line(again),
        line(ashift),
        qw,
        line(qb),
        kw,
        vw,
        line(vb),
        ow,
        line(ob),
        line(fgain),
        line(fshift),
        iw,
        line(ib),
        uw,
        line(ub),
    )


def solution(mesh):
    one, two = P("dp"), P("dp", None)
    atoms_spec, pair_spec = P("dp", "rows", None), P("dp", None, "rows", None)
    in_specs = (atoms_spec, pair_spec, two) + (P(),) * 15 + (atoms_spec, pair_spec)
    out_specs = (
        (atoms_spec, pair_spec, atoms_spec, pair_spec, one, one, two, one, two, two, one, two)
        + (one, one, one, two, one, two, one)
    )
    run = functools.partial(local, mesh.shape["dp"], mesh.shape["rows"])
    return jax.shard_map(run, mesh=mesh, in_specs=in_specs, out_specs=out_specs, check_vma=False)
```

```python
import functools

import jax
import jax.numpy as jnp
from jax import lax
from jax.experimental import pallas as pl
from jax.experimental.pallas import tpu as pltpu
from jax.sharding import PartitionSpec as P

f32, bf16 = jnp.float32, jnp.bfloat16
BIG = 1e9
HPL = 16
WIDE = 16
CHUNK = 8
STEP = 64
VMEM_PAIR = 22 << 20
VMEM_BACK = 26 << 20
MESH = pl.DeviceIdType.MESH
PIECES = (
    ("d0", (("outer", 0), ("outer", 1))),
    ("y", (("outer", 2),)),
    ("d1", (("outer", 3),)),
    ("d0", (("inner", 0),)),
    ("y", (("inner", 1), ("inner", 2))),
    ("d1", (("inner", 3), ("out", 0))),
)


def standardize(value):
    centred = value - jnp.mean(value, axis=-1, keepdims=True)
    inverse = lax.rsqrt(jnp.mean(centred * centred, axis=-1, keepdims=True) + 1e-05)
    return (centred * inverse, inverse)


def norm_back(grad_normed, standard, inverse):
    return inverse * (
        grad_normed
        - jnp.mean(grad_normed, axis=-1, keepdims=True)
        - standard * jnp.mean(grad_normed * standard, axis=-1, keepdims=True)
    )


def matmul(left, right):
    return jnp.dot(left, right, preferred_element_type=f32)


def times_transposed(left, right):
    return lax.dot_general(left, right, (((1,), (1,)), ((), ())), preferred_element_type=f32)


def outer_sum(left, right):
    return lax.dot_general(left, right, (((0,), (0,)), ((), ())), preferred_element_type=f32)


def other_bit(index, bit, const):
    own = (index // (1 << bit)) % 2
    return 1 - own if (const >> bit) & 1 else own


def xor(index, const, bits):
    return sum(other_bit(index, b, const) * (1 << b) for b in range(bits))


def remote(source, target, send_sem, recv_sem, device):
    copy = pltpu.make_async_remote_copy(
        src_ref=source, dst_ref=target, send_sem=send_sem, recv_sem=recv_sem, device_id=device, device_id_type=MESH
    )
    copy.start()
    return copy


def meet(devices):
    barrier = pltpu.get_barrier_semaphore()
    for device in devices:
        pl.semaphore_signal(barrier, inc=1, device_id=device, device_id_type=MESH)
    pl.semaphore_wait(barrier, len(devices))


def wide(ref):
    return ref[...].astype(f32).reshape(1, -1)


def front_kernel(
    scale,
    atoms_ref,
    counts_ref,
    gain_ref,
    shift_ref,
    query_b,
    value_b,
    query_w,
    key_w,
    value_w,
    all_ref,
    mask_ref,
    q_ref,
    qt_ref,
    k_ref,
    kt_ref,
    v_ref,
    vt_ref,
    qw,
    kw,
    vw,
    load_sem,
    send_sem,
    recv_sem,
):
    slots, rows, width = atoms_ref.shape
    full = mask_ref.shape[2]
    row, dp = lax.axis_index("rows"), lax.axis_index("dp")
    core, y = row % 2, row // 2
    beside, across = row + 1 - 2 * core, row + 2 - 4 * y
    loads = [
        pltpu.make_async_copy(hbm, vmem, load_sem.at[i])
        for i, (hbm, vmem) in enumerate(((query_w, qw), (key_w, kw), (value_w, vw)))
    ]
    for copy in loads:
        copy.start()
    meet([(dp, beside), (dp, across)])
    at = lambda r: pl.ds(pl.multiple_of(r * rows, rows), rows)
    here = lambda s: all_ref.at[s, at(row), :]
    there = lambda s: all_ref.at[s, at(across), :]
    far = [remote(atoms_ref.at[s], here(s), send_sem.at[s], recv_sem.at[s], (dp, across)) for s in range(slots)]
    near = [
        remote(atoms_ref.at[s], here(s), send_sem.at[slots + s], recv_sem.at[slots + s], (dp, beside))
        for s in range(slots)
    ]
    gain, shift = wide(gain_ref), wide(shift_ref)
    bias = wide(value_b)
    for s in range(slots):
        all_ref[s, at(row), :] = atoms_ref[s]
    own = atoms_ref[...].reshape(slots * rows, width).astype(f32)
    normed = (standardize(own)[0] * gain + shift).astype(bf16)
    loads[0].wait()
    queries = ((matmul(normed, qw[...]) + wide(query_b)) * scale).astype(bf16)
    for s in range(slots):
        part = queries[rows * s : rows * (s + 1)]
        q_ref[s] = part
        qt_ref[s] = part.T
    loads[1].wait()
    loads[2].wait()

    def project(s, chip):
        some = pl.ds(pl.multiple_of(chip * 2 * rows, 2 * rows), 2 * rows)
        normed = (standardize(all_ref[s, some, :].astype(f32))[0] * gain + shift).astype(bf16)
        keys = matmul(normed, kw[...]).astype(bf16)
        k_ref[s, some, :] = keys
        kt_ref[s, :, some] = keys.T
        values = (matmul(normed, vw[...]) + bias).astype(bf16)
        v_ref[s, some, :] = values
        vt_ref[s, :, some] = values.T

    def masks(s):
        ends = [counts_ref[s, 0]]
        for m in range(1, counts_ref.shape[1]):
            ends.append(ends[-1] + counts_ref[s, m])
        keys_at = lax.broadcasted_iota(jnp.int32, (1, full), 1)
        queries_at = lax.broadcasted_iota(jnp.int32, (rows, 1), 0) + row * rows
        count = lambda at: sum((end <= at).astype(jnp.int32) for end in ends)
        mask_ref[s] = jnp.where(count(keys_at) == count(queries_at), 0.0, -BIG)

    forward = []

    def pass_on(s):
        far[s].wait()
        n = 2 * slots + s
        forward.append(remote(there(s), there(s), send_sem.at[n], recv_sem.at[n], (dp, beside)))

    for s in range(slots):
        if s == slots - 1:
            pass_on(0)
        near[s].wait()
        project(s, y)
    for s in range(slots):
        masks(s)
    for s in range(1, slots):
        pass_on(s)
        forward[s - 1].wait()
        project(s - 1, 1 - y)
    forward[-1].wait()
    project(slots - 1, 1 - y)


def front(scale, full, atoms, counts, vectors, query_w, key_w, value_w):
    slots, rows, width = atoms.shape
    vm = pl.BlockSpec(memory_space=pltpu.VMEM)
    hbm = pl.BlockSpec(memory_space=pltpu.HBM)
    like = lambda *shape: jax.ShapeDtypeStruct(shape, bf16)
    out_shape = [
        like(slots, full, width),
        jax.ShapeDtypeStruct((slots, rows, full), f32),
        like(slots, rows, width),
        like(slots, width, rows),
        like(slots, full, width),
        like(slots, width, full),
        like(slots, full, width),
        like(slots, width, full),
    ]
    return pl.pallas_call(
        functools.partial(front_kernel, scale),
        in_specs=[vm, pl.BlockSpec(memory_space=pltpu.SMEM)] + [vm] * 4 + [hbm] * 3,
        out_specs=[vm] * len(out_shape),
        out_shape=out_shape,
        scratch_shapes=[pltpu.VMEM((width, width), bf16)] * 3
        + [
            pltpu.SemaphoreType.DMA((3,)),
            pltpu.SemaphoreType.DMA((3 * slots,)),
            pltpu.SemaphoreType.DMA((3 * slots,)),
        ],
        name="front",
        cost_estimate=pl.CostEstimate(
            flops=48 * slots * full * width * width, transcendentals=0, bytes_accessed=32 << 20
        ),
        compiler_params=pltpu.CompilerParams(vmem_limit_bytes=18 << 20, collective_id=0, has_side_effects=True),
    )(*(pltpu.with_memory_space_constraint(array, pltpu.HBM) for array in (atoms, counts, *vectors, query_w, key_w, value_w)))


def forward_kernel(q_ref, kt_ref, v_ref, bias_ref, mask_ref, out_ref, e_ref, mix_ref, rl_ref):
    _, heads, rows, full = bias_ref.shape
    lane_head = lax.broadcasted_iota(jnp.int32, (rows, 128), 1) // 8
    mask = mask_ref[0]
    ones = jnp.ones((full, 128), bf16)
    for b in range(heads // HPL):
        cols = slice(128 * b, 128 * b + 128)
        q = q_ref[0, :, cols].astype(f32)
        kt = kt_ref[0, cols, :]
        v = jnp.concatenate([v_ref[0, :, cols], ones], axis=1)
        mixed = jnp.zeros((rows, 128), f32)
        total = jnp.zeros((rows, 128), f32)
        for c in range(HPL // WIDE):
            own = [lane_head == WIDE * c + i for i in range(WIDE)]
            left = jnp.concatenate([jnp.where(o, q, 0.0).astype(bf16) for o in own], axis=0)
            scores = matmul(left, kt).reshape(WIDE, rows, full)
            hs = slice(HPL * b + WIDE * c, HPL * b + WIDE * (c + 1))
            scores = scores + bias_ref[0, hs].astype(f32)
            out_ref[0, hs] = scores.astype(bf16)
            scores = scores + mask[None]
            highest = jnp.max(scores, axis=-1, keepdims=True)
            e = jnp.exp(scores - highest).astype(bf16)
            e_ref[0, hs] = e
            sums = matmul(e.reshape(WIDE * rows, full), v)
            for i, o in enumerate(own):
                mixed = jnp.where(o, sums[rows * i : rows * (i + 1), :128], mixed)
                total = jnp.where(o, sums[rows * i : rows * (i + 1), 128:], total)
        inverse = 1.0 / total
        mix_ref[0, :, cols] = mixed * inverse
        rl_ref[0, :, cols] = inverse


def attention_forward(q, kt, v, bias, mask):
    slots, heads, rows, full = bias.shape
    step = min(STEP, heads)
    width = step * 8
    natural = lambda n: pl.BlockSpec((1, n, width), lambda s, h: (s, 0, h))
    pair = pl.BlockSpec((1, step, rows, full), lambda s, h: (s, h, 0, 0))
    return pl.pallas_call(
        forward_kernel,
        grid=(slots, heads // step),
        in_specs=[
            natural(rows),
            pl.BlockSpec((1, width, full), lambda s, h: (s, h, 0)),
            natural(full),
            pair,
            pl.BlockSpec((1, rows, full), lambda s, h: (s, 0, 0)),
        ],
        out_specs=[pair, pair, natural(rows), natural(rows)],
        out_shape=[
            jax.ShapeDtypeStruct(bias.shape, bf16),
            jax.ShapeDtypeStruct(bias.shape, bf16),
            jax.ShapeDtypeStruct(q.shape, f32),
            jax.ShapeDtypeStruct(q.shape, f32),
        ],
        name="attention_forward",
        cost_estimate=pl.CostEstimate(
            flops=2 * bias.size * 512, transcendentals=bias.size, bytes_accessed=bias.size * 6
        ),
        compiler_params=pltpu.CompilerParams(vmem_limit_bytes=VMEM_PAIR),
    )(q, kt, v, bias, mask)


def attention_backward(s, b, qt_ref, dm_ref, dmt_ref, nm_ref, k_ref, vt_ref, e_ref, cot_ref, pg_ref, dq_ref, dkt_ref, dvt_ref):
    _, heads, rows, full = cot_ref.shape
    lane_head = lax.broadcasted_iota(jnp.int32, (rows, 128), 1) // 8
    shape = (8 * CHUNK, CHUNK * rows)
    same = lax.broadcasted_iota(jnp.int32, shape, 0) // 8 == lax.broadcasted_iota(jnp.int32, shape, 1) // rows
    ones = jnp.ones((128, full), bf16)
    cols = pl.ds(pl.multiple_of(128 * b, 128), 128)
    dm = dm_ref[s, :, cols].astype(f32)
    nm = nm_ref[s, :, cols].astype(f32)
    vt = jnp.concatenate([vt_ref[s, cols, :], ones], axis=0)
    k = k_ref[s, :, cols]
    dq = jnp.zeros((rows, 128), f32)
    for c in range(HPL // CHUNK):
        own = [lane_head == CHUNK * c + i for i in range(CHUNK)]
        left = jnp.concatenate(
            [
                jnp.concatenate([jnp.where(o, dm, 0.0), jnp.where(o, nm, 0.0)], axis=1).astype(bf16)
                for o in own
            ],
            axis=0,
        )
        centred = matmul(left, vt).reshape(CHUNK, rows, full)
        hs = pl.ds(HPL * b + CHUNK * c, CHUNK)
        e = e_ref[s, hs]
        grad = (e.astype(f32) * centred + cot_ref[s, hs].astype(f32)).astype(bf16)
        pg_ref[s, hs] = grad
        grad = grad.reshape(CHUNK * rows, full)
        sums = matmul(grad, k)
        for i, o in enumerate(own):
            dq = jnp.where(o, sums[rows * i : rows * (i + 1)], dq)
        rs = pl.ds(pl.multiple_of(128 * b + 8 * CHUNK * c, 8 * CHUNK), 8 * CHUNK)
        spread = lambda ref: jnp.where(
            same, jnp.concatenate([ref[s, rs, :].astype(f32)] * CHUNK, axis=1), 0.0
        ).astype(bf16)
        dkt_ref[s, rs, :] = matmul(spread(qt_ref), grad).astype(bf16)
        dvt_ref[s, rs, :] = matmul(spread(dmt_ref), e.reshape(CHUNK * rows, full)).astype(bf16)
    dq_ref[s, :, cols] = dq.astype(bf16)


def middle_kernel(
    parts,
    mix_ref,
    rl_ref,
    atoms_ref,
    dy_ref,
    out_b,
    gain_ref,
    shift_ref,
    outer_b,
    bias_ref,
    ow,
    iw,
    uw,
    out_ref,
    *refs,
):
    pieces, refs = refs[: 2 * len(PIECES)], refs[2 * len(PIECES) :]
    (
    dm_ref,
    nm_ref,
    dmt_ref,
    dmid_ref,
    vec_ref,
    act,
    dpre,
    dpre_in,
    inner,
    mixed,
    branch,
    branch_in,
    dyh,
    dy_in,
    grads,
    send_sem,
    recv_sem,
    ) = refs
    here, width = atoms_ref.shape
    half = width // 2
    blocks = act.shape[1]
    slots, _, rows = dmt_ref.shape
    bits = parts.bit_length() - 1
    row = lax.axis_index("rows")
    dp = lax.axis_index("dp")
    core = row % 2
    y = row // 2
    sibling = (dp, row + 1 - 2 * core)

    barrier = pltpu.get_barrier_semaphore()
    pl.semaphore_signal(barrier, inc=1, device_id=sibling, device_id_type=pl.DeviceIdType.MESH)
    sent = []

    def send(source, target):
        n = len(sent)
        copy = pltpu.make_async_remote_copy(
            src_ref=source,
            dst_ref=target,
            send_sem=send_sem.at[n],
            recv_sem=recv_sem.at[n],
            device_id=sibling,
            device_id_type=pl.DeviceIdType.MESH,
        )
        copy.start()
        sent.append(copy)

    dy = dy_ref[...]
    dyh[0] = dy[:, :half]
    dyh[1] = dy[:, half:]
    mix = mix_ref[...]
    mixed[0] = mix.astype(bf16)
    middle = atoms_ref[...].astype(f32) + matmul(mixed[0], ow[...]) + wide(out_b)
    standard, inverse = standardize(middle)
    gain = wide(gain_ref)
    inner[0] = (standard * gain + wide(shift_ref)).astype(bf16)
    pl.semaphore_wait(barrier, 1)
    send(dyh.at[1 - core], dy_in)
    send(mixed.at[0], mixed.at[1])
    send(inner.at[0], inner.at[1])
    result = middle + wide(outer_b)
    bias = wide(bias_ref)
    grad_inner = jnp.zeros((here, width), f32)
    for b in range(blocks):
        cols = slice(width * b, width * (b + 1))
        pre = matmul(inner[0], iw[:, cols]) + bias[:, cols]
        cdf = 0.5 + 0.5 * lax.erf(pre * (0.5**0.5))
        low = (pre * cdf).astype(bf16)
        act[0, b] = low
        send(act.at[0, b], act.at[1, b])
        slope = cdf + pre * (jnp.exp(-0.5 * pre * pre) * 0.3989422804014327)
        grad = (times_transposed(dy, uw[cols, :]) * slope).astype(bf16)
        dpre[b] = grad
        result = result + matmul(low, uw[cols, :])
        grad_inner = grad_inner + times_transposed(grad, iw[:, cols])
        vec_ref[b : b + 1, :] = jnp.sum(grad.astype(f32), axis=0, keepdims=True)
    for i in range(blocks // 2):
        send(dpre.at[(blocks // 2) * (1 - core) + i], dpre_in.at[i])
    out_ref[...] = result.astype(bf16)
    dy_wide = dy.astype(f32)
    grad_middle = dy_wide + norm_back(grad_inner * gain, standard, inverse)
    dmid_ref[...] = grad_middle
    low = grad_middle.astype(bf16)
    branch[0] = low[:, :half]
    branch[1] = low[:, half:]
    send(branch.at[1 - core], branch_in)
    down = lambda value: jnp.sum(value, axis=0, keepdims=True)
    vec_ref[blocks : blocks + 1, :] = down(low.astype(f32))
    vec_ref[blocks + 1 : blocks + 2, :] = down(grad_inner * standard)
    vec_ref[blocks + 2 : blocks + 3, :] = down(grad_inner)
    vec_ref[blocks + 3 : blocks + 4, :] = down(dy_wide)
    scaled = times_transposed(low, ow[...]).astype(bf16).astype(f32) * rl_ref[...]
    nm_ref[...] = (-scaled * mix).astype(bf16)
    scaled = scaled.astype(bf16)
    dm_ref[...] = scaled
    for s in range(slots):
        dmt_ref[s] = scaled[rows * s : rows * (s + 1)].astype(f32).T.astype(bf16)

    for copy in sent:
        copy.wait()
    tall, short = blocks * width // parts, width // parts
    dy_own = dyh[core]
    for b in range(blocks):
        grads[width * b : width * (b + 1), :] = outer_sum(act[0, b], dy_own) + outer_sum(act[1, b], dy_in[...])
    base = blocks * width
    for i in range(blocks // 2):
        grad = outer_sum(inner[0], dpre[(blocks // 2) * core + i]) + outer_sum(inner[1], dpre_in[i])
        for k in range(2):
            grads[base + width * (2 * i + k) : base + width * (2 * i + k + 1), :] = grad[:, half * k : half * (k + 1)]
    last = base + width * blocks
    grads[last:, :] = outer_sum(mixed[0], branch[core]) + outer_sum(mixed[1], branch_in[...])

    def at(start, n, h):
        return grads[pl.ds(pl.multiple_of(start, 8), n), pl.ds(pl.multiple_of(h * 128, 128), 128)]

    start = {"outer": (0, tall), "inner": (base, short), "out": (last, short)}
    step = {"outer": short, "inner": width, "out": 0}
    for p in range(parts):
        j = xor(dp, p, bits)
        for r in range(2):
            h = other_bit(y, 0, r)
            for n, (opening, parts_of) in enumerate(PIECES):
                if opening == "y":
                    gone, q = r, p
                elif opening == "d0":
                    gone, q = p & 1, 2 * (p >> 1) + r
                else:
                    gone, q = (p >> 1) & 1, 2 * ((p >> 2) * 2 + (p & 1)) + r
                ref = pieces[2 * n + gone]
                for i, (kind, k) in enumerate(parts_of):
                    first, per = start[kind]
                    ref[q, short * i : short * (i + 1)] = at(first + step[kind] * k + per * j, short, h).astype(ref.dtype)


def middle(parts, mix, rl, atoms, dy, vectors, out_w, inner_w, outer_w, slots):
    here, width = atoms.shape
    hidden = inner_w.shape[1]
    blocks, half, rows = hidden // width, width // 2, here // slots
    tall, short = hidden // parts, width // parts
    assert hidden == 4 * width
    vm = pl.BlockSpec(memory_space=pltpu.VMEM)
    like = jax.ShapeDtypeStruct
    out_shape = [
        like((here, width), bf16),
        *(like((parts, len(blocks_of) * short, 128), kind) for _, blocks_of in PIECES for kind in (f32, bf16)),
        like((here, width), bf16),
        like((here, width), bf16),
        like((slots, width, rows), bf16),
        like((here, width), f32),
        like((blocks + 4, width), f32),
    ]
    transfers = 3 + blocks + blocks // 2 + 1
    return pl.pallas_call(
        functools.partial(middle_kernel, parts),
        in_specs=[vm] * 12,
        out_specs=[vm] * len(out_shape),
        out_shape=out_shape,
        scratch_shapes=[
            pltpu.VMEM((2, blocks, here, width), bf16),
            pltpu.VMEM((blocks, here, width), bf16),
            pltpu.VMEM((blocks // 2, here, width), bf16),
            pltpu.VMEM((2, here, width), bf16),
            pltpu.VMEM((2, here, width), bf16),
            pltpu.VMEM((2, here, half), bf16),
            pltpu.VMEM((here, half), bf16),
            pltpu.VMEM((2, here, half), bf16),
            pltpu.VMEM((here, half), bf16),
            pltpu.VMEM((2 * hidden + width, half), f32),
            pltpu.SemaphoreType.DMA((transfers,)),
            pltpu.SemaphoreType.DMA((transfers,)),
        ],
        name="middle",
        cost_estimate=pl.CostEstimate(
            flops=12 * here * width * hidden, transcendentals=2 * here * hidden, bytes_accessed=12 << 20
        ),
        compiler_params=pltpu.CompilerParams(
            vmem_limit_bytes=20 << 20, collective_id=1, has_side_effects=True
        ),
    )(
        mix, rl, atoms, dy, *vectors, out_w, inner_w, outer_w,
    )


class Part:
    def __init__(self, names, order, rows, dtype=bf16, opening=None):
        self.opening = opening
        self.names, self.order, self.rows, self.dtype = names, order, rows, dtype
        self.steps, left = [], list(names)
        for name in order:
            others = [n for n in left if n != name]
            spots = []
            for q in range(1 << len(others)):
                base = sum(
                    self.stride(n) for i, n in enumerate(others) if (q >> (len(others) - 1 - i)) & 1
                )
                spots.append((base, base + self.stride(name)))
            self.steps.append((name, spots))
            left = others

    def stride(self, name):
        return 1 << (len(self.names) - 1 - self.names.index(name))

    def scratch(self):
        shapes = [pltpu.VMEM((1 << len(self.names), self.rows, 128), f32)]
        if self.opening:
            shapes.append(pltpu.VMEM((1 << len(self.names), self.rows, 128), self.dtype))
        for _, spots in self.steps:
            shapes += [pltpu.VMEM((len(spots), self.rows, 128), self.dtype)] * 2
        n = len(self.steps) + 1
        return shapes + [pltpu.SemaphoreType.DMA((n,)), pltpu.SemaphoreType.DMA((n,))]

    def bind(self, refs, partner):
        self.state, refs = refs[0], refs[1:]
        if self.opening:
            self.first, refs = refs[0], refs[1:]
        self.sends, self.recvs = refs[0:-2:2], refs[1:-2:2]
        self.send_sem, self.recv_sem, self.partner = refs[-2], refs[-1], partner

    def open(self, send):
        n = len(self.steps)
        self.copy = remote(send, self.first, self.send_sem.at[n], self.recv_sem.at[n], self.partner(self.opening))

    def opened(self, keep):
        self.copy.wait()
        self.state[...] = keep[...] + self.first[...].astype(f32)

    def go(self, n):
        name, spots = self.steps[n]
        for q, (_, far) in enumerate(spots):
            self.sends[n][q] = self.state[far].astype(self.dtype)
        self.copy = remote(
            self.sends[n], self.recvs[n], self.send_sem.at[n], self.recv_sem.at[n], self.partner(name)
        )

    def come(self, n):
        self.copy.wait()
        for q, (near, _) in enumerate(self.steps[n][1]):
            self.state[near] = self.state[near] + self.recvs[n][q].astype(f32)

    def share(self, ref):
        ref[...] = self.state[0].astype(ref.dtype)


def make_parts(parts, width, hidden):
    bits = ["d%d" % b for b in range(parts.bit_length() - 1)]
    high = bits[::-1]
    short = width // parts
    without = lambda name: [n for n in high if n != name]
    kinds = {
        "d0": (without("d0") + ["y"], ["y", "d1"]),
        "y": (high, ["d1", "d0"]),
        "d1": (without("d1") + ["y"], ["d0", "y"]),
    }
    early = [
        Part(kinds[opening][0], kinds[opening][1] + bits[2:], len(blocks) * short, opening=opening)
        for opening, blocks in PIECES
    ]
    q = Part(high + ["y"], ["d0", "y", "d1"] + bits[2:], short)
    k = Part(high + ["y"], ["y", "d1", "d0"] + bits[2:], short)
    v = Part(high + ["y"], ["d1", "d0", "y"] + bits[2:], short)
    s = Part(high + ["y"], ["d1", "d0", "y"] + bits[2:], 16, f32)
    return early, [q, k, v, s]


def back_kernel(parts, scale, hidden, *refs):
    (
        qt, dm, dmt, nm, k_ref, vt, e_ref, cot, atoms, dmid, gain_ref, shift_ref, vec_ref,
        *refs,
    ) = refs
    made, refs = refs[: 2 * len(PIECES)], refs[2 * len(PIECES) :]
    (
        query_w, key_w, value_w,
        pg, out_ref, total,
        dkt, dvt, dq, qw, kw, vw,
        dk_in, dv_in, dqh, dqh_in, vec_own, vec_in, standard, normed, partial, beside_send, beside_recv,
        across_send, across_recv, grads, vec_all, load_sem, send_sem, recv_sem,
        *refs,
    ) = refs
    slots, width, full = dkt.shape
    rows, half = dq.shape[1], width // 2
    bits = parts.bit_length() - 1
    short, tall = width // parts, hidden // parts
    row, dp = lax.axis_index("rows"), lax.axis_index("dp")
    core, y = row % 2, row // 2
    beside, across = (dp, row + 1 - 2 * core), (dp, row + 2 - 4 * y)

    def partner(name):
        if name == "y":
            return across
        b = int(name[1:])
        return (xor(dp, 1 << b, bits), row)

    early, late = make_parts(parts, width, hidden)
    for piece in early + late:
        n = len(piece.scratch())
        piece.bind(refs[:n], partner)
        refs = refs[n:]
    one, two = early[:3], early[3:]
    steps, late_steps = len(early[0].steps), len(late[0].steps)

    def opened(group):
        for piece in group:
            piece.opened(made[2 * early.index(piece)])
            piece.go(0)

    def advance(group, n):
        for piece in group:
            piece.come(n)
            if n + 1 < len(piece.steps):
                piece.go(n + 1)

    loads = [
        pltpu.make_async_copy(hbm, vmem, load_sem.at[i])
        for i, (hbm, vmem) in enumerate(((query_w, qw), (key_w, kw), (value_w, vw)))
    ]
    for copy in loads:
        copy.start()
    corner = (dp, 3 - row)
    meet([beside, across, corner] + [partner("d%d" % b) for b in range(bits)])
    for n, piece in enumerate(early):
        piece.open(made[2 * n + 1])

    sent = 0

    def send(source, target, device):
        nonlocal sent
        sent += 1
        return remote(source, target, send_sem.at[sent - 1], recv_sem.at[sent - 1], device)

    other = pl.ds(pl.multiple_of((1 - core) * half, half), half)
    mine = pl.ds(pl.multiple_of(core * half, half), half)
    gain, shift = wide(gain_ref), wide(shift_ref)
    down = lambda value: jnp.sum(value, axis=0, keepdims=True)
    gain_grad = shift_grad = value_bias = 0.0
    send_on, to_sibling = [], []
    for s in range(slots):
        def block(b, carry):
            attention_backward(s, b, qt, dm, dmt, nm, k_ref, vt, e_ref, cot, pg, dq, dkt, dvt)
            return carry

        lax.fori_loop(0, width // 128, block, 0)
        to_sibling.append(send(dkt.at[s, other, :], dk_in.at[s], beside))
        to_sibling.append(send(dvt.at[s, other, :], dv_in.at[s], beside))
        if s == 0:
            for copy in loads:
                copy.wait()
        standard[s] = standardize(atoms[s].astype(f32))[0]
        normed[s] = (standard[s] * gain + shift).astype(bf16)
        dv = dvt[s].T
        grad = times_transposed(dkt[s].T, kw[...]) + times_transposed(dv, vw[...])
        value_bias = value_bias + down(dv.astype(f32))
        gain_grad = gain_grad + down(grad * standard[s])
        shift_grad = shift_grad + down(grad)
        for i in range(full // rows):
            partial[xor(row, i, 2), s] = grad[rows * i : rows * (i + 1)]
        beside_send[s, 0] = partial[1, s].astype(bf16)
        beside_send[s, 1] = partial[3, s].astype(bf16)
        send_on.append(send(beside_send.at[s], beside_recv.at[s], beside))
        if s == slots - 2:
            opened(one)
    opened(two)
    dq_low = jnp.concatenate([dq[s] for s in range(slots)], axis=0)
    dqh[0] = dq_low[:, :half]
    dqh[1] = dq_low[:, half:]
    to_sibling.append(send(dqh.at[1 - core], dqh_in, beside))
    own = pl.ds(pl.multiple_of(row * rows, rows), rows)
    next_to = pl.ds(pl.multiple_of((row + 1 - 2 * core) * rows, rows), rows)
    rows_of = lambda ref, which: jnp.concatenate([ref[s, which, :] for s in range(slots)], axis=0)
    query_grad = times_transposed(dq_low, qw[...]) * scale
    vec_own[0:1, :] = gain_grad + down(query_grad * rows_of(standard, own))
    vec_own[1:2, :] = shift_grad + down(query_grad)
    vec_own[2:3, :] = down(dq_low.astype(f32)) * scale
    vec_own[3:4, :] = value_bias
    vec_own[4:12, :] = vec_ref[...]
    vec_own[12:16, :] = jnp.zeros((4, width), f32)
    vec_sent = send(vec_own, vec_in, beside)

    for s in range(slots):
        send_on[s].wait()
        across_send[s] = (partial[2, s] + beside_recv[s, 1].astype(f32)).astype(bf16)
    over = send(across_send, across_recv, across)

    for copy in to_sibling:
        copy.wait()
    grads[0] = (
        outer_sum(rows_of(normed, own), dqh[core]) + outer_sum(rows_of(normed, next_to), dqh_in[...])
    ) * scale
    key_total = value_total = 0.0
    add = lambda left, right: (left.astype(f32) + right.astype(f32)).astype(bf16)
    for s in range(slots):
        turned = normed[s].T
        key_total = key_total + times_transposed(turned, add(dkt[s, mine, :], dk_in[s]))
        value_total = value_total + times_transposed(turned, add(dvt[s, mine, :], dv_in[s]))
    grads[1] = key_total
    grads[2] = value_total
    advance(one, 0)
    vec_sent.wait()
    vec = vec_own[...] + vec_in[...]
    vec_all[...] = jnp.zeros_like(vec_all)
    for j in range(parts):
        vec_all[j, 0:4, :short] = vec[0:4, short * j : short * (j + 1)]
        vec_all[j, 4:8, :short] = vec[8:12, short * j : short * (j + 1)]
        start = tall * j
        vec_all[j, 8:9, :tall] = vec[4 + start // width : 5 + start // width, start % width : start % width + tall]
    for p in range(parts):
        j = xor(dp, p, bits)
        for r in range(2):
            lanes = pl.ds(pl.multiple_of(other_bit(y, 0, r) * 128, 128), 128)
            for i, piece in enumerate(late[:3]):
                piece.state[2 * p + r] = grads[i, pl.ds(pl.multiple_of(j * short, short), short), lanes]
            late[3].state[2 * p + r] = vec_all[j, :, lanes]
    for piece in late:
        piece.go(0)

    advance(two, 0)
    advance(one, 1)
    advance(late, 0)
    advance(two, 1)
    over.wait()
    for s in range(slots):
        some = slice(rows * s, rows * (s + 1))
        grad = partial[0, s] + beside_recv[s, 0].astype(f32) + across_recv[s].astype(f32) + query_grad[some]
        stand, inverse = standardize(atoms[s, own, :].astype(f32))
        out_ref[some, :] = (dmid[some, :] + norm_back(grad * gain, stand, inverse)).astype(bf16)
    for n in range(2, steps):
        advance(one, n)
        advance(late, n - 1)
        advance(two, n)

    def place(group, at):
        for piece in group:
            piece.share(total.at[row, at : at + piece.rows])
            at += piece.rows
        return at

    cut = place(early, 0)
    mine, theirs = total.at[row, :cut], total.at[across[1], :cut]
    arrive = send(mine, mine, across)
    ends = [send(mine, mine, beside)]
    for n in range(steps - 1, late_steps):
        advance(late, n)
    place(late, cut)
    rest = total.at[row, cut:]
    ends += [send(rest, rest, device) for device in (across, corner, beside)]
    arrive.wait()
    ends.append(send(theirs, theirs, beside))
    for copy in ends:
        copy.wait()


def back(parts, scale, qt, dm, dmt, nm, k, vt, weights, cot, atoms, dmid, vectors, vec, pieces, query_w, key_w, value_w):
    slots, width, full = vt.shape
    rows, half = qt.shape[2], width // 2
    here, hidden = slots * rows, width * 4
    vm = pl.BlockSpec(memory_space=pltpu.VMEM)
    far = pl.BlockSpec(memory_space=pltpu.HBM)
    kinds = sum(make_parts(parts, width, hidden), [])
    count = sum(piece.rows for piece in kinds)
    transfers = 3 * slots + 9
    scratch = [
        pltpu.VMEM((slots, width, full), bf16),
        pltpu.VMEM((slots, width, full), bf16),
        pltpu.VMEM((slots, rows, width), bf16),
        pltpu.VMEM((width, width), bf16),
        pltpu.VMEM((width, width), bf16),
        pltpu.VMEM((width, width), bf16),
        pltpu.VMEM((slots, half, full), bf16),
        pltpu.VMEM((slots, half, full), bf16),
        pltpu.VMEM((2, here, half), bf16),
        pltpu.VMEM((here, half), bf16),
        pltpu.VMEM((16, width), f32),
        pltpu.VMEM((16, width), f32),
        pltpu.VMEM((slots, full, width), f32),
        pltpu.VMEM((slots, full, width), bf16),
        pltpu.VMEM((4, slots, rows, width), f32),
        pltpu.VMEM((slots, 2, rows, width), bf16),
        pltpu.VMEM((slots, 2, rows, width), bf16),
        pltpu.VMEM((slots, rows, width), bf16),
        pltpu.VMEM((slots, rows, width), bf16),
        pltpu.VMEM((3, width, half), f32),
        pltpu.VMEM((parts, 16, half), f32),
        pltpu.SemaphoreType.DMA((3,)),
        pltpu.SemaphoreType.DMA((transfers,)),
        pltpu.SemaphoreType.DMA((transfers,)),
    ]
    for piece in kinds:
        scratch += piece.scratch()
    return pl.pallas_call(
        functools.partial(back_kernel, parts, scale, hidden),
        in_specs=[vm] * (13 + 2 * len(PIECES)) + [far] * 3,
        out_specs=[vm] * 3,
        out_shape=[
            jax.ShapeDtypeStruct(cot.shape, bf16),
            jax.ShapeDtypeStruct((here, width), bf16),
            jax.ShapeDtypeStruct((4, count, 128), bf16),
        ],
        scratch_shapes=scratch,
        name="back",
        cost_estimate=pl.CostEstimate(
            flops=40 * slots * full * width * width, transcendentals=0, bytes_accessed=32 << 20
        ),
        compiler_params=pltpu.CompilerParams(vmem_limit_bytes=VMEM_BACK, collective_id=2, has_side_effects=True),
    )(
        qt, dm, dmt, nm, k, vt, weights, cot, atoms, dmid, *vectors, vec, *pieces,
        *(pltpu.with_memory_space_constraint(array, pltpu.HBM) for array in (query_w, key_w, value_w)),
    )


def last_kernel(total, grad_ref, made_ref, pair, *refs):
    count = 18
    outs, refs = refs[:count], refs[count:]
    (grad_out, made_out, *_, pair_out), (uw, ow, iw, qw, kw, vw), small, sem = outs, refs[:6], refs[6:15], refs[15]
    copies = []

    def move(source, target):
        copy = pltpu.make_async_copy(source, target, sem.at[len(copies)])
        copy.start()
        copies.append(copy)

    move(pair, pair_out)
    move(grad_ref, grad_out)
    move(made_ref, made_out)
    short = ow.shape[0]
    blocks = iw.shape[1] // 2 // 256
    spots = [spot for _, of in PIECES for spot in of] + [("query", 0), ("key", 0), ("value", 0)]
    refs = {"outer": uw, "inner": iw, "out": ow, "query": qw, "key": kw, "value": vw}
    at = 0
    for name, k in spots:
        ref = refs[name]
        first = short * k if name == "outer" else 0
        for r in range(4):
            core, y = r % 2, r // 2
            col = 256 * (core * blocks + k if name == "inner" else core) + 128 * y
            ref[first : first + short, col : col + 128] = total[r, at : at + short, :].astype(f32)
        at += short
    for ref, out in zip((uw, ow, iw, qw, kw, vw), outs[2:8]):
        move(ref, out)
    for i, ref in enumerate(small[:8]):
        ref[...] = total[0, at : at + 16, :].astype(f32)[i : i + 1, :short]
    ib = small[8]
    for y in range(2):
        n = min(128, ib.shape[1] - 128 * y)
        if n > 0:
            ib[:, 128 * y : 128 * y + n] = total[2 * y, at : at + 16, :].astype(f32)[8:9, :n]
    for ref, out in zip(small, outs[8:17]):
        move(ref, out)
    for copy in copies:
        copy.wait()


def last(parts, total, grad, made, pair, hidden):
    here, width = grad.shape
    short, tall = width // parts, hidden // parts
    vm = pl.BlockSpec(memory_space=pltpu.VMEM)
    hbm = pl.BlockSpec(memory_space=pl.ANY)
    shapes = [(tall, width), (short, width), (short, hidden)] + [(short, width)] * 3
    shapes += [(1, short)] * 8 + [(1, tall)]
    out_shape = [jax.ShapeDtypeStruct(grad.shape, bf16)] * 2
    out_shape += [jax.ShapeDtypeStruct(shape, f32) for shape in shapes]
    out_shape.append(jax.ShapeDtypeStruct(pair.shape, bf16))
    return pl.pallas_call(
        last_kernel,
        in_specs=[vm] + [hbm] * 3,
        out_specs=[hbm] * len(out_shape),
        out_shape=out_shape,
        scratch_shapes=[pltpu.VMEM(shape, f32) for shape in shapes] + [pltpu.SemaphoreType.DMA((len(out_shape),))],
        name="last",
        compiler_params=pltpu.CompilerParams(vmem_limit_bytes=16 << 20),
    )(total, grad, made, pair)


def local(
    parts,
    group,
    atoms,
    pair_bias,
    mol_counts,
    attn_gain,
    attn_shift,
    query_weight,
    query_bias,
    key_weight,
    value_weight,
    value_bias,
    out_weight,
    out_bias,
    ffn_gain,
    ffn_shift,
    inner_weight,
    inner_bias,
    outer_weight,
    outer_bias,
    atoms_cotangent,
    pair_cotangent,
):
    slots, part_rows, width = atoms.shape
    heads = pair_bias.shape[1]
    full = pair_bias.shape[3]
    scale = (width // heads) ** (-0.5)
    here = slots * part_rows
    hidden = inner_weight.shape[1]
    flat = lambda array: array.reshape(here, width)
    all_atoms, mask, q, qt, k, kt, v, vt = front(
        scale, full, atoms, mol_counts, (attn_gain, attn_shift, query_bias, value_bias), query_weight, key_weight, value_weight
    )
    pair_out, weights, mixed, inverse_sum = attention_forward(q, kt, v, pair_bias, mask)
    atoms_out, *pieces, scaled, centre, scaled_turned, grad_middle, vec = middle(
        parts,
        flat(mixed),
        flat(inverse_sum),
        flat(atoms),
        flat(atoms_cotangent),
        (out_bias, ffn_gain, ffn_shift, outer_bias, inner_bias),
        out_weight,
        inner_weight,
        outer_weight,
        slots,
    )
    pair_grad, grad, total = back(
        parts,
        scale,
        qt,
        scaled.reshape(q.shape),
        scaled_turned,
        centre.reshape(q.shape),
        k,
        vt,
        weights,
        pair_cotangent,
        all_atoms,
        grad_middle,
        (attn_gain, attn_shift),
        vec,
        pieces,
        query_weight,
        key_weight,
        value_weight,
    )
    grad, made, uw, ow, iw, qw, kw, vw, again, ashift, qb, vb, ob, fgain, fshift, ub, ib, pair_grad = last(
        parts, total, grad, atoms_out, pair_grad, hidden
    )
    line = lambda array: array.reshape(-1)
    return (
        made.reshape(atoms.shape),
        pair_out,
        grad.reshape(atoms.shape),
        pair_grad,
        line(again),
        line(ashift),
        qw,
        line(qb),
        kw,
        vw,
        line(vb),
        ow,
        line(ob),
        line(fgain),
        line(fshift),
        iw,
        line(ib),
        uw,
        line(ub),
    )


def solution(mesh):
    one, two = P("dp"), P("dp", None)
    atoms_spec, pair_spec = P("dp", "rows", None), P("dp", None, "rows", None)
    in_specs = (atoms_spec, pair_spec, two) + (P(),) * 15 + (atoms_spec, pair_spec)
    out_specs = (
        (atoms_spec, pair_spec, atoms_spec, pair_spec, one, one, two, one, two, two, one, two)
        + (one, one, one, two, one, two, one)
    )
    run = functools.partial(local, mesh.shape["dp"], mesh.shape["rows"])
    return jax.shard_map(run, mesh=mesh, in_specs=in_specs, out_specs=out_specs, check_vma=False)
```
